256 devices in a mesh: vel: 16 (over y_hi, x, core), gx: 16 (over z, y_lo).
Axes of the slice: x: 4, y: 4 (y_hi: 2, y_lo: 2; y = y_hi * 2 + y_lo), z: 8, core: 2. Of those that a mesh axis runs over, the one named last changes fastest.
Arguments:
- distribution: float32 [4096, 32768], P('vel', 'gx'), as said below
- wall_mask: int32 [64, 512], replicated, may hold values 0 or 1
- boundary_kind: int32 [2, 512], replicated, may hold values from 0 to 1
- inflow: float32 [4096], P('vel'), may hold values from 0.5 to 3
Outputs:
- evolved: float32 [4096, 32768], P('vel', 'gx')
The draws below stay inside these ranges and needn't reach their ends.
Inputs may be any that keep to these rules, and one draw needn't show every extreme that they name: `distribution`: every entry is positive. `wall_mask`: 1 marks a solid cell. `boundary_kind`: 0 is an outflow face, 1 an inflow face.
All inputs are finite; a program needn't handle non-finite values.
Results may differ from the reference program's by a relative error of at most 0.0003.
Values sent between devices are 32-bit elements; how exact they have to be, the bound alone decides.
No kernel may reach another device: no remote copies, remote signals or barrier semaphores. Data moves between devices by JAX's collectives and lax.ppermute only.
A program may use at most 64 MiB of HBM per device.

```python
import math
import jax
import jax.numpy as jnp
from jax import lax

VS = 16
NY = 16
NZ = 32
STEPS = 3
NV = 4096
NX = 64
NYZ = 512
CELLS = 32768


def draw_distribution(key, part):
    first, second = jax.random.split(jax.random.fold_in(key, 7), 2)
    ramp = (jnp.arange(NV) // (VS * VS)).astype(jnp.float32) / (VS - 1)
    base = jnp.exp(jax.random.uniform(first, (NV, CELLS), jnp.float32, -0.7, 0.7))
    row_scale = 1.0 + 2.0 * ramp
    cell_scale = jnp.exp(jax.random.uniform(second, (CELLS,), jnp.float32, math.log(0.3), math.log(3.0)))
    return base * row_scale[:, None] * cell_scale[None, :]


def plant(values, key, least, high):
    dims = values.shape
    index_at = [jax.random.randint(jax.random.fold_in(key, axis), (), 0, dims[axis]) for axis in range(len(dims))]
    values = values.at[tuple(index_at)].set(least)
    longest = dims.index(max(dims))
    index_at[longest] = (index_at[longest] + 1) % dims[longest]
    return values.at[tuple(index_at)].set(high)


def shard_levels(rng, dims, cuts, least, high):
    def one(axis_at, parts):
        steps = jax.random.uniform(jax.random.fold_in(jax.random.fold_in(rng, 6), axis_at), (parts,), jnp.float32, least / len(cuts), high / len(cuts))
        return jnp.repeat(jnp.exp(steps), dims[axis_at] // parts).reshape((-1,) + (1,) * (len(dims) - axis_at - 1))

    gain = one(*cuts[0])
    for cut in cuts[1:]:
        gain = gain * one(*cut)
    return gain


def setup_inputs(seed: int = 0) -> dict:
    arg_keys = jax.random.split(jax.random.key(seed), 5)
    return {
        "distribution": draw_distribution(jax.random.fold_in(arg_keys[4], 71), 0),
        "wall_mask": plant((jax.random.randint(arg_keys[1], (NX, NYZ), 0, 8) < 1).astype(jnp.int32), jax.random.fold_in(arg_keys[1], 1), 0, 1),
        "boundary_kind": plant(jax.random.randint(arg_keys[2], (2, NYZ), 0, 2), jax.random.fold_in(arg_keys[2], 1), 0, 1).astype(jnp.int32),
        "inflow": jnp.clip(jnp.exp(math.log(3.0) - 1.7917595 * jax.random.uniform(arg_keys[3], (NV,), jnp.float32) ** shard_levels(arg_keys[3], (NV,), ((0, 16),), -0.2, 0.2)), 0.5, 3.0),
    }


vel_limit = 4.5
time_step = 0.075
relax_rate = 0.6
viscous_thermal_ratio = 0.6666667


def velocity_rows(lattice_lines):
    square = VS * VS
    half = square // 2
    across = lattice_lines // square
    rest = lattice_lines % square
    upper = rest // half
    inner = rest % half
    along = jnp.where(upper == 1, VS // 2 + inner // VS, VS // 2 - 1 - inner // VS)
    depth = inner % VS
    spacing = 2.0 * vel_limit / VS

    def coord(index):
        return -vel_limit + (index.astype(jnp.float32) + 0.5) * spacing

    return coord(along), coord(across), coord(depth)


def poly_basis(speed_x, speed_y, speed_z):
    energy = speed_x * speed_x + speed_y * speed_y + speed_z * speed_z
    return jnp.stack([jnp.ones_like(speed_x), speed_x, speed_y, speed_z,
                      speed_x * speed_x, speed_y * speed_y, speed_z * speed_z,
                      speed_x * speed_y, speed_x * speed_z, speed_y * speed_z,
                      energy * speed_x, energy * speed_y, energy * speed_z], axis=1)


def exp_basis(speed_x, speed_y, speed_z):
    energy = speed_x * speed_x + speed_y * speed_y + speed_z * speed_z
    return jnp.stack([jnp.ones_like(speed_x), speed_x, speed_y, speed_z, energy], axis=1)


def shakhov_coefficients(moments):
    particle_concentration = moments[0]
    mean_drift_first = moments[1] / particle_concentration
    mean_drift_second = moments[2] / particle_concentration
    mean_drift_third_dir = moments[3] / particle_concentration
    second = moments[4:10]
    motion_work_content = mean_drift_first * mean_drift_first + mean_drift_second * mean_drift_second + mean_drift_third_dir * mean_drift_third_dir
    pressure_diagonal_sum = second[0] + second[1] + second[2]
    thermal_level = (pressure_diagonal_sum / particle_concentration - motion_work_content) / 3.0
    press_x = second[0] * mean_drift_first + second[3] * mean_drift_second + second[4] * mean_drift_third_dir
    press_y = second[3] * mean_drift_first + second[1] * mean_drift_second + second[5] * mean_drift_third_dir
    press_z = second[4] * mean_drift_first + second[5] * mean_drift_second + second[2] * mean_drift_third_dir
    heat_x = 0.5 * (moments[10] - 2.0 * press_x - mean_drift_first * pressure_diagonal_sum + 2.0 * particle_concentration * motion_work_content * mean_drift_first)
    heat_y = 0.5 * (moments[11] - 2.0 * press_y - mean_drift_second * pressure_diagonal_sum + 2.0 * particle_concentration * motion_work_content * mean_drift_second)
    heat_z = 0.5 * (moments[12] - 2.0 * press_z - mean_drift_third_dir * pressure_diagonal_sum + 2.0 * particle_concentration * motion_work_content * mean_drift_third_dir)
    heat_diffusivity_coef = (1.0 - viscous_thermal_ratio) / (5.0 * particle_concentration * thermal_level * thermal_level)
    quadrature_scale = heat_diffusivity_coef / thermal_level
    mixed = mean_drift_first * heat_x + mean_drift_second * heat_y + mean_drift_third_dir * heat_z
    foremost_dimension = jnp.log(particle_concentration) - 1.5 * jnp.log(2.0 * jnp.pi * thermal_level) - motion_work_content / (2.0 * thermal_level)
    lattice_lines = [foremost_dimension, mean_drift_first / thermal_level, mean_drift_second / thermal_level, mean_drift_third_dir / thermal_level, -0.5 / thermal_level,
            1.0 - quadrature_scale * mixed * motion_work_content + 5.0 * heat_diffusivity_coef * mixed,
            quadrature_scale * (heat_x * motion_work_content + 2.0 * mixed * mean_drift_first) - 5.0 * heat_diffusivity_coef * heat_x,
            quadrature_scale * (heat_y * motion_work_content + 2.0 * mixed * mean_drift_second) - 5.0 * heat_diffusivity_coef * heat_y,
            quadrature_scale * (heat_z * motion_work_content + 2.0 * mixed * mean_drift_third_dir) - 5.0 * heat_diffusivity_coef * heat_z,
            -2.0 * quadrature_scale * heat_x * mean_drift_first - quadrature_scale * mixed,
            -2.0 * quadrature_scale * heat_y * mean_drift_second - quadrature_scale * mixed,
            -2.0 * quadrature_scale * heat_z * mean_drift_third_dir - quadrature_scale * mixed,
            -2.0 * quadrature_scale * (heat_x * mean_drift_second + heat_y * mean_drift_first),
            -2.0 * quadrature_scale * (heat_x * mean_drift_third_dir + heat_z * mean_drift_first),
            -2.0 * quadrature_scale * (heat_y * mean_drift_third_dir + heat_z * mean_drift_second),
            quadrature_scale * heat_x, quadrature_scale * heat_y, quadrature_scale * heat_z]
    return jnp.stack(lattice_lines, axis=0)


def relax(moved, coefficients, expo_rows, poly_rows):
    power = jnp.dot(expo_rows, coefficients[0:5], precision=lax.Precision.HIGHEST)
    shape = jnp.dot(poly_rows, coefficients[5:18], precision=lax.Precision.HIGHEST)
    return moved + relax_rate * (jnp.exp(power) * shape - moved)


def reference(distribution, wall_mask, boundary_kind, inflow):
    rows_all = jnp.arange(NV, dtype=jnp.int32)
    speed_x, speed_y, speed_z = velocity_rows(rows_all)
    poly = poly_basis(speed_x, speed_y, speed_z)
    expo = exp_basis(speed_x, speed_y, speed_z)
    weight = (2.0 * vel_limit / VS) ** 3
    openness = (1 - wall_mask).astype(jnp.float32).reshape(NX, NY, NZ)
    open_pad = jnp.pad(openness, ((1, 1), (0, 0), (0, 0)), constant_values=1.0)
    low_in = (boundary_kind[0] == 1).reshape(NY, NZ)
    high_in = (boundary_kind[1] == 1).reshape(NY, NZ)
    block = VS * VS
    count = NV // block

    def split(array):
        return array.reshape((count, block) + array.shape[1:])

    def transport(pieces):
        values, along_x, along_y, along_z, entering = pieces
        cube = values.reshape(block, NX, NY, NZ)
        low_ghost = jnp.where(low_in[None], entering[:, None, None], cube[:, 0])
        high_ghost = jnp.where(high_in[None], entering[:, None, None], cube[:, NX - 1])
        extended = jnp.concatenate([low_ghost[:, None], cube, high_ghost[:, None]], axis=1)
        speed = along_x[:, None, None, None]
        upwind = jnp.where(speed > 0, extended[:, :-1], extended[:, 1:])
        flux = speed * upwind * (open_pad[:-1] * open_pad[1:])
        change = flux[:, 1:] - flux[:, :-1]
        speed = along_y[:, None, None, None]
        upwind = jnp.where(speed > 0, cube[:, :, :-1], cube[:, :, 1:])
        flux = speed * upwind * (openness[:, :-1] * openness[:, 1:])
        flux = jnp.pad(flux, ((0, 0), (0, 0), (1, 1), (0, 0)))
        change = change + (flux[:, :, 1:] - flux[:, :, :-1])
        speed = along_z[:, None, None, None]
        upwind = jnp.where(speed > 0, cube[:, :, :, :-1], cube[:, :, :, 1:])
        flux = speed * upwind * (openness[:, :, :-1] * openness[:, :, 1:])
        flux = jnp.pad(flux, ((0, 0), (0, 0), (0, 0), (1, 1)))
        change = change + (flux[:, :, :, 1:] - flux[:, :, :, :-1])
        return (cube - time_step * change).reshape(block, CELLS)

    def accumulate(total, pieces):
        values, poly_block = pieces
        return total + jnp.dot(poly_block.T, values, precision=lax.Precision.HIGHEST), None

    state = split(distribution)
    for step in range(STEPS):
        moved = lax.map(transport, (state, split(speed_x), split(speed_y), split(speed_z), split(inflow)))
        total, unused = lax.scan(accumulate, jnp.zeros((13, CELLS), jnp.float32), (moved, split(poly)))
        coefficients = shakhov_coefficients(weight * total)

        def relax_block(pieces):
            values, expo_block, poly_block = pieces
            return relax(values, coefficients, expo_block, poly_block)

        state = lax.map(relax_block, (moved, split(expo), split(poly)))
    return state.reshape(NV, CELLS)
```

```python
import functools
import math

import jax
import jax.numpy as jnp
from jax import lax
from jax.experimental import pallas as pl
from jax.experimental.pallas import tpu as pltpu
from jax.sharding import PartitionSpec as P

VS = 16
NY = 16
NZ = 32
STEPS = 3
SEC = NY * NZ
DEPTH = 4
TILES = SEC // 128

LIMIT = 4.5
DT = 0.075
RATE = 0.6
KEEP = 1.0 - RATE
RATIO = 0.6666667
H = 2.0 * LIMIT / VS
WEIGHT = H**3
HALF = VS * VS // 2
ROWS = VS * VS
OWN = DEPTH * TILES


def vy_of(index):
    return -LIMIT + (index.astype(jnp.float32) + 0.5) * H


def sub_iota():
    return lax.broadcasted_iota(jnp.int32, (8, 128), 0).astype(jnp.float32)


def vz_tile(b):
    q = sub_iota()
    return (q + 0.5) * H if b else (q - 7.5) * H


def row(ref, *index):
    return jnp.broadcast_to(ref[index], (8, 128))


def prepare_masks(wall_ref, faces, position, count, forward):
    opened = []
    for slot in range(DEPTH + 2):
        at = position * DEPTH + slot - 1
        inside = jnp.logical_and(at >= 0, at < count * DEPTH)
        line = wall_ref[pl.ds(jnp.clip(at, 0, count * DEPTH - 1), 1), :]
        opened.append(jnp.where(inside, (1 - line).astype(jnp.float32), 1.0))
    zero = jnp.zeros_like(opened[0])
    o = jnp.concatenate(opened + [zero, zero], axis=0)
    cell = lax.broadcasted_iota(jnp.int32, (8, SEC), 1)
    up_x = o * pltpu.roll(o, 7, 0)
    up_y = o * pltpu.roll(o, SEC - NZ, 1) * (cell < SEC - NZ).astype(jnp.float32)
    up_z = o * pltpu.roll(o, SEC - 1, 1) * ((cell & (NZ - 1)) < NZ - 1).astype(jnp.float32)
    down_y = pltpu.roll(up_y, NZ, 1)
    down_z = pltpu.roll(up_z, 1, 1)
    planes = [
        up_x, jnp.where(forward, up_y, down_y), jnp.where(forward, down_y, up_y), down_z, up_z
    ]
    for k, plane in enumerate(planes):
        for slot in range(DEPTH + 1):
            for t in range(TILES):
                line = plane[slot : slot + 1, t * 128 : (t + 1) * 128]
                faces[k, slot, t] = jnp.broadcast_to(line, (8, 128))


def fill_ends(state, inflow_ref, kind_ref, position, count):
    lane = lax.broadcasted_iota(jnp.int32, (8, 128), 1)
    sub = lax.broadcasted_iota(jnp.int32, (8, 128), 0)

    def one(side, base, inner, outer):
        @pl.when(position == (0 if side == 0 else count - 1))
        def _():
            for tile in range(HALF // 8):
                start = base + tile * 8
                line = row(inflow_ref, pl.ds(start // 128, 1), slice(None))
                picked = jnp.where(lane == sub + start % 128, line, 0.0)
                column = jnp.sum(picked, axis=1, keepdims=True)
                for t in range(TILES):
                    kind = row(kind_ref, pl.ds(side, 1), pl.ds(t * 128, 128))
                    inside = state[pl.ds(start, 8), pl.ds(inner * SEC + t * 128, 128)]
                    state[pl.ds(start, 8), pl.ds(outer * SEC + t * 128, 128)] = jnp.where(
                        kind == 1, jnp.broadcast_to(column, (8, 128)), inside
                    )

    one(0, HALF, 1, 0)
    one(1, 0, DEPTH, DEPTH + 1)


def transport(state, faces, moved, sums, iy):
    forward = iy >= VS // 2
    speed_y = jnp.abs(vy_of(iy)) * (KEEP * DT)
    lane = lax.broadcasted_iota(jnp.int32, (8, 128), 1)
    take = jnp.logical_or(
        jnp.logical_and(forward, lane < NZ), jnp.logical_and(~forward, lane >= 128 - NZ)
    )
    shift_y = jnp.where(forward, NZ, 128 - NZ)

    def section(i, carry):
        total = [[None] * 8 for _ in range(TILES)]
        tiles = [jnp.where(forward, k, TILES - 1 - k) for k in range(TILES)]
        lanes = [pl.multiple_of(t * 128, 128) for t in tiles]
        for b in range(2):
            vz = vz_tile(b)
            az = jnp.abs(vz) * (KEEP * DT)
            below = [faces[0, i, t] for t in tiles]
            above = [faces[0, i + 1, t] for t in tiles]
            keep, in_y, in_z = [], [], []
            for t in tiles:
                out_y = faces[1, i + 1, t]
                out_z = faces[4 if b else 3, i + 1, t]
                keep.append(KEEP - speed_y * out_y - az * out_z)
                in_y.append(speed_y * faces[2, i + 1, t])
                in_z.append(az * faces[3 if b else 4, i + 1, t])
            acc = [[None] * 4 for _ in range(TILES)]
            for a in range(VS // 2):
                speed = (a + 0.5) * H
                cx = KEEP * DT * speed
                lo = [cx * x for x in below]
                hi = [cx * x for x in above]
                both = []
                for sign in range(2):
                    start = sign * HALF + a * VS + 8 * b
                    here, shifted = [], []
                    for l in lanes:
                        at = pl.multiple_of((i + 1) * SEC + l, 128)
                        value = state[start : start + 8, pl.ds(at, 128)]
                        here.append(value)
                        shifted.append(pltpu.roll(value, shift_y, 1))
                    result = []
                    for k, l in enumerate(lanes):
                        at = pl.multiple_of((i + (0 if sign else 2)) * SEC + l, 128)
                        before = state[start : start + 8, pl.ds(at, 128)]
                        out_x, in_x = (hi[k], lo[k]) if sign else (lo[k], hi[k])
                        along_y = jnp.where(take, shifted[k - 1], shifted[k]) if k else shifted[k]
                        along_z = pltpu.roll(here[k], 1 if b else 127, 1)
                        value = (
                            here[k] * (keep[k] - out_x)
                            + before * in_x
                            + along_y * in_y[k]
                            + along_z * in_z[k]
                        )
                        at = pl.multiple_of(i * SEC + l, 128)
                        moved[start : start + 8, pl.ds(at, 128)] = value
                        result.append(value)
                    both.append(result)
                for k in range(TILES):
                    even = both[1][k] + both[0][k]
                    odd = both[1][k] - both[0][k]
                    terms = [even, speed * odd, (speed * speed) * even, (speed**3) * odd]
                    for p in range(4):
                        acc[k][p] = terms[p] if acc[k][p] is None else acc[k][p] + terms[p]
            vz2 = vz * vz
            for k in range(TILES):
                a0, a1, a2, a3 = acc[k]
                terms = [
                    a0, a1, vz * a0, a2, vz2 * a0, vz * a1,
                    a3 + vz2 * a1, vz * (a2 + vz2 * a0),
                ]
                for p in range(8):
                    total[k][p] = terms[p] if b == 0 else total[k][p] + terms[p]
        for k, t in enumerate(tiles):
            for p in range(8):
                sums[p, i * TILES + t] = total[k][p]
        return carry

    lax.fori_loop(0, DEPTH, section, 0)


def fold(sums, p, first):
    sub = lax.broadcasted_iota(jnp.int32, (8, 128), 0)
    values = [sums[p, first + t] for t in range(8)]
    for step in (4, 2, 1):
        low = (sub & step) == 0
        merged = []
        for t in range(step):
            a, b = values[t], values[t + step]
            a = a + pltpu.roll(a, 8 - step, 0)
            b = b + pltpu.roll(b, step, 0)
            merged.append(jnp.where(low, a, b))
        values = merged
    return values[0]


def expand(sums, vy):
    s0, sx, sz, sxx, szz, sxz, ex, ez = sums
    y2 = vy * vy
    return [
        s0, sx, vy * s0, sz, sxx, y2 * s0, szz, vy * sx, sxz, vy * sz,
        ex + y2 * sx, vy * (sxx + szz + y2 * s0), ez + y2 * sz,
    ]


def coefficients(m, vy):
    n = m[0]
    inverse = 1.0 / n
    ux, uy, uz = m[1] * inverse, m[2] * inverse, m[3] * inverse
    xx, yy, zz, xy, xz, yz = m[4:10]
    u2 = ux * ux + uy * uy + uz * uz
    trace = xx + yy + zz
    temp = (trace * inverse - u2) / 3.0
    px = xx * ux + xy * uy + xz * uz
    py = xy * ux + yy * uy + yz * uz
    pz = xz * ux + yz * uy + zz * uz
    common = 2.0 * n * u2 - trace
    qx = 0.5 * (m[10] - 2.0 * px + common * ux)
    qy = 0.5 * (m[11] - 2.0 * py + common * uy)
    qz = 0.5 * (m[12] - 2.0 * pz + common * uz)
    inv_t = 1.0 / temp
    kappa = (1.0 - RATIO) / 5.0 * inverse * inv_t * inv_t
    s = kappa * inv_t
    i2t = 0.5 * inv_t
    cy = vy - uy
    level = 0.5 * (
        jnp.log(n) - 1.5 * jnp.log((2.0 * math.pi) * temp) - cy * cy * i2t
    )
    return [ux, uz, i2t, level, qx, qz, s, qy * cy, s * cy * cy - 5.0 * kappa]


def relax(moved, coefs, lines, state, count):
    q = sub_iota()

    def tile(j, carry):
        ux, uz, i2t, level, qx, qz, s, qyc, rest = [coefs[k, j] for k in range(9)]
        for sign in range(2):
            cx = (q + 0.5) * (H if sign else -H) - ux
            c2 = cx * cx
            lines[sign, 0] = jnp.exp(level - c2 * i2t) * RATE
            lines[sign, 1] = qx * cx + qyc
            lines[sign, 2] = s * c2 + rest
        along = []
        for b in range(2):
            cz = vz_tile(b) - uz
            c2 = cz * cz
            along.append((jnp.exp(level - c2 * i2t), qz * cz, s * c2))
        at = pl.multiple_of(j * 128, 128)
        for sign in range(2):
            for a in range(VS // 2):
                ex = row(lines, sign, 0, pl.ds(a, 1), slice(None))
                qa = row(lines, sign, 1, pl.ds(a, 1), slice(None))
                sa = row(lines, sign, 2, pl.ds(a, 1), slice(None))
                for b in range(2):
                    ez, qb, sb = along[b]
                    start = sign * HALF + a * VS + 8 * b
                    value = moved[start : start + 8, pl.ds(at, 128)]
                    state[start : start + 8, pl.ds(at, 128)] = value + (ex * ez) * (
                        1.0 + (qa + qb) * (sa + sb)
                    )
        return carry

    lax.fori_loop(0, count, tile, 0)


def move_kernel(
    count, dist, left, right, wall, kind, inflow, moved, mine, other, state, faces, sums, sems
):
    iy = lax.axis_index("vel")
    position = lax.axis_index("gx")
    copies = [
        pltpu.make_async_copy(dist, state.at[:, pl.ds(SEC, DEPTH * SEC)], sems.at[0]),
        pltpu.make_async_copy(left, state.at[pl.ds(HALF, HALF), pl.ds(0, SEC)], sems.at[1]),
        pltpu.make_async_copy(
            right, state.at[pl.ds(0, HALF), pl.ds((DEPTH + 1) * SEC, SEC)], sems.at[2]
        ),
    ]
    for copy in copies:
        copy.start()
    prepare_masks(wall, faces, position, count, iy >= VS // 2)
    for copy in copies:
        copy.wait()
    fill_ends(state, inflow, kind, position, count)
    transport(state, faces, moved, sums, iy)
    core = lax.rem(iy, 2)
    for p in range(8):
        mine[p] = fold(sums, p, core * 8)
        other[p] = fold(sums, p, 8 - core * 8)


VM = pl.BlockSpec(memory_space=pltpu.VMEM)
ANY = pl.BlockSpec(memory_space=pl.ANY)


def move(dist, left, right, wall, kind, inflow, count):
    part = jax.ShapeDtypeStruct((8, 8, 128), jnp.float32)
    return pl.pallas_call(
        functools.partial(move_kernel, count),
        out_shape=(jax.ShapeDtypeStruct((ROWS, DEPTH * SEC), jnp.float32), part, part),
        in_specs=[ANY, ANY, ANY, VM, VM, VM],
        out_specs=(VM, VM, VM),
        scratch_shapes=[
            pltpu.VMEM((ROWS, (DEPTH + 2) * SEC), jnp.float32),
            pltpu.VMEM((5, DEPTH + 1, TILES, 8, 128), jnp.float32),
            pltpu.VMEM((8, OWN, 8, 128), jnp.float32),
            pltpu.SemaphoreType.DMA((3,)),
        ],
        name="move",
    )(dist, left, right, wall, kind, inflow)


def join_kernel(mine, other, out):
    iy = lax.axis_index("vel")
    mate = iy + 1 - 2 * lax.rem(iy, 2)
    a = expand([mine[p] for p in range(8)], vy_of(iy))
    b = expand([other[p] for p in range(8)], vy_of(mate))
    for k in range(13):
        value = a[k] + b[k]
        for chip in range(8):
            out[chip, k] = value


def total_kernel(parts, out):
    for k in range(13):
        value = parts[0, k]
        for chip in range(1, 8):
            value = value + parts[chip, k]
        out[k] = value * (WEIGHT / KEEP)


def swap_cores(array):
    return lax.ppermute(array, "vel", [(i, i ^ 1) for i in range(VS)])


def all_moments(mine, other):
    got = swap_cores(other)
    shape = jax.ShapeDtypeStruct((8, 13, 8, 128), jnp.float32)
    sent = pl.pallas_call(
        join_kernel, out_shape=shape, in_specs=[VM, VM], out_specs=VM, name="join"
    )(mine, got)
    groups = [[2 * i + c for i in range(VS // 2)] for c in range(2)]
    parts = lax.all_to_all(sent, "vel", 0, 0, axis_index_groups=groups, tiled=True)
    own = pl.pallas_call(
        total_kernel,
        out_shape=jax.ShapeDtypeStruct((13, 8, 128), jnp.float32),
        in_specs=[VM],
        out_specs=VM,
        name="total",
    )(parts)
    return own, swap_cores(own)


def relax_kernel(last, moved, mine, other, *refs):
    if last:
        state, coefs, lines = refs
    else:
        state, to_right, to_left, coefs, lines = refs
    iy = lax.axis_index("vel")
    core = lax.rem(iy, 2)
    vy = vy_of(iy)
    for ref, half in ((mine, core), (other, 1 - core)):
        values = coefficients([ref[k] for k in range(13)], vy)
        for k, value in enumerate(values):
            for t in range(8):
                coefs[k, half * 8 + t] = jnp.broadcast_to(value[t : t + 1], (8, 128))
    relax(moved, coefs, lines, state, OWN)
    if not last:
        to_right[...] = state[HALF:, (DEPTH - 1) * SEC :]
        to_left[...] = state[:HALF, :SEC]


def relaxed(moved, mine, other, last):
    whole = jax.ShapeDtypeStruct((ROWS, DEPTH * SEC), jnp.float32)
    rim = jax.ShapeDtypeStruct((HALF, SEC), jnp.float32)
    outs = (whole,) if last else (whole, rim, rim)
    return pl.pallas_call(
        functools.partial(relax_kernel, last),
        out_shape=outs,
        in_specs=[VM, VM, VM],
        out_specs=(VM,) * len(outs),
        scratch_shapes=[
            pltpu.VMEM((9, OWN, 8, 128), jnp.float32),
            pltpu.VMEM((2, 3, 8, 128), jnp.float32),
        ],
        name="relax",
    )(moved, mine, other)


def send_rims(to_right, to_left, peers):
    from_left = lax.ppermute(to_right, "gx", [(i, i + 1) for i in range(peers - 1)])
    from_right = lax.ppermute(to_left, "gx", [(i + 1, i) for i in range(peers - 1)])
    return from_left, from_right


def per_device(distribution, wall_mask, boundary_kind, inflow):
    count = lax.axis_size("gx")
    inflow = inflow.reshape(2, 128)
    state = distribution
    left, right = send_rims(state[HALF:, (DEPTH - 1) * SEC :], state[:HALF, :SEC], count)
    for step in range(STEPS):
        last = step + 1 == STEPS
        moved, mine, other = move(state, left, right, wall_mask, boundary_kind, inflow, count)
        own, got = all_moments(mine, other)
        outs = relaxed(moved, own, got, last)
        state = outs[0]
        if not last:
            left, right = send_rims(outs[1], outs[2], count)
    return state


def solution(mesh):
    placed = (P("vel", "gx"), P(), P(), P("vel"))
    return jax.shard_map(
        per_device, mesh=mesh, in_specs=placed, out_specs=P("vel", "gx"), check_vma=False
    )
```

```python
import functools
import math

import jax
import jax.numpy as jnp
from jax import lax
from jax.experimental import pallas as pl
from jax.experimental.pallas import tpu as pltpu
from jax.sharding import PartitionSpec as P

VS = 16
NY = 16
NZ = 32
STEPS = 3
SEC = NY * NZ
DEPTH = 4
TILES = SEC // 128

LIMIT = 4.5
DT = 0.075
RATE = 0.6
KEEP = 1.0 - RATE
RATIO = 0.6666667
H = 2.0 * LIMIT / VS
WEIGHT = H**3
HALF = VS * VS // 2
ROWS = VS * VS
OWN = DEPTH * TILES


def vy_of(index):
    return -LIMIT + (index.astype(jnp.float32) + 0.5) * H


def sub_iota():
    return lax.broadcasted_iota(jnp.int32, (8, 128), 0).astype(jnp.float32)


def vz_tile(b):
    q = sub_iota()
    return (q + 0.5) * H if b else (q - 7.5) * H


def row(ref, *index):
    return jnp.broadcast_to(ref[index], (8, 128))


def prepare_masks(wall_ref, faces, position, count, forward):
    opened = []
    for slot in range(DEPTH + 2):
        at = position * DEPTH + slot - 1
        inside = jnp.logical_and(at >= 0, at < count * DEPTH)
        line = wall_ref[pl.ds(jnp.clip(at, 0, count * DEPTH - 1), 1), :]
        opened.append(jnp.where(inside, (1 - line).astype(jnp.float32), 1.0))
    zero = jnp.zeros_like(opened[0])
    o = jnp.concatenate(opened + [zero, zero], axis=0)
    cell = lax.broadcasted_iota(jnp.int32, (8, SEC), 1)
    up_x = o * pltpu.roll(o, 7, 0)
    up_y = o * pltpu.roll(o, SEC - NZ, 1) * (cell < SEC - NZ).astype(jnp.float32)
    up_z = o * pltpu.roll(o, SEC - 1, 1) * ((cell & (NZ - 1)) < NZ - 1).astype(jnp.float32)
    down_y = pltpu.roll(up_y, NZ, 1)
    down_z = pltpu.roll(up_z, 1, 1)
    planes = [
        up_x, jnp.where(forward, up_y, down_y), jnp.where(forward, down_y, up_y), down_z, up_z
    ]
    for k, plane in enumerate(planes):
        for slot in range(DEPTH + 1):
            for t in range(TILES):
                line = plane[slot : slot + 1, t * 128 : (t + 1) * 128]
                faces[k, slot, t] = jnp.broadcast_to(line, (8, 128))


def fill_ends(state, inflow_ref, kind_ref, position, count):
    lane = lax.broadcasted_iota(jnp.int32, (8, 128), 1)
    sub = lax.broadcasted_iota(jnp.int32, (8, 128), 0)

    def one(side, base, inner, outer):
        @pl.when(position == (0 if side == 0 else count - 1))
        def _():
            for tile in range(HALF // 8):
                start = base + tile * 8
                line = row(inflow_ref, pl.ds(start // 128, 1), slice(None))
                picked = jnp.where(lane == sub + start % 128, line, 0.0)
                column = jnp.sum(picked, axis=1, keepdims=True)
                for t in range(TILES):
                    kind = row(kind_ref, pl.ds(side, 1), pl.ds(t * 128, 128))
                    inside = state[pl.ds(start, 8), pl.ds(inner * SEC + t * 128, 128)]
                    state[pl.ds(start, 8), pl.ds(outer * SEC + t * 128, 128)] = jnp.where(
                        kind == 1, jnp.broadcast_to(column, (8, 128)), inside
                    )

    one(0, HALF, 1, 0)
    one(1, 0, DEPTH, DEPTH + 1)


def transport(state, faces, moved, sums, iy):
    forward = iy >= VS // 2
    speed_y = jnp.abs(vy_of(iy)) * (KEEP * DT)
    lane = lax.broadcasted_iota(jnp.int32, (8, 128), 1)
    take = jnp.logical_or(
        jnp.logical_and(forward, lane < NZ), jnp.logical_and(~forward, lane >= 128 - NZ)
    )
    shift_y = jnp.where(forward, NZ, 128 - NZ)

    def section(i, carry):
        total = [[None] * 8 for _ in range(TILES)]
        tiles = [jnp.where(forward, k, TILES - 1 - k) for k in range(TILES)]
        lanes = [pl.multiple_of(t * 128, 128) for t in tiles]
        for b in range(2):
            vz = vz_tile(b)
            az = jnp.abs(vz) * (KEEP * DT)
            below = [faces[0, i, t] for t in tiles]
            above = [faces[0, i + 1, t] for t in tiles]
            keep, in_y, in_z = [], [], []
            for t in tiles:
                out_y = faces[1, i + 1, t]
                out_z = faces[4 if b else 3, i + 1, t]
                keep.append(KEEP - speed_y * out_y - az * out_z)
                in_y.append(speed_y * faces[2, i + 1, t])
                in_z.append(az * faces[3 if b else 4, i + 1, t])
            acc = [[None] * 4 for _ in range(TILES)]
            for a in range(VS // 2):
                speed = (a + 0.5) * H
                cx = KEEP * DT * speed
                lo = [cx * x for x in below]
                hi = [cx * x for x in above]
                both = []
                for sign in range(2):
                    start = sign * HALF + a * VS + 8 * b
                    here, shifted = [], []
                    for l in lanes:
                        at = pl.multiple_of((i + 1) * SEC + l, 128)
                        value = state[start : start + 8, pl.ds(at, 128)]
                        here.append(value)
                        shifted.append(pltpu.roll(value, shift_y, 1))
                    result = []
                    for k, l in enumerate(lanes):
                        at = pl.multiple_of((i + (0 if sign else 2)) * SEC + l, 128)
                        before = state[start : start + 8, pl.ds(at, 128)]
                        out_x, in_x = (hi[k], lo[k]) if sign else (lo[k], hi[k])
                        along_y = jnp.where(take, shifted[k - 1], shifted[k]) if k else shifted[k]
                        along_z = pltpu.roll(here[k], 1 if b else 127, 1)
                        value = (
                            here[k] * (keep[k] - out_x)
                            + before * in_x
                            + along_y * in_y[k]
                            + along_z * in_z[k]
                        )
                        at = pl.multiple_of(i * SEC + l, 128)
                        moved[start : start + 8, pl.ds(at, 128)] = value
                        result.append(value)
                    both.append(result)
                for k in range(TILES):
                    even = both[1][k] + both[0][k]
                    odd = both[1][k] - both[0][k]
                    terms = [even, speed * odd, (speed * speed) * even, (speed**3) * odd]
                    for p in range(4):
                        acc[k][p] = terms[p] if acc[k][p] is None else acc[k][p] + terms[p]
            vz2 = vz * vz
            for k in range(TILES):
                a0, a1, a2, a3 = acc[k]
                terms = [
                    a0, a1, vz * a0, a2, vz2 * a0, vz * a1,
                    a3 + vz2 * a1, vz * (a2 + vz2 * a0),
                ]
                for p in range(8):
                    total[k][p] = terms[p] if b == 0 else total[k][p] + terms[p]
        for k, t in enumerate(tiles):
            for p in range(8):
                sums[p, i * TILES + t] = total[k][p]
        return carry

    lax.fori_loop(0, DEPTH, section, 0)


def fold(sums, p, first):
    sub = lax.broadcasted_iota(jnp.int32, (8, 128), 0)
    values = [sums[p, first + t] for t in range(8)]
    for step in (4, 2, 1):
        low = (sub & step) == 0
        merged = []
        for t in range(step):
            a, b = values[t], values[t + step]
            a = a + pltpu.roll(a, 8 - step, 0)
            b = b + pltpu.roll(b, step, 0)
            merged.append(jnp.where(low, a, b))
        values = merged
    return values[0]


def expand(sums, vy):
    s0, sx, sz, sxx, szz, sxz, ex, ez = sums
    y2 = vy * vy
    return [
        s0, sx, vy * s0, sz, sxx, y2 * s0, szz, vy * sx, sxz, vy * sz,
        ex + y2 * sx, vy * (sxx + szz + y2 * s0), ez + y2 * sz,
    ]


def coefficients(m, vy):
    n = m[0]
    inverse = 1.0 / n
    ux, uy, uz = m[1] * inverse, m[2] * inverse, m[3] * inverse
    xx, yy, zz, xy, xz, yz = m[4:10]
    u2 = ux * ux + uy * uy + uz * uz
    trace = xx + yy + zz
    temp = (trace * inverse - u2) / 3.0
    px = xx * ux + xy * uy + xz * uz
    py = xy * ux + yy * uy + yz * uz
    pz = xz * ux + yz * uy + zz * uz
    common = 2.0 * n * u2 - trace
    qx = 0.5 * (m[10] - 2.0 * px + common * ux)
    qy = 0.5 * (m[11] - 2.0 * py + common * uy)
    qz = 0.5 * (m[12] - 2.0 * pz + common * uz)
    inv_t = 1.0 / temp
    kappa = (1.0 - RATIO) / 5.0 * inverse * inv_t * inv_t
    s = kappa * inv_t
    i2t = 0.5 * inv_t
    cy = vy - uy
    level = 0.5 * (
        jnp.log(n) - 1.5 * jnp.log((2.0 * math.pi) * temp) - cy * cy * i2t
    )
    return [ux, uz, i2t, level, qx, qz, s, qy * cy, s * cy * cy - 5.0 * kappa]


def point(coefs, j):
    return [coefs[k, j] for k in range(9)]


def across(values, sign):
    ux, uz, i2t, level, qx, qz, s, qyc, rest = values
    cx = (sub_iota() + 0.5) * (H if sign else -H) - ux
    c2 = cx * cx
    return jnp.exp(level - c2 * i2t) * RATE, qx * cx + qyc, s * c2 + rest


def along(values, b):
    ux, uz, i2t, level, qx, qz, s, qyc, rest = values
    cz = vz_tile(b) - uz
    c2 = cz * cz
    return jnp.exp(level - c2 * i2t), qz * cz, s * c2


def store_lines(lines, values, sign):
    for k, value in enumerate(across(values, sign)):
        lines[sign, k] = value


def relax_rows(read, write, lines, fixed, sign):
    for a in range(VS // 2):
        ex, qa, sa = [row(lines, sign, k, pl.ds(a, 1), slice(None)) for k in range(3)]
        for b in range(2):
            ez, qb, sb = fixed[b]
            start = a * VS + 8 * b
            write(start, read(start) + (ex * ez) * (1.0 + (qa + qb) * (sa + sb)))


def relax(moved, coefs, lines, state, shift):
    def tile(j, carry):
        values = point(coefs, j)
        for sign in range(2):
            store_lines(lines, values, sign)
        fixed = [along(values, b) for b in range(2)]
        at = pl.multiple_of(j * 128, 128)
        to = pl.multiple_of(j * 128 + shift, 128)
        for sign in range(2):
            base = sign * HALF

            def read(start):
                return moved[base + start : base + start + 8, pl.ds(at, 128)]

            def write(start, value):
                state[base + start : base + start + 8, pl.ds(to, 128)] = value

            relax_rows(read, write, lines, fixed, sign)
        return carry

    lax.fori_loop(0, OWN, tile, 0)


def relax_ghosts(ghosts, coefs, lines, state):
    def tile(t, carry):
        at = pl.multiple_of(t * 128, 128)
        for sign in range(2):
            values = point(coefs, t + TILES * sign)
            store_lines(lines, values, sign)
            fixed = [along(values, b) for b in range(2)]
            base = sign * HALF
            to = pl.multiple_of(t * 128 + (0 if sign else (DEPTH + 1) * SEC), 128)

            def read(start):
                return ghosts[sign, start : start + 8, pl.ds(at, 128)]

            def write(start, value):
                state[base + start : base + start + 8, pl.ds(to, 128)] = value

            relax_rows(read, write, lines, fixed, sign)
        return carry

    lax.fori_loop(0, TILES, tile, 0)


def spread(coefs, values, first):
    for k, value in enumerate(values):
        for t in range(8):
            coefs[k, first + t] = jnp.broadcast_to(value[t : t + 1], (8, 128))


def finish(state, faces, sums, wall, kind, inflow, moved, mine, other, rims, count):
    iy = lax.axis_index("vel")
    position = lax.axis_index("gx")
    fill_ends(state, inflow, kind, position, count)
    transport(state, faces, moved, sums, iy)
    core = lax.rem(iy, 2)
    vy = vy_of(iy)
    for ref, first in ((mine, core * 8), (other, 8 - core * 8)):
        values = expand([fold(sums, p, first) * (WEIGHT / KEEP) for p in range(8)], vy)
        for k, value in enumerate(values):
            ref[k] = value
    if rims:
        even = lax.rem(position, 2) == 0
        up = (slice(HALF, ROWS), slice((DEPTH - 1) * SEC, DEPTH * SEC))
        down = (slice(0, HALF), slice(0, SEC))

        @pl.when(even)
        def _():
            rims[0][...] = moved[up]
            rims[1][...] = moved[down]

        @pl.when(~even)
        def _():
            rims[0][...] = moved[down]
            rims[1][...] = moved[up]


def first_kernel(count, dist, pair_a, pair_b, wall, kind, inflow, *refs):
    moved, mine, other, rim_a, rim_b, state, faces, sums, sems = refs
    iy = lax.axis_index("vel")
    position = lax.axis_index("gx")
    even = lax.rem(position, 2) == 0
    left = state.at[pl.ds(HALF, HALF), pl.ds(0, SEC)]
    right = state.at[pl.ds(0, HALF), pl.ds((DEPTH + 1) * SEC, SEC)]
    main = pltpu.make_async_copy(dist, state.at[:, pl.ds(SEC, DEPTH * SEC)], sems.at[0])
    main.start()
    prepare_masks(wall, faces, position, count, iy >= VS // 2)

    def bring(one, two):
        copies = [
            pltpu.make_async_copy(pair_a, one, sems.at[1]),
            pltpu.make_async_copy(pair_b, two, sems.at[2]),
        ]
        for copy in copies:
            copy.start()
        for copy in copies:
            copy.wait()

    pl.when(even)(lambda: bring(right, left))
    pl.when(~even)(lambda: bring(left, right))
    main.wait()
    finish(
        state, faces, sums, wall, kind, inflow, moved, mine, other, (rim_a, rim_b), count
    )


def middle_kernel(count, rims, old, pair_a, pair_b, got, swapped, wall, kind, inflow, *refs):
    state, moved, mine, other = refs[:4]
    out_rims = refs[4 : 4 + 2 * rims]
    ghosts, coefs, lines, faces, sums, sems = refs[4 + 2 * rims :]
    iy = lax.axis_index("vel")
    position = lax.axis_index("gx")
    odd = lax.rem(position, 2)
    copies = [
        pltpu.make_async_copy(pair_a, ghosts.at[odd], sems.at[0]),
        pltpu.make_async_copy(pair_b, ghosts.at[1 - odd], sems.at[1]),
    ]
    for copy in copies:
        copy.start()
    prepare_masks(wall, faces, position, count, iy >= VS // 2)
    sub = lax.broadcasted_iota(jnp.int32, (8, 128), 0)
    pick = (sub >= TILES) == (lax.rem(iy, 2) == 0)
    values = [jnp.where(pick, got[k], swapped[k]) for k in range(13)]
    spread(coefs, coefficients(values, vy_of(iy)), 0)
    for copy in copies:
        copy.wait()
    relax_ghosts(ghosts, coefs, lines, state)
    finish(state, faces, sums, wall, kind, inflow, moved, mine, other, out_rims, count)


VM = pl.BlockSpec(memory_space=pltpu.VMEM)
ANY = pl.BlockSpec(memory_space=pl.ANY)
PARAMS = pltpu.CompilerParams(vmem_limit_bytes=12 << 20)
F32 = jnp.float32
WHOLE = jax.ShapeDtypeStruct((ROWS, DEPTH * SEC), F32)
WIDE = jax.ShapeDtypeStruct((ROWS, (DEPTH + 2) * SEC), F32)
RIM = jax.ShapeDtypeStruct((HALF, SEC), F32)
PART = jax.ShapeDtypeStruct((13, 8, 128), F32)
FACES = pltpu.VMEM((5, DEPTH + 1, TILES, 8, 128), F32)
SUMS = pltpu.VMEM((8, OWN, 8, 128), F32)
LINES = pltpu.VMEM((2, 3, 8, 128), F32)


def move_first(dist, pair_a, pair_b, wall, kind, inflow, count):
    outs = (WHOLE, PART, PART, RIM, RIM)
    return pl.pallas_call(
        functools.partial(first_kernel, count),
        out_shape=outs,
        in_specs=[ANY, ANY, ANY, VM, VM, VM],
        out_specs=(VM,) * len(outs),
        scratch_shapes=[
            pltpu.VMEM(WIDE.shape, F32), FACES, SUMS, pltpu.SemaphoreType.DMA((3,))
        ],
        compiler_params=PARAMS,
        name="move_first",
    )(dist, pair_a, pair_b, wall, kind, inflow)


def move_middle(state, pairs, got, swapped, wall, kind, inflow, count, rims):
    outs = (WIDE, WHOLE, PART, PART) + (RIM, RIM) * rims
    return pl.pallas_call(
        functools.partial(middle_kernel, count, rims),
        out_shape=outs,
        in_specs=[VM, ANY, ANY] + [VM] * 5,
        out_specs=(VM,) * len(outs),
        input_output_aliases={0: 0},
        scratch_shapes=[
            pltpu.VMEM((2, HALF, SEC), F32),
            pltpu.VMEM((9, 8, 8, 128), F32),
            LINES,
            FACES,
            SUMS,
            pltpu.SemaphoreType.DMA((2,)),
        ],
        compiler_params=PARAMS,
        name="move_middle",
    )(state, *pairs, got, swapped, wall, kind, inflow)[1:]


def relax_kernel(shift, moved, mine, other, state, coefs, lines):
    iy = lax.axis_index("vel")
    core = lax.rem(iy, 2)
    vy = vy_of(iy)
    for ref, half in ((mine, core), (other, 1 - core)):
        spread(coefs, coefficients([ref[k] for k in range(13)], vy), half * 8)
    relax(moved, coefs, lines, state, shift)


def relaxed(moved, mine, other, last):
    return pl.pallas_call(
        functools.partial(relax_kernel, 0 if last else SEC),
        out_shape=WHOLE if last else WIDE,
        in_specs=[VM, VM, VM],
        out_specs=VM,
        scratch_shapes=[pltpu.VMEM((9, OWN, 8, 128), F32), LINES],
        compiler_params=PARAMS,
        name="relax_last" if last else "relax",
    )(moved, mine, other)


def swap_cores(array):
    return lax.ppermute(array, "vel", [(i, i ^ 1) for i in range(VS)])


def shift_x(array, by):
    def mate(i):
        return i ^ (2 * by)

    return lax.ppermute(array, "vel", [(i, mate(i)) for i in range(VS)])


def all_moments(mine, other):
    value = mine + swap_cores(other)
    parts = [shift_x(value, by) for by in (1, 3, 2)]
    value = (value + parts[2]) + (parts[0] + parts[1])
    return value + lax.ppermute(value, "vel", [(i, i ^ 8) for i in range(VS)])


def swap_rims(pair_a, pair_b, count):
    near = [(i, i ^ 1) for i in range(count)]
    far = []
    for i in range(1, count - 1, 2):
        far += [(i, i + 1), (i + 1, i)]
    return lax.ppermute(pair_a, "gx", near), lax.ppermute(pair_b, "gx", far)


def swap_moments(half, count):
    pairs = []
    for v in range(0, VS, 2):
        for g in range(count - 1):
            one, two = (v + 1) * count + g, v * count + g + 1
            pairs += [(one, two), (two, one)]
    return lax.ppermute(half, ("vel", "gx"), pairs)


def per_device(distribution, wall_mask, boundary_kind, inflow):
    count = lax.axis_size("gx")
    inflow = inflow.reshape(2, 128)
    even = lax.rem(lax.axis_index("gx"), 2) == 0
    up = distribution[HALF:, (DEPTH - 1) * SEC :]
    down = distribution[:HALF, :SEC]
    pairs = swap_rims(jnp.where(even, up, down), jnp.where(even, down, up), count)
    outs = move_first(distribution, *pairs, wall_mask, boundary_kind, inflow, count)
    for step in range(STEPS):
        moved, mine, other = outs[:3]
        last = step + 1 == STEPS
        if not last:
            pairs = swap_rims(outs[3], outs[4], count)
        half = all_moments(mine, other)
        if last:
            return relaxed(moved, half, swap_cores(half), True)
        halo = swap_moments(half, count)
        state = relaxed(moved, half, swap_cores(half), False)
        outs = move_middle(
            state, pairs, halo, swap_cores(halo), wall_mask, boundary_kind, inflow, count,
            rims=step + 2 < STEPS,
        )


def solution(mesh):
    placed = (P("vel", "gx"), P(), P(), P("vel"))
    return jax.shard_map(
        per_device, mesh=mesh, in_specs=placed, out_specs=P("vel", "gx"), check_vma=False
    )
```

```python
import functools
import math

import jax
import jax.numpy as jnp
from jax import lax
from jax.experimental import pallas as pl
from jax.experimental.pallas import tpu as pltpu
from jax.sharding import PartitionSpec as P

VS = 16
NY = 16
NZ = 32
STEPS = 3
SEC = NY * NZ
DEPTH = 4
TILES = SEC // 128

LIMIT = 4.5
DT = 0.075
RATE = 0.6
KEEP = 1.0 - RATE
RATIO = 0.6666667
H = 2.0 * LIMIT / VS
WEIGHT = H**3
HALF = VS * VS // 2
ROWS = VS * VS
OWN = DEPTH * TILES


def vy_of(index):
    return -LIMIT + (index.astype(jnp.float32) + 0.5) * H


def sub_iota():
    return lax.broadcasted_iota(jnp.int32, (8, 128), 0).astype(jnp.float32)


def vz_tile(b):
    q = sub_iota()
    return (q + 0.5) * H if b else (q - 7.5) * H


def row(ref, *index):
    return jnp.broadcast_to(ref[index], (8, 128))


def prepare_masks(wall_ref, faces, position, count, forward):
    opened = []
    for slot in range(DEPTH + 2):
        at = position * DEPTH + slot - 1
        inside = jnp.logical_and(at >= 0, at < count * DEPTH)
        line = wall_ref[pl.ds(jnp.clip(at, 0, count * DEPTH - 1), 1), :]
        opened.append(jnp.where(inside, (1 - line).astype(jnp.float32), 1.0))
    zero = jnp.zeros_like(opened[0])
    o = jnp.concatenate(opened + [zero, zero], axis=0)
    cell = lax.broadcasted_iota(jnp.int32, (8, SEC), 1)
    up_x = o * pltpu.roll(o, 7, 0)
    up_y = o * pltpu.roll(o, SEC - NZ, 1) * (cell < SEC - NZ).astype(jnp.float32)
    up_z = o * pltpu.roll(o, SEC - 1, 1) * ((cell & (NZ - 1)) < NZ - 1).astype(jnp.float32)
    down_y = pltpu.roll(up_y, NZ, 1)
    down_z = pltpu.roll(up_z, 1, 1)
    planes = [
        up_x, jnp.where(forward, up_y, down_y), jnp.where(forward, down_y, up_y), down_z, up_z
    ]
    for k, plane in enumerate(planes):
        for slot in range(DEPTH + 1):
            for t in range(TILES):
                line = plane[slot : slot + 1, t * 128 : (t + 1) * 128]
                faces[k, slot, t] = jnp.broadcast_to(line, (8, 128))


def fill_ends(state, inflow_ref, kind_ref, position, count):
    lane = lax.broadcasted_iota(jnp.int32, (8, 128), 1)
    sub = lax.broadcasted_iota(jnp.int32, (8, 128), 0)

    def one(side, base, inner, outer):
        @pl.when(position == (0 if side == 0 else count - 1))
        def _():
            for tile in range(HALF // 8):
                start = base + tile * 8
                line = row(inflow_ref, pl.ds(start // 128, 1), slice(None))
                picked = jnp.where(lane == sub + start % 128, line, 0.0)
                column = jnp.sum(picked, axis=1, keepdims=True)
                for t in range(TILES):
                    kind = row(kind_ref, pl.ds(side, 1), pl.ds(t * 128, 128))
                    inside = state[pl.ds(start, 8), pl.ds(inner * SEC + t * 128, 128)]
                    state[pl.ds(start, 8), pl.ds(outer * SEC + t * 128, 128)] = jnp.where(
                        kind == 1, jnp.broadcast_to(column, (8, 128)), inside
                    )

    one(0, HALF, 1, 0)
    one(1, 0, DEPTH, DEPTH + 1)


def transport(state, faces, moved, sums, iy):
    forward = iy >= VS // 2
    speed_y = jnp.abs(vy_of(iy)) * (KEEP * DT)
    lane = lax.broadcasted_iota(jnp.int32, (8, 128), 1)
    take = jnp.logical_or(
        jnp.logical_and(forward, lane < NZ), jnp.logical_and(~forward, lane >= 128 - NZ)
    )
    shift_y = jnp.where(forward, NZ, 128 - NZ)

    def section(i, carry):
        total = [[None] * 8 for _ in range(TILES)]
        tiles = [jnp.where(forward, k, TILES - 1 - k) for k in range(TILES)]
        lanes = [pl.multiple_of(t * 128, 128) for t in tiles]
        for b in range(2):
            vz = vz_tile(b)
            az = jnp.abs(vz) * (KEEP * DT)
            below = [faces[0, i, t] for t in tiles]
            above = [faces[0, i + 1, t] for t in tiles]
            keep, in_y, in_z = [], [], []
            for t in tiles:
                out_y = faces[1, i + 1, t]
                out_z = faces[4 if b else 3, i + 1, t]
                keep.append(KEEP - speed_y * out_y - az * out_z)
                in_y.append(speed_y * faces[2, i + 1, t])
                in_z.append(az * faces[3 if b else 4, i + 1, t])
            acc = [[None] * 4 for _ in range(TILES)]
            for a in range(VS // 2):
                speed = (a + 0.5) * H
                cx = KEEP * DT * speed
                lo = [cx * x for x in below]
                hi = [cx * x for x in above]
                both = []
                for sign in range(2):
                    start = sign * HALF + a * VS + 8 * b
                    here, shifted = [], []
                    for l in lanes:
                        at = pl.multiple_of((i + 1) * SEC + l, 128)
                        value = state[start : start + 8, pl.ds(at, 128)]
                        here.append(value)
                        shifted.append(pltpu.roll(value, shift_y, 1))
                    result = []
                    for k, l in enumerate(lanes):
                        at = pl.multiple_of((i + (0 if sign else 2)) * SEC + l, 128)
                        before = state[start : start + 8, pl.ds(at, 128)]
                        out_x, in_x = (hi[k], lo[k]) if sign else (lo[k], hi[k])
                        along_y = jnp.where(take, shifted[k - 1], shifted[k]) if k else shifted[k]
                        along_z = pltpu.roll(here[k], 1 if b else 127, 1)
                        value = (
                            here[k] * (keep[k] - out_x)
                            + before * in_x
                            + along_y * in_y[k]
                            + along_z * in_z[k]
                        )
                        at = pl.multiple_of(i * SEC + l, 128)
                        moved[start : start + 8, pl.ds(at, 128)] = value
                        result.append(value)
                    both.append(result)
                for k in range(TILES):
                    even = both[1][k] + both[0][k]
                    odd = both[1][k] - both[0][k]
                    terms = [even, speed * odd, (speed * speed) * even, (speed**3) * odd]
                    for p in range(4):
                        acc[k][p] = terms[p] if acc[k][p] is None else acc[k][p] + terms[p]
            vz2 = vz * vz
            for k in range(TILES):
                a0, a1, a2, a3 = acc[k]
                terms = [
                    a0, a1, vz * a0, a2, vz2 * a0, vz * a1,
                    a3 + vz2 * a1, vz * (a2 + vz2 * a0),
                ]
                for p in range(8):
                    total[k][p] = terms[p] if b == 0 else total[k][p] + terms[p]
        for k, t in enumerate(tiles):
            for p in range(8):
                sums[p, i * TILES + t] = total[k][p]
        return carry

    lax.fori_loop(0, DEPTH, section, 0)


def fold(sums, p, first):
    sub = lax.broadcasted_iota(jnp.int32, (8, 128), 0)
    values = [sums[p, first + t] for t in range(8)]
    for step in (4, 2, 1):
        low = (sub & step) == 0
        merged = []
        for t in range(step):
            a, b = values[t], values[t + step]
            a = a + pltpu.roll(a, 8 - step, 0)
            b = b + pltpu.roll(b, step, 0)
            merged.append(jnp.where(low, a, b))
        values = merged
    return values[0]


def expand(sums, vy):
    s0, sx, sz, sxx, szz, sxz, ex, ez = sums
    y2 = vy * vy
    return [
        s0, sx, vy * s0, sz, sxx, y2 * s0, szz, vy * sx, sxz, vy * sz,
        ex + y2 * sx, vy * (sxx + szz + y2 * s0), ez + y2 * sz,
    ]


def coefficients(m, vy):
    n = m[0]
    inverse = 1.0 / n
    ux, uy, uz = m[1] * inverse, m[2] * inverse, m[3] * inverse
    xx, yy, zz, xy, xz, yz = m[4:10]
    u2 = ux * ux + uy * uy + uz * uz
    trace = xx + yy + zz
    temp = (trace * inverse - u2) / 3.0
    px = xx * ux + xy * uy + xz * uz
    py = xy * ux + yy * uy + yz * uz
    pz = xz * ux + yz * uy + zz * uz
    common = 2.0 * n * u2 - trace
    qx = 0.5 * (m[10] - 2.0 * px + common * ux)
    qy = 0.5 * (m[11] - 2.0 * py + common * uy)
    qz = 0.5 * (m[12] - 2.0 * pz + common * uz)
    inv_t = 1.0 / temp
    kappa = (1.0 - RATIO) / 5.0 * inverse * inv_t * inv_t
    s = kappa * inv_t
    i2t = 0.5 * inv_t
    cy = vy - uy
    level = 0.5 * (
        jnp.log(n) - 1.5 * jnp.log((2.0 * math.pi) * temp) - cy * cy * i2t
    )
    return [ux, uz, i2t, level, qx, qz, s, qy * cy, s * cy * cy - 5.0 * kappa]


def point(coefs, j):
    return [coefs[k, j] for k in range(9)]


def across(values, sign):
    ux, uz, i2t, level, qx, qz, s, qyc, rest = values
    cx = (sub_iota() + 0.5) * (H if sign else -H) - ux
    c2 = cx * cx
    return jnp.exp(level - c2 * i2t) * RATE, qx * cx + qyc, s * c2 + rest


def along(values, b):
    ux, uz, i2t, level, qx, qz, s, qyc, rest = values
    cz = vz_tile(b) - uz
    c2 = cz * cz
    return jnp.exp(level - c2 * i2t), qz * cz, s * c2


def store_lines(lines, values, sign):
    for k, value in enumerate(across(values, sign)):
        lines[sign, k] = value


def relax_rows(read, write, lines, fixed, sign):
    for a in range(VS // 2):
        ex, qa, sa = [row(lines, sign, k, pl.ds(a, 1), slice(None)) for k in range(3)]
        for b in range(2):
            ez, qb, sb = fixed[b]
            start = a * VS + 8 * b
            write(start, read(start) + (ex * ez) * (1.0 + (qa + qb) * (sa + sb)))


def relax(moved, coefs, lines, state, shift):
    def tile(j, carry):
        values = point(coefs, j)
        for sign in range(2):
            store_lines(lines, values, sign)
        fixed = [along(values, b) for b in range(2)]
        at = pl.multiple_of(j * 128, 128)
        to = pl.multiple_of(j * 128 + shift, 128)
        for sign in range(2):
            base = sign * HALF

            def read(start):
                return moved[base + start : base + start + 8, pl.ds(at, 128)]

            def write(start, value):
                state[base + start : base + start + 8, pl.ds(to, 128)] = value

            relax_rows(read, write, lines, fixed, sign)
        return carry

    lax.fori_loop(0, OWN, tile, 0)


def relax_ghosts(ghosts, coefs, lines, state):
    def tile(t, carry):
        at = pl.multiple_of(t * 128, 128)
        for sign in range(2):
            values = point(coefs, t + TILES * sign)
            store_lines(lines, values, sign)
            fixed = [along(values, b) for b in range(2)]
            base = sign * HALF
            to = pl.multiple_of(t * 128 + (0 if sign else (DEPTH + 1) * SEC), 128)

            def read(start):
                return ghosts[sign, start : start + 8, pl.ds(at, 128)]

            def write(start, value):
                state[base + start : base + start + 8, pl.ds(to, 128)] = value

            relax_rows(read, write, lines, fixed, sign)
        return carry

    lax.fori_loop(0, TILES, tile, 0)


def spread(coefs, values, first):
    for k, value in enumerate(values):
        for t in range(8):
            coefs[k, first + t] = jnp.broadcast_to(value[t : t + 1], (8, 128))


def finish(state, faces, sums, kind, inflow, moved, mine, other, rims, count):
    iy = lax.axis_index("vel")
    position = lax.axis_index("gx")
    fill_ends(state, inflow, kind, position, count)
    transport(state, faces, moved, sums, iy)
    core = lax.rem(iy, 2)
    vy = vy_of(iy)
    for ref, first in ((mine, core * 8), (other, 8 - core * 8)):
        values = expand([fold(sums, p, first) * (WEIGHT / KEEP) for p in range(8)], vy)
        for k, value in enumerate(values):
            ref[k] = value
    if rims:
        even = lax.rem(position, 2) == 0
        up = (slice(HALF, ROWS), slice((DEPTH - 1) * SEC, DEPTH * SEC))
        down = (slice(0, HALF), slice(0, SEC))

        @pl.when(even)
        def _():
            rims[0][...] = moved[up]
            rims[1][...] = moved[down]

        @pl.when(~even)
        def _():
            rims[0][...] = moved[down]
            rims[1][...] = moved[up]


def prepare_kernel(count, dist, wall, state, faces, sem):
    load = pltpu.make_async_copy(dist, state.at[:, pl.ds(SEC, DEPTH * SEC)], sem.at[0])
    load.start()
    forward = lax.axis_index("vel") >= VS // 2
    prepare_masks(wall, faces, lax.axis_index("gx"), count, forward)
    load.wait()


def first_kernel(count, old, pair_a, pair_b, faces, kind, inflow, *refs):
    state, moved, mine, other, rim_a, rim_b, sums, sems = refs
    even = lax.rem(lax.axis_index("gx"), 2) == 0
    left = state.at[pl.ds(HALF, HALF), pl.ds(0, SEC)]
    right = state.at[pl.ds(0, HALF), pl.ds((DEPTH + 1) * SEC, SEC)]

    def bring(one, two):
        copies = [
            pltpu.make_async_copy(pair_a, one, sems.at[0]),
            pltpu.make_async_copy(pair_b, two, sems.at[1]),
        ]
        for copy in copies:
            copy.start()
        for copy in copies:
            copy.wait()

    pl.when(even)(lambda: bring(right, left))
    pl.when(~even)(lambda: bring(left, right))
    finish(state, faces, sums, kind, inflow, moved, mine, other, (rim_a, rim_b), count)


def middle_kernel(count, rims, old, pair_a, pair_b, got, swapped, faces, kind, inflow, *refs):
    state, moved, mine, other = refs[:4]
    out_rims = refs[4 : 4 + 2 * rims]
    ghosts, coefs, lines, sums, sems = refs[4 + 2 * rims :]
    iy = lax.axis_index("vel")
    position = lax.axis_index("gx")
    odd = lax.rem(position, 2)
    copies = [
        pltpu.make_async_copy(pair_a, ghosts.at[odd], sems.at[0]),
        pltpu.make_async_copy(pair_b, ghosts.at[1 - odd], sems.at[1]),
    ]
    for copy in copies:
        copy.start()
    sub = lax.broadcasted_iota(jnp.int32, (8, 128), 0)
    pick = (sub >= TILES) == (lax.rem(iy, 2) == 0)
    values = [jnp.where(pick, got[k], swapped[k]) for k in range(13)]
    spread(coefs, coefficients(values, vy_of(iy)), 0)
    for copy in copies:
        copy.wait()
    relax_ghosts(ghosts, coefs, lines, state)
    finish(state, faces, sums, kind, inflow, moved, mine, other, out_rims, count)


VM = pl.BlockSpec(memory_space=pltpu.VMEM)
ANY = pl.BlockSpec(memory_space=pl.ANY)
PARAMS = pltpu.CompilerParams(vmem_limit_bytes=12 << 20)
F32 = jnp.float32
WHOLE = jax.ShapeDtypeStruct((ROWS, DEPTH * SEC), F32)
WIDE = jax.ShapeDtypeStruct((ROWS, (DEPTH + 2) * SEC), F32)
RIM = jax.ShapeDtypeStruct((HALF, SEC), F32)
PART = jax.ShapeDtypeStruct((13, 8, 128), F32)
FACES = jax.ShapeDtypeStruct((5, DEPTH + 1, TILES, 8, 128), F32)
SUMS = pltpu.VMEM((8, OWN, 8, 128), F32)
LINES = pltpu.VMEM((2, 3, 8, 128), F32)


def prepare(dist, wall, count):
    return pl.pallas_call(
        functools.partial(prepare_kernel, count),
        out_shape=(WIDE, FACES),
        in_specs=[ANY, VM],
        out_specs=(VM, VM),
        scratch_shapes=[pltpu.SemaphoreType.DMA((1,))],
        compiler_params=pltpu.CompilerParams(vmem_limit_bytes=16 << 20),
        name="prepare",
    )(dist, wall)


def move_first(state, pair_a, pair_b, faces, kind, inflow, count):
    outs = (WIDE, WHOLE, PART, PART, RIM, RIM)
    return pl.pallas_call(
        functools.partial(first_kernel, count),
        out_shape=outs,
        in_specs=[VM, ANY, ANY, VM, VM, VM],
        out_specs=(VM,) * len(outs),
        input_output_aliases={0: 0},
        scratch_shapes=[SUMS, pltpu.SemaphoreType.DMA((2,))],
        compiler_params=PARAMS,
        name="move_first",
    )(state, pair_a, pair_b, faces, kind, inflow)[1:]


def move_middle(state, pairs, got, swapped, faces, kind, inflow, count, rims):
    outs = (WIDE, WHOLE, PART, PART) + (RIM, RIM) * rims
    return pl.pallas_call(
        functools.partial(middle_kernel, count, rims),
        out_shape=outs,
        in_specs=[VM, ANY, ANY] + [VM] * 5,
        out_specs=(VM,) * len(outs),
        input_output_aliases={0: 0},
        scratch_shapes=[
            pltpu.VMEM((2, HALF, SEC), F32),
            pltpu.VMEM((9, 8, 8, 128), F32),
            LINES,
            SUMS,
            pltpu.SemaphoreType.DMA((2,)),
        ],
        compiler_params=PARAMS,
        name="move_middle",
    )(state, *pairs, got, swapped, faces, kind, inflow)[1:]


def relax_kernel(shift, moved, mine, other, state, coefs, lines):
    iy = lax.axis_index("vel")
    core = lax.rem(iy, 2)
    vy = vy_of(iy)
    for ref, half in ((mine, core), (other, 1 - core)):
        spread(coefs, coefficients([ref[k] for k in range(13)], vy), half * 8)
    relax(moved, coefs, lines, state, shift)


def relaxed(moved, mine, other, last):
    return pl.pallas_call(
        functools.partial(relax_kernel, 0 if last else SEC),
        out_shape=WHOLE if last else WIDE,
        in_specs=[VM, VM, VM],
        out_specs=VM,
        scratch_shapes=[pltpu.VMEM((9, OWN, 8, 128), F32), LINES],
        compiler_params=PARAMS,
        name="relax_last" if last else "relax",
    )(moved, mine, other)


def swap_cores(array):
    return lax.ppermute(array, "vel", [(i, i ^ 1) for i in range(VS)])


def shift_x(array, by):
    def mate(i):
        return i ^ (2 * by)

    return lax.ppermute(array, "vel", [(i, mate(i)) for i in range(VS)])


def all_moments(mine, other, rims):
    value = mine + swap_cores(other)
    value = value + lax.ppermute(value, "vel", [(i, i ^ 8) for i in range(VS)])
    if rims:
        value, *rims = lax.optimization_barrier((value, *rims))
    parts = [shift_x(value, by) for by in (1, 3, 2)]
    return (value + parts[2]) + (parts[0] + parts[1]), rims


def swap_rims(pair_a, pair_b, count):
    near = [(i, i ^ 1) for i in range(count)]
    far = []
    for i in range(1, count - 1, 2):
        far += [(i, i + 1), (i + 1, i)]
    return lax.ppermute(pair_a, "gx", near), lax.ppermute(pair_b, "gx", far)


def swap_moments(half, count):
    pairs = []
    for v in range(0, VS, 2):
        for g in range(count - 1):
            one, two = (v + 1) * count + g, v * count + g + 1
            pairs += [(one, two), (two, one)]
    return lax.ppermute(half, ("vel", "gx"), pairs)


def per_device(distribution, wall_mask, boundary_kind, inflow):
    count = lax.axis_size("gx")
    inflow = inflow.reshape(2, 128)
    even = lax.rem(lax.axis_index("gx"), 2) == 0
    up = distribution[HALF:, (DEPTH - 1) * SEC :]
    down = distribution[:HALF, :SEC]
    pairs = swap_rims(jnp.where(even, up, down), jnp.where(even, down, up), count)
    state, faces = prepare(distribution, wall_mask, count)
    outs = move_first(state, *pairs, faces, boundary_kind, inflow, count)
    for step in range(STEPS):
        moved, mine, other = outs[:3]
        last = step + 1 == STEPS
        half, rims = all_moments(mine, other, outs[3:])
        if last:
            return relaxed(moved, half, swap_cores(half), True)
        pairs = swap_rims(*rims, count)
        halo = swap_moments(half, count)
        state = relaxed(moved, half, swap_cores(half), False)
        halo, state = lax.optimization_barrier((halo, state))
        outs = move_middle(
            state, pairs, halo, swap_cores(halo), faces, boundary_kind, inflow, count,
            rims=step + 2 < STEPS,
        )


def solution(mesh):
    placed = (P("vel", "gx"), P(), P(), P("vel"))
    return jax.shard_map(
        per_device, mesh=mesh, in_specs=placed, out_specs=P("vel", "gx"), check_vma=False
    )
```

```python
import functools
import math

import jax
import jax.numpy as jnp
from jax import lax
from jax.experimental import pallas as pl
from jax.experimental.pallas import tpu as pltpu
from jax.sharding import PartitionSpec as P

VS = 16
NY = 16
NZ = 32
STEPS = 3
SEC = NY * NZ
DEPTH = 4
TILES = SEC // 128

LIMIT = 4.5
DT = 0.075
RATE = 0.6
KEEP = 1.0 - RATE
RATIO = 0.6666667
H = 2.0 * LIMIT / VS
WEIGHT = H**3
HALF = VS * VS // 2
ROWS = VS * VS
OWN = DEPTH * TILES


def vy_of(index):
    return -LIMIT + (index.astype(jnp.float32) + 0.5) * H


def sub_iota():
    return lax.broadcasted_iota(jnp.int32, (8, 128), 0).astype(jnp.float32)


def vz_tile(b):
    q = sub_iota()
    return (q + 0.5) * H if b else (q - 7.5) * H


def row(ref, *index):
    return jnp.broadcast_to(ref[index], (8, 128))


def prepare_masks(wall_ref, faces, position, count, forward):
    opened = []
    for slot in range(DEPTH + 2):
        at = position * DEPTH + slot - 1
        inside = jnp.logical_and(at >= 0, at < count * DEPTH)
        line = wall_ref[pl.ds(jnp.clip(at, 0, count * DEPTH - 1), 1), :]
        opened.append(jnp.where(inside, (1 - line).astype(jnp.float32), 1.0))
    zero = jnp.zeros_like(opened[0])
    o = jnp.concatenate(opened + [zero, zero], axis=0)
    cell = lax.broadcasted_iota(jnp.int32, (8, SEC), 1)
    up_x = o * pltpu.roll(o, 7, 0)
    up_y = o * pltpu.roll(o, SEC - NZ, 1) * (cell < SEC - NZ).astype(jnp.float32)
    up_z = o * pltpu.roll(o, SEC - 1, 1) * ((cell & (NZ - 1)) < NZ - 1).astype(jnp.float32)
    down_y = pltpu.roll(up_y, NZ, 1)
    down_z = pltpu.roll(up_z, 1, 1)
    planes = [
        up_x, jnp.where(forward, up_y, down_y), jnp.where(forward, down_y, up_y), down_z, up_z
    ]
    for k, plane in enumerate(planes):
        for slot in range(DEPTH + 1):
            for t in range(TILES):
                line = plane[slot : slot + 1, t * 128 : (t + 1) * 128]
                faces[k, slot, t] = jnp.broadcast_to(line, (8, 128))


def fill_ends(state, inflow_ref, kind_ref, position, count):
    lane = lax.broadcasted_iota(jnp.int32, (8, 128), 1)
    sub = lax.broadcasted_iota(jnp.int32, (8, 128), 0)

    def one(side, base, inner, outer):
        @pl.when(position == (0 if side == 0 else count - 1))
        def _():
            for tile in range(HALF // 8):
                start = base + tile * 8
                line = row(inflow_ref, pl.ds(start // 128, 1), slice(None))
                picked = jnp.where(lane == sub + start % 128, line, 0.0)
                column = jnp.sum(picked, axis=1, keepdims=True)
                for t in range(TILES):
                    kind = row(kind_ref, pl.ds(side, 1), pl.ds(t * 128, 128))
                    inside = state[pl.ds(start, 8), pl.ds(inner * SEC + t * 128, 128)]
                    state[pl.ds(start, 8), pl.ds(outer * SEC + t * 128, 128)] = jnp.where(
                        kind == 1, jnp.broadcast_to(column, (8, 128)), inside
                    )

    one(0, HALF, 1, 0)
    one(1, 0, DEPTH, DEPTH + 1)


def transport(state, faces, moved, sums, iy):
    forward = iy >= VS // 2
    speed_y = jnp.abs(vy_of(iy)) * (KEEP * DT)
    lane = lax.broadcasted_iota(jnp.int32, (8, 128), 1)
    take = jnp.logical_or(
        jnp.logical_and(forward, lane < NZ), jnp.logical_and(~forward, lane >= 128 - NZ)
    )
    shift_y = jnp.where(forward, NZ, 128 - NZ)

    def section(i, carry):
        total = [[None] * 8 for _ in range(TILES)]
        tiles = [jnp.where(forward, k, TILES - 1 - k) for k in range(TILES)]
        lanes = [pl.multiple_of(t * 128, 128) for t in tiles]
        for b in range(2):
            vz = vz_tile(b)
            az = jnp.abs(vz) * (KEEP * DT)
            below = [faces[0, i, t] for t in tiles]
            above = [faces[0, i + 1, t] for t in tiles]
            keep, in_y, in_z = [], [], []
            for t in tiles:
                out_y = faces[1, i + 1, t]
                out_z = faces[4 if b else 3, i + 1, t]
                keep.append(KEEP - speed_y * out_y - az * out_z)
                in_y.append(speed_y * faces[2, i + 1, t])
                in_z.append(az * faces[3 if b else 4, i + 1, t])
            acc = [[None] * 4 for _ in range(TILES)]
            for a in range(VS // 2):
                speed = (a + 0.5) * H
                cx = KEEP * DT * speed
                lo = [cx * x for x in below]
                hi = [cx * x for x in above]
                both = []
                for sign in range(2):
                    start = sign * HALF + a * VS + 8 * b
                    here, shifted = [], []
                    for l in lanes:
                        at = pl.multiple_of((i + 1) * SEC + l, 128)
                        value = state[start : start + 8, pl.ds(at, 128)]
                        here.append(value)
                        shifted.append(pltpu.roll(value, shift_y, 1))
                    result = []
                    for k, l in enumerate(lanes):
                        at = pl.multiple_of((i + (0 if sign else 2)) * SEC + l, 128)
                        before = state[start : start + 8, pl.ds(at, 128)]
                        out_x, in_x = (hi[k], lo[k]) if sign else (lo[k], hi[k])
                        along_y = jnp.where(take, shifted[k - 1], shifted[k]) if k else shifted[k]
                        along_z = pltpu.roll(here[k], 1 if b else 127, 1)
                        value = (
                            here[k] * (keep[k] - out_x)
                            + before * in_x
                            + along_y * in_y[k]
                            + along_z * in_z[k]
                        )
                        at = pl.multiple_of(i * SEC + l, 128)
                        moved[start : start + 8, pl.ds(at, 128)] = value
                        result.append(value)
                    both.append(result)
                for k in range(TILES):
                    even = both[1][k] + both[0][k]
                    odd = both[1][k] - both[0][k]
                    terms = [even, speed * odd, (speed * speed) * even, (speed**3) * odd]
                    for p in range(4):
                        acc[k][p] = terms[p] if acc[k][p] is None else acc[k][p] + terms[p]
            vz2 = vz * vz
            for k in range(TILES):
                a0, a1, a2, a3 = acc[k]
                terms = [
                    a0, a1, vz * a0, a2, vz2 * a0, vz * a1,
                    a3 + vz2 * a1, vz * (a2 + vz2 * a0),
                ]
                for p in range(8):
                    total[k][p] = terms[p] if b == 0 else total[k][p] + terms[p]
        for k, t in enumerate(tiles):
            for p in range(8):
                sums[p, i * TILES + t] = total[k][p]
        return carry

    lax.fori_loop(0, DEPTH, section, 0)


def fold(sums, p, first):
    sub = lax.broadcasted_iota(jnp.int32, (8, 128), 0)
    values = [sums[p, first + t] for t in range(8)]
    for step in (4, 2, 1):
        low = (sub & step) == 0
        merged = []
        for t in range(step):
            a, b = values[t], values[t + step]
            a = a + pltpu.roll(a, 8 - step, 0)
            b = b + pltpu.roll(b, step, 0)
            merged.append(jnp.where(low, a, b))
        values = merged
    return values[0]


def expand(sums, vy):
    s0, sx, sz, sxx, szz, sxz, ex, ez = sums
    y2 = vy * vy
    return [
        s0, sx, vy * s0, sz, sxx, y2 * s0, szz, vy * sx, sxz, vy * sz,
        ex + y2 * sx, vy * (sxx + szz + y2 * s0), ez + y2 * sz,
    ]


def coefficients(m, vy):
    n = m[0]
    inverse = 1.0 / n
    ux, uy, uz = m[1] * inverse, m[2] * inverse, m[3] * inverse
    xx, yy, zz, xy, xz, yz = m[4:10]
    u2 = ux * ux + uy * uy + uz * uz
    trace = xx + yy + zz
    temp = (trace * inverse - u2) / 3.0
    px = xx * ux + xy * uy + xz * uz
    py = xy * ux + yy * uy + yz * uz
    pz = xz * ux + yz * uy + zz * uz
    common = 2.0 * n * u2 - trace
    qx = 0.5 * (m[10] - 2.0 * px + common * ux)
    qy = 0.5 * (m[11] - 2.0 * py + common * uy)
    qz = 0.5 * (m[12] - 2.0 * pz + common * uz)
    inv_t = 1.0 / temp
    kappa = (1.0 - RATIO) / 5.0 * inverse * inv_t * inv_t
    s = kappa * inv_t
    i2t = 0.5 * inv_t
    cy = vy - uy
    level = 0.5 * (
        jnp.log(n) - 1.5 * jnp.log((2.0 * math.pi) * temp) - cy * cy * i2t
    )
    return [ux, uz, i2t, level, qx, qz, s, qy * cy, s * cy * cy - 5.0 * kappa]


def point(coefs, j):
    return [coefs[k, j] for k in range(9)]


def across(values, sign):
    ux, uz, i2t, level, qx, qz, s, qyc, rest = values
    cx = (sub_iota() + 0.5) * (H if sign else -H) - ux
    c2 = cx * cx
    return jnp.exp(level - c2 * i2t) * RATE, qx * cx + qyc, s * c2 + rest


def along(values, b):
    ux, uz, i2t, level, qx, qz, s, qyc, rest = values
    cz = vz_tile(b) - uz
    c2 = cz * cz
    return jnp.exp(level - c2 * i2t), qz * cz, s * c2


def store_lines(lines, values, sign):
    for k, value in enumerate(across(values, sign)):
        lines[sign, k] = value


def relax_rows(read, write, lines, fixed, sign):
    for a in range(VS // 2):
        ex, qa, sa = [row(lines, sign, k, pl.ds(a, 1), slice(None)) for k in range(3)]
        for b in range(2):
            ez, qb, sb = fixed[b]
            start = a * VS + 8 * b
            write(start, read(start) + (ex * ez) * (1.0 + (qa + qb) * (sa + sb)))


def relax(moved, coefs, lines, state, shift):
    def tile(j, carry):
        values = point(coefs, j)
        for sign in range(2):
            store_lines(lines, values, sign)
        fixed = [along(values, b) for b in range(2)]
        at = pl.multiple_of(j * 128, 128)
        to = pl.multiple_of(j * 128 + shift, 128)
        for sign in range(2):
            base = sign * HALF

            def read(start):
                return moved[base + start : base + start + 8, pl.ds(at, 128)]

            def write(start, value):
                state[base + start : base + start + 8, pl.ds(to, 128)] = value

            relax_rows(read, write, lines, fixed, sign)
        return carry

    lax.fori_loop(0, OWN, tile, 0)


def relax_ghosts(ghosts, coefs, lines, state):
    def tile(t, carry):
        at = pl.multiple_of(t * 128, 128)
        for sign in range(2):
            values = point(coefs, t + TILES * sign)
            store_lines(lines, values, sign)
            fixed = [along(values, b) for b in range(2)]
            base = sign * HALF
            to = pl.multiple_of(t * 128 + (0 if sign else (DEPTH + 1) * SEC), 128)

            def read(start):
                return ghosts[sign, start : start + 8, pl.ds(at, 128)]

            def write(start, value):
                state[base + start : base + start + 8, pl.ds(to, 128)] = value

            relax_rows(read, write, lines, fixed, sign)
        return carry

    lax.fori_loop(0, TILES, tile, 0)


def spread(coefs, values, first):
    for k, value in enumerate(values):
        for t in range(8):
            coefs[k, first + t] = jnp.broadcast_to(value[t : t + 1], (8, 128))


def finish(state, faces, sums, kind, inflow, moved, mine, other, rims, count):
    iy = lax.axis_index("vel")
    position = lax.axis_index("gx")
    fill_ends(state, inflow, kind, position, count)
    transport(state, faces, moved, sums, iy)
    core = lax.rem(iy, 2)
    vy = vy_of(iy)
    for ref, first in ((mine, core * 8), (other, 8 - core * 8)):
        values = expand([fold(sums, p, first) * (WEIGHT / KEEP) for p in range(8)], vy)
        for k, value in enumerate(values):
            ref[k] = value
    if rims:
        even = lax.rem(position, 2) == 0
        up = (slice(HALF, ROWS), slice((DEPTH - 1) * SEC, DEPTH * SEC))
        down = (slice(0, HALF), slice(0, SEC))

        @pl.when(even)
        def _():
            rims[0][...] = moved[up]
            rims[1][...] = moved[down]

        @pl.when(~even)
        def _():
            rims[0][...] = moved[down]
            rims[1][...] = moved[up]


def low_rows():
    return lax.broadcasted_iota(jnp.int32, (8, 128), 0) < TILES


def pack(values):
    low = low_rows()
    values = values + [jnp.zeros_like(values[0])]
    return [jnp.where(low, values[k], values[k + 1]) for k in range(0, 14, 2)]


def doubled(packed, k):
    turned = pltpu.roll(packed, TILES, 0)
    if k % 2:
        return jnp.where(low_rows(), turned, packed)
    return jnp.where(low_rows(), packed, turned)


def rim_flux(state, sums):
    def tile(t, carry):
        for sign in range(2):
            at = pl.multiple_of((DEPTH if sign else 1) * SEC + t * 128, 128)
            total = [None] * 8
            for b in range(2):
                vz = vz_tile(b)
                vz2 = vz * vz
                acc = [None] * 4
                for a in range(VS // 2):
                    speed = (a + 0.5) * H
                    start = sign * HALF + a * VS + 8 * b
                    value = state[start : start + 8, pl.ds(at, 128)] * speed
                    for p in range(4):
                        acc[p] = value if acc[p] is None else acc[p] + value
                        value = value * (speed if sign else -speed)
                a0, a1, a2, a3 = acc
                terms = [
                    a0, a1, vz * a0, a2, vz2 * a0, vz * a1,
                    a3 + vz2 * a1, vz * (a2 + vz2 * a0),
                ]
                total = terms if b == 0 else [x + y for x, y in zip(total, terms)]
            for p in range(8):
                sums[p, TILES * sign + t] = total[p]
        return carry

    lax.fori_loop(0, TILES, tile, 0)


def first_kernel(count, dist, wall, kind, inflow, *refs):
    faces, moved, mine, other, rim_a, rim_b, state, sums, flux, sems = refs
    iy = lax.axis_index("vel")
    position = lax.axis_index("gx")
    loads = [
        pltpu.make_async_copy(
            dist.at[:, pl.ds(i * SEC, SEC)], state.at[:, pl.ds((i + 1) * SEC, SEC)], sems.at[i]
        )
        for i in range(DEPTH)
    ]
    for load in loads:
        load.start()
    prepare_masks(wall, faces, position, count, iy >= VS // 2)
    state[HALF:, :SEC] = jnp.zeros((HALF, SEC), F32)
    state[:HALF, (DEPTH + 1) * SEC :] = jnp.zeros((HALF, SEC), F32)
    for load in loads:
        load.wait()
    finish(state, faces, sums, kind, inflow, moved, mine, other, (rim_a, rim_b), count)
    rim_flux(state, flux)
    values = expand([fold(flux, p, 0) * (WEIGHT / KEEP) for p in range(8)], vy_of(iy))
    turned = [pltpu.roll(value, TILES, 0) for value in values]
    low = low_rows()
    halves = [
        pack([value if k % 2 == 0 else turned[k] for k, value in enumerate(values)]),
        pack([turned[k] if k % 2 == 0 else value for k, value in enumerate(values)]),
    ]
    inner = lax.rem(iy, 2) == 0
    for k in range(7):
        mine[13 + k] = jnp.where(inner, halves[0][k], halves[1][k])
        other[13 + k] = jnp.where(inner, halves[1][k], halves[0][k])


def y_kernel(first, value, across_y, near, far, *refs):
    out = refs[-1]
    low = low_rows()
    inner = lax.rem(lax.axis_index("vel"), 2) == 0
    own_rows = low == inner
    own = [value[k] + across_y[k] for k in range(20 if first else 13)]
    halo = [near[k] + far[k] for k in range(20 if first else 13)]
    if first:
        faces = refs[0]
        sub = lax.broadcasted_iota(jnp.int32, (8, 128), 0)
        edge = jnp.zeros((8, 128), F32)
        for t in range(TILES):
            edge = jnp.where(sub == t, faces[0, 0, t], edge)
            edge = jnp.where(sub == t + TILES, faces[0, DEPTH, t], edge)
        edge = edge * (KEEP * DT)
        turned = pltpu.roll(edge, TILES, 0)
        for k in range(13):
            add = edge * doubled(halo[13 + k // 2], k)
            own[k] = own[k] + jnp.where(own_rows, add, 0.0)
        for k in range(13):
            halo[k] = halo[k] + turned * doubled(own[13 + k // 2], k)
    for k in range(13):
        out[k] = own[k]
    both = [jnp.where(own_rows, pltpu.roll(halo[k], TILES, 0), halo[k]) for k in range(13)]
    for k, value in enumerate(pack(both)):
        out[13 + k] = value


def add_rims(ghosts, faces, state):
    def tile(t, carry):
        at = pl.multiple_of(t * 128, 128)
        for sign in range(2):
            to = pl.multiple_of((1 if sign else DEPTH) * SEC + t * 128, 128)
            open_x = faces[0, 0 if sign else DEPTH, t]
            for a in range(VS // 2):
                scale = open_x * (KEEP * DT * (a + 0.5) * H)
                for b in range(2):
                    start = a * VS + 8 * b
                    rows = slice(sign * HALF + start, sign * HALF + start + 8)
                    state[rows, pl.ds(to, 128)] = state[rows, pl.ds(to, 128)] + scale * (
                        ghosts[sign, start : start + 8, pl.ds(at, 128)]
                    )
        return carry

    lax.fori_loop(0, TILES, tile, 0)


def own_coefficients(mine, other, coefs):
    iy = lax.axis_index("vel")
    core = lax.rem(iy, 2)
    for ref, half in ((mine, core), (other, 1 - core)):
        spread(coefs, coefficients([ref[k] for k in range(13)], vy_of(iy)), half * 8)


def middle_kernel(count, first, source, mine_in, other_in, faces, kind, inflow, *refs):
    pairs = refs[: 4 if first else 2]
    refs = refs[len(pairs) :]
    moved, mine, other = refs[:3]
    out_rims = refs[3 : 3 + 2 * first]
    state, ghosts, coefs, edges, lines, sums, sems = refs[3 + 2 * first :]
    iy = lax.axis_index("vel")
    odd = lax.rem(lax.axis_index("gx"), 2)
    copies = []
    for n in range(len(pairs) // 2):
        for m in range(2):
            at = 2 * n + (odd if m == 0 else 1 - odd)
            copies.append(
                pltpu.make_async_copy(pairs[2 * n + m], ghosts.at[at], sems.at[2 * n + m])
            )
    for copy in copies:
        copy.start()
    own_coefficients(mine_in, other_in, coefs)
    inner = lax.rem(iy, 2) == 0
    low = low_rows()
    values = []
    for k in range(13):
        a, b = mine_in[13 + k // 2], other_in[13 + k // 2]
        left, right = jnp.where(inner, a, b), jnp.where(inner, b, a)
        values.append(jnp.where(low, doubled(right, k), doubled(left, k)))
    spread(edges, coefficients(values, vy_of(iy)), 0)
    relax(source, coefs, lines, state, SEC)
    for copy in copies:
        copy.wait()
    relax_ghosts(ghosts, edges, lines, state)
    if first:
        add_rims(ghosts.at[pl.ds(2, 2)], faces, state)
    finish(state, faces, sums, kind, inflow, moved, mine, other, out_rims, count)


VM = pl.BlockSpec(memory_space=pltpu.VMEM)
ANY = pl.BlockSpec(memory_space=pl.ANY)
HBM = pl.BlockSpec(memory_space=pltpu.HBM)
PARAMS = pltpu.CompilerParams(vmem_limit_bytes=12 << 20)
F32 = jnp.float32
WHOLE = jax.ShapeDtypeStruct((ROWS, DEPTH * SEC), F32)
WIDE = jax.ShapeDtypeStruct((ROWS, (DEPTH + 2) * SEC), F32)
RIM = jax.ShapeDtypeStruct((HALF, SEC), F32)
PART = jax.ShapeDtypeStruct((13, 8, 128), F32)
FULL = jax.ShapeDtypeStruct((20, 8, 128), F32)
FACES = jax.ShapeDtypeStruct((5, DEPTH + 1, TILES, 8, 128), F32)
SUMS = pltpu.VMEM((8, OWN, 8, 128), F32)
LINES = pltpu.VMEM((2, 3, 8, 128), F32)


def move_first(dist, wall, kind, inflow, count):
    outs = (FACES, WHOLE, FULL, FULL, RIM, RIM)
    return pl.pallas_call(
        functools.partial(first_kernel, count),
        out_shape=outs,
        in_specs=[HBM, VM, VM, VM],
        out_specs=(VM,) * len(outs),
        scratch_shapes=[
            pltpu.VMEM(WIDE.shape, F32),
            SUMS,
            pltpu.VMEM((8, 8, 8, 128), F32),
            pltpu.SemaphoreType.DMA((DEPTH,)),
        ],
        compiler_params=PARAMS,
        name="move_first",
    )(dist, wall, kind, inflow)


def y_sum(first, *arrays):
    return pl.pallas_call(
        functools.partial(y_kernel, first),
        out_shape=FULL,
        in_specs=[VM] * len(arrays),
        out_specs=VM,
        compiler_params=pltpu.CompilerParams(vmem_limit_bytes=4 << 20),
        name="y_sum",
    )(*arrays)


def move_middle(source, mine, other, faces, kind, inflow, pairs, count, first):
    outs = (WHOLE, PART, PART) + (RIM, RIM) * first
    return pl.pallas_call(
        functools.partial(middle_kernel, count, first),
        out_shape=outs,
        in_specs=[VM] * 6 + [ANY] * len(pairs),
        out_specs=(VM,) * len(outs),
        scratch_shapes=[
            pltpu.VMEM(WIDE.shape, F32),
            pltpu.VMEM((len(pairs), HALF, SEC), F32),
            pltpu.VMEM((9, OWN, 8, 128), F32),
            pltpu.VMEM((9, 8, 8, 128), F32),
            LINES,
            SUMS,
            pltpu.SemaphoreType.DMA((len(pairs),)),
        ],
        compiler_params=PARAMS,
        name="move_middle",
    )(source, mine, other, faces, kind, inflow, *pairs)


def last_kernel(moved, mine, other, state, coefs, lines):
    own_coefficients(mine, other, coefs)
    relax(moved, coefs, lines, state, 0)


def relax_last(moved, mine, other):
    return pl.pallas_call(
        last_kernel,
        out_shape=WHOLE,
        in_specs=[VM, VM, VM],
        out_specs=VM,
        scratch_shapes=[pltpu.VMEM((9, OWN, 8, 128), F32), LINES],
        compiler_params=PARAMS,
        name="relax_last",
    )(moved, mine, other)


def swap_cores(array):
    return lax.ppermute(array, "vel", [(i, i ^ 1) for i in range(VS)])


def shift_x(array, by):
    def mate(i):
        return i ^ (2 * by)

    return lax.ppermute(array, "vel", [(i, mate(i)) for i in range(VS)])


def flip_y(array):
    return lax.ppermute(array, "vel", [(i, i ^ 8) for i in range(VS)])


def sum_x(value):
    parts = [shift_x(value, by) for by in (1, 3, 2)]
    return (value + parts[2]) + (parts[0] + parts[1])


def swap_rims(pair_a, pair_b, count):
    near = [(i, i ^ 1) for i in range(count)]
    far = []
    for i in range(1, count - 1, 2):
        far += [(i, i + 1), (i + 1, i)]
    return lax.ppermute(pair_a, "gx", near), lax.ppermute(pair_b, "gx", far)


def to_neighbours(half, count, flip):
    pairs = []
    for v in range(0, VS, 2):
        for g in range(count - 1):
            one, two = (v + 1) * count + g, (v ^ flip) * count + g + 1
            pairs += [(one, two), (two, one)]
    return lax.ppermute(half, ("vel", "gx"), pairs)


def stage_y(value, count, *faces):
    moves = (flip_y(value), to_neighbours(value, count, 0), to_neighbours(value, count, 8))
    return y_sum(bool(faces), value, *moves, *faces)


def per_device(distribution, wall_mask, boundary_kind, inflow):
    count = lax.axis_size("gx")
    inflow = inflow.reshape(2, 128)
    even = lax.rem(lax.axis_index("gx"), 2) == 0
    up = distribution[HALF:, (DEPTH - 1) * SEC :]
    down = distribution[:HALF, :SEC]
    start = swap_rims(jnp.where(even, up, down), jnp.where(even, down, up), count)
    faces, *outs = move_first(distribution, wall_mask, boundary_kind, inflow, count)
    moved, mine, other, *rims = outs
    pairs = swap_rims(*rims, count)
    half = stage_y(sum_x(mine + swap_cores(other)), count, faces)
    outs = move_middle(
        moved, half, swap_cores(half), faces, boundary_kind, inflow, (*pairs, *start), count, True
    )
    moved, mine, other, *rims = outs
    half = stage_y(mine + swap_cores(other), count)
    half, *rims = lax.optimization_barrier((half, *rims))
    pairs = swap_rims(*rims, count)
    half = sum_x(half)
    moved, mine, other = move_middle(
        moved, half, swap_cores(half), faces, boundary_kind, inflow, pairs, count, False
    )
    half = sum_x(flip_y_sum(mine + swap_cores(other)))
    return relax_last(moved, half, swap_cores(half))


def flip_y_sum(value):
    return value + flip_y(value)


def solution(mesh):
    placed = (P("vel", "gx"), P(), P(), P("vel"))
    return jax.shard_map(
        per_device, mesh=mesh, in_specs=placed, out_specs=P("vel", "gx"), check_vma=False
    )
```

```python
import functools
import math

import jax
import jax.numpy as jnp
from jax import lax
from jax.experimental import pallas as pl
from jax.experimental.pallas import tpu as pltpu
from jax.sharding import PartitionSpec as P


VS = 16
NY = 16
NZ = 32
SEC = NY * NZ
DEPTH = 4
TILES = SEC // 128

LIMIT = 4.5
DT = 0.075
RATE = 0.6
KEEP = 1.0 - RATE
RATIO = 0.6666667
H = 2.0 * LIMIT / VS
WEIGHT = H**3
HALF = VS * VS // 2
ROWS = VS * VS
OWN = DEPTH * TILES


def vy_of(index):
    return -LIMIT + (index.astype(jnp.float32) + 0.5) * H


def sub_iota():
    return lax.broadcasted_iota(jnp.int32, (8, 128), 0).astype(jnp.float32)


def vz_tile(b):
    q = sub_iota()
    return (q + 0.5) * H if b else (q - 7.5) * H


def row(ref, *index):
    return jnp.broadcast_to(ref[index], (8, 128))


def prepare_masks(wall_ref, faces, position, count, forward):
    opened = []
    for slot in range(DEPTH + 2):
        at = position * DEPTH + slot - 1
        inside = jnp.logical_and(at >= 0, at < count * DEPTH)
        line = wall_ref[pl.ds(jnp.clip(at, 0, count * DEPTH - 1), 1), :]
        opened.append(jnp.where(inside, (1 - line).astype(jnp.float32), 1.0))
    zero = jnp.zeros_like(opened[0])
    o = jnp.concatenate(opened + [zero, zero], axis=0)
    cell = lax.broadcasted_iota(jnp.int32, (8, SEC), 1)
    up_x = o * pltpu.roll(o, 7, 0)
    up_y = o * pltpu.roll(o, SEC - NZ, 1) * (cell < SEC - NZ).astype(jnp.float32)
    up_z = o * pltpu.roll(o, SEC - 1, 1) * ((cell & (NZ - 1)) < NZ - 1).astype(jnp.float32)
    down_y = pltpu.roll(up_y, NZ, 1)
    down_z = pltpu.roll(up_z, 1, 1)
    planes = [
        up_x, jnp.where(forward, up_y, down_y), jnp.where(forward, down_y, up_y), down_z, up_z
    ]
    for k, plane in enumerate(planes):
        for slot in range(DEPTH + 1):
            for t in range(TILES):
                line = plane[slot : slot + 1, t * 128 : (t + 1) * 128]
                faces[k, slot, t] = jnp.broadcast_to(line, (8, 128))


def fill_ends(state, inflow_ref, kind_ref, position, count):
    lane = lax.broadcasted_iota(jnp.int32, (8, 128), 1)
    sub = lax.broadcasted_iota(jnp.int32, (8, 128), 0)

    def one(side, base, inner, outer):
        @pl.when(position == (0 if side == 0 else count - 1))
        def _():
            for tile in range(HALF // 8):
                start = base + tile * 8
                line = row(inflow_ref, pl.ds(start // 128, 1), slice(None))
                picked = jnp.where(lane == sub + start % 128, line, 0.0)
                column = jnp.sum(picked, axis=1, keepdims=True)
                for t in range(TILES):
                    kind = row(kind_ref, pl.ds(side, 1), pl.ds(t * 128, 128))
                    inside = state[pl.ds(start, 8), pl.ds(inner * SEC + t * 128, 128)]
                    state[pl.ds(start, 8), pl.ds(outer * SEC + t * 128, 128)] = jnp.where(
                        kind == 1, jnp.broadcast_to(column, (8, 128)), inside
                    )

    one(0, HALF, 1, 0)
    one(1, 0, DEPTH, DEPTH + 1)


def transport(state, faces, moved, sums, iy):
    forward = iy >= VS // 2
    speed_y = jnp.abs(vy_of(iy)) * (KEEP * DT)
    lane = lax.broadcasted_iota(jnp.int32, (8, 128), 1)
    take = jnp.logical_or(
        jnp.logical_and(forward, lane < NZ), jnp.logical_and(~forward, lane >= 128 - NZ)
    )
    shift_y = jnp.where(forward, NZ, 128 - NZ)

    def section(i, carry):
        total = [[None] * 8 for _ in range(TILES)]
        tiles = [jnp.where(forward, k, TILES - 1 - k) for k in range(TILES)]
        lanes = [pl.multiple_of(t * 128, 128) for t in tiles]
        for b in range(2):
            vz = vz_tile(b)
            az = jnp.abs(vz) * (KEEP * DT)
            below = [faces[0, i, t] for t in tiles]
            above = [faces[0, i + 1, t] for t in tiles]
            keep, in_y, in_z = [], [], []
            for t in tiles:
                out_y = faces[1, i + 1, t]
                out_z = faces[4 if b else 3, i + 1, t]
                keep.append(KEEP - speed_y * out_y - az * out_z)
                in_y.append(speed_y * faces[2, i + 1, t])
                in_z.append(az * faces[3 if b else 4, i + 1, t])
            acc = [[None] * 4 for _ in range(TILES)]
            for a in range(VS // 2):
                speed = (a + 0.5) * H
                cx = KEEP * DT * speed
                lo = [cx * x for x in below]
                hi = [cx * x for x in above]
                both = []
                for sign in range(2):
                    start = sign * HALF + a * VS + 8 * b
                    here, shifted = [], []
                    for l in lanes:
                        at = pl.multiple_of((i + 1) * SEC + l, 128)
                        value = state[start : start + 8, pl.ds(at, 128)]
                        here.append(value)
                        shifted.append(pltpu.roll(value, shift_y, 1))
                    result = []
                    for k, l in enumerate(lanes):
                        at = pl.multiple_of((i + (0 if sign else 2)) * SEC + l, 128)
                        before = state[start : start + 8, pl.ds(at, 128)]
                        out_x, in_x = (hi[k], lo[k]) if sign else (lo[k], hi[k])
                        along_y = jnp.where(take, shifted[k - 1], shifted[k]) if k else shifted[k]
                        along_z = pltpu.roll(here[k], 1 if b else 127, 1)
                        value = (
                            here[k] * (keep[k] - out_x)
                            + before * in_x
                            + along_y * in_y[k]
                            + along_z * in_z[k]
                        )
                        at = pl.multiple_of(i * SEC + l, 128)
                        moved[start : start + 8, pl.ds(at, 128)] = value
                        result.append(value)
                    both.append(result)
                for k in range(TILES):
                    even = both[1][k] + both[0][k]
                    odd = both[1][k] - both[0][k]
                    terms = [even, speed * odd, (speed * speed) * even, (speed**3) * odd]
                    for p in range(4):
                        acc[k][p] = terms[p] if acc[k][p] is None else acc[k][p] + terms[p]
            vz2 = vz * vz
            for k in range(TILES):
                a0, a1, a2, a3 = acc[k]
                terms = [
                    a0, a1, vz * a0, a2, vz2 * a0, vz * a1,
                    a3 + vz2 * a1, vz * (a2 + vz2 * a0),
                ]
                for p in range(8):
                    total[k][p] = terms[p] if b == 0 else total[k][p] + terms[p]
        for k, t in enumerate(tiles):
            for p in range(8):
                sums[p, i * TILES + t] = total[k][p]
        return carry

    lax.fori_loop(0, DEPTH, section, 0)


def fold(sums, p, first):
    sub = lax.broadcasted_iota(jnp.int32, (8, 128), 0)
    values = [sums[p, first + t] for t in range(8)]
    for step in (4, 2, 1):
        low = (sub & step) == 0
        merged = []
        for t in range(step):
            a, b = values[t], values[t + step]
            a = a + pltpu.roll(a, 8 - step, 0)
            b = b + pltpu.roll(b, step, 0)
            merged.append(jnp.where(low, a, b))
        values = merged
    return values[0]


def expand(sums, vy):
    s0, sx, sz, sxx, szz, sxz, ex, ez = sums
    y2 = vy * vy
    return [
        s0, sx, vy * s0, sz, sxx, y2 * s0, szz, vy * sx, sxz, vy * sz,
        ex + y2 * sx, vy * (sxx + szz + y2 * s0), ez + y2 * sz,
    ]


def coefficients(m, vy):
    n = m[0]
    inverse = 1.0 / n
    ux, uy, uz = m[1] * inverse, m[2] * inverse, m[3] * inverse
    xx, yy, zz, xy, xz, yz = m[4:10]
    u2 = ux * ux + uy * uy + uz * uz
    trace = xx + yy + zz
    temp = (trace * inverse - u2) / 3.0
    px = xx * ux + xy * uy + xz * uz
    py = xy * ux + yy * uy + yz * uz
    pz = xz * ux + yz * uy + zz * uz
    common = 2.0 * n * u2 - trace
    qx = 0.5 * (m[10] - 2.0 * px + common * ux)
    qy = 0.5 * (m[11] - 2.0 * py + common * uy)
    qz = 0.5 * (m[12] - 2.0 * pz + common * uz)
    inv_t = 1.0 / temp
    kappa = (1.0 - RATIO) / 5.0 * inverse * inv_t * inv_t
    s = kappa * inv_t
    i2t = 0.5 * inv_t
    cy = vy - uy
    level = 0.5 * (
        jnp.log(n) - 1.5 * jnp.log((2.0 * math.pi) * temp) - cy * cy * i2t
    )
    return [ux, uz, i2t, level, qx, qz, s, qy * cy, s * cy * cy - 5.0 * kappa]


def point(coefs, j):
    return [coefs[k, j] for k in range(9)]


def across(values, sign):
    ux, _, i2t, level, qx, _, s, qyc, rest = values
    cx = (sub_iota() + 0.5) * (H if sign else -H) - ux
    c2 = cx * cx
    return jnp.exp(level - c2 * i2t) * RATE, qx * cx + qyc, s * c2 + rest


def along(values, b):
    _, uz, i2t, level, _, qz, s, _, _ = values
    cz = vz_tile(b) - uz
    c2 = cz * cz
    return jnp.exp(level - c2 * i2t), qz * cz, s * c2


def store_lines(lines, values, sign):
    for k, value in enumerate(across(values, sign)):
        lines[sign, k] = value


def relax_rows(read, write, lines, fixed, sign):
    for a in range(VS // 2):
        ex, qa, sa = [row(lines, sign, k, pl.ds(a, 1), slice(None)) for k in range(3)]
        for b in range(2):
            ez, qb, sb = fixed[b]
            start = a * VS + 8 * b
            write(start, read(start) + (ex * ez) * (1.0 + (qa + qb) * (sa + sb)))


def relax(moved, coefs, lines, state, shift):
    def tile(j, carry):
        values = point(coefs, j)
        for sign in range(2):
            store_lines(lines, values, sign)
        fixed = [along(values, b) for b in range(2)]
        at = pl.multiple_of(j * 128, 128)
        to = pl.multiple_of(j * 128 + shift, 128)
        for sign in range(2):
            base = sign * HALF

            def read(start):
                return moved[base + start : base + start + 8, pl.ds(at, 128)]

            def write(start, value):
                state[base + start : base + start + 8, pl.ds(to, 128)] = value

            relax_rows(read, write, lines, fixed, sign)
        return carry

    lax.fori_loop(0, OWN, tile, 0)


def relax_ghosts(ghosts, coefs, lines, state):
    def tile(t, carry):
        at = pl.multiple_of(t * 128, 128)
        for sign in range(2):
            values = point(coefs, t + TILES * sign)
            store_lines(lines, values, sign)
            fixed = [along(values, b) for b in range(2)]
            base = sign * HALF
            to = pl.multiple_of(t * 128 + (0 if sign else (DEPTH + 1) * SEC), 128)

            def read(start):
                return ghosts[sign, start : start + 8, pl.ds(at, 128)]

            def write(start, value):
                state[base + start : base + start + 8, pl.ds(to, 128)] = value

            relax_rows(read, write, lines, fixed, sign)
        return carry

    lax.fori_loop(0, TILES, tile, 0)


def spread(coefs, values, first):
    for k, value in enumerate(values):
        for t in range(8):
            coefs[k, first + t] = jnp.broadcast_to(value[t : t + 1], (8, 128))


def finish(state, faces, sums, kind, inflow, moved, mine, other, rims, count):
    iy = lax.axis_index("vel")
    position = lax.axis_index("gx")
    fill_ends(state, inflow, kind, position, count)
    transport(state, faces, moved, sums, iy)
    core = lax.rem(iy, 2)
    vy = vy_of(iy)
    for ref, first in ((mine, core * 8), (other, 8 - core * 8)):
        values = expand([fold(sums, p, first) * (WEIGHT / KEEP) for p in range(8)], vy)
        for k, value in enumerate(values):
            ref[k] = value
    if rims:
        even = lax.rem(position, 2) == 0
        up = (slice(HALF, ROWS), slice((DEPTH - 1) * SEC, DEPTH * SEC))
        down = (slice(0, HALF), slice(0, SEC))

        @pl.when(even)
        def _():
            rims[0][...] = moved[up]
            rims[1][...] = moved[down]

        @pl.when(~even)
        def _():
            rims[0][...] = moved[down]
            rims[1][...] = moved[up]


def low_rows():
    return lax.broadcasted_iota(jnp.int32, (8, 128), 0) < TILES


def pack(values):
    low = low_rows()
    values = values + [jnp.zeros_like(values[0])]
    return [jnp.where(low, values[k], values[k + 1]) for k in range(0, 14, 2)]


def doubled(packed, k):
    turned = pltpu.roll(packed, TILES, 0)
    if k % 2:
        return jnp.where(low_rows(), turned, packed)
    return jnp.where(low_rows(), packed, turned)


def rim_flux(state, sums):
    def tile(t, carry):
        for sign in range(2):
            at = pl.multiple_of((DEPTH if sign else 1) * SEC + t * 128, 128)
            total = [None] * 8
            for b in range(2):
                vz = vz_tile(b)
                vz2 = vz * vz
                acc = [None] * 4
                for a in range(VS // 2):
                    speed = (a + 0.5) * H
                    start = sign * HALF + a * VS + 8 * b
                    value = state[start : start + 8, pl.ds(at, 128)] * speed
                    for p in range(4):
                        acc[p] = value if acc[p] is None else acc[p] + value
                        value = value * (speed if sign else -speed)
                a0, a1, a2, a3 = acc
                terms = [
                    a0, a1, vz * a0, a2, vz2 * a0, vz * a1,
                    a3 + vz2 * a1, vz * (a2 + vz2 * a0),
                ]
                total = terms if b == 0 else [x + y for x, y in zip(total, terms)]
            for p in range(8):
                sums[p, TILES * sign + t] = total[p]
        return carry

    lax.fori_loop(0, TILES, tile, 0)


def first_kernel(count, dist, wall, kind, inflow, *refs):
    faces, moved, mine, other, rim_a, rim_b, state, sums, flux, sems = refs
    iy = lax.axis_index("vel")
    position = lax.axis_index("gx")
    loads = [
        pltpu.make_async_copy(
            dist.at[:, pl.ds(i * SEC, SEC)], state.at[:, pl.ds((i + 1) * SEC, SEC)], sems.at[i]
        )
        for i in range(DEPTH)
    ]
    for load in loads:
        load.start()
    prepare_masks(wall, faces, position, count, iy >= VS // 2)
    state[HALF:, :SEC] = jnp.zeros((HALF, SEC), F32)
    state[:HALF, (DEPTH + 1) * SEC :] = jnp.zeros((HALF, SEC), F32)
    for load in loads:
        load.wait()
    finish(state, faces, sums, kind, inflow, moved, mine, other, (rim_a, rim_b), count)
    rim_flux(state, flux)
    values = expand([fold(flux, p, 0) * (WEIGHT / KEEP) for p in range(8)], vy_of(iy))
    turned = [pltpu.roll(value, TILES, 0) for value in values]
    low = low_rows()
    halves = [
        pack([value if k % 2 == 0 else turned[k] for k, value in enumerate(values)]),
        pack([turned[k] if k % 2 == 0 else value for k, value in enumerate(values)]),
    ]
    inner = lax.rem(iy, 2) == 0
    for k in range(7):
        mine[13 + k] = jnp.where(inner, halves[0][k], halves[1][k])
        other[13 + k] = jnp.where(inner, halves[1][k], halves[0][k])


def add_rims(ghosts, faces, state):
    def tile(t, carry):
        at = pl.multiple_of(t * 128, 128)
        for sign in range(2):
            to = pl.multiple_of((1 if sign else DEPTH) * SEC + t * 128, 128)
            open_x = faces[0, 0 if sign else DEPTH, t]
            for a in range(VS // 2):
                scale = open_x * (KEEP * DT * (a + 0.5) * H)
                for b in range(2):
                    start = a * VS + 8 * b
                    rows = slice(sign * HALF + start, sign * HALF + start + 8)
                    state[rows, pl.ds(to, 128)] = state[rows, pl.ds(to, 128)] + scale * (
                        ghosts[sign, start : start + 8, pl.ds(at, 128)]
                    )
        return carry

    lax.fori_loop(0, TILES, tile, 0)


def own_coefficients(mine, other, coefs):
    iy = lax.axis_index("vel")
    core = lax.rem(iy, 2)
    for ref, half in ((mine, core), (other, 1 - core)):
        spread(coefs, coefficients([ref[k] for k in range(13)], vy_of(iy)), half * 8)


def first_moments(mine, other, got, swapped, faces):
    inner = lax.rem(lax.axis_index("vel"), 2) == 0
    low = low_rows()
    sub = lax.broadcasted_iota(jnp.int32, (8, 128), 0)
    edge = jnp.zeros((8, 128), F32)
    for t in range(TILES):
        edge = jnp.where(sub == t, faces[0, 0, t], edge)
        edge = jnp.where(sub == t + TILES, faces[0, DEPTH, t], edge)
    edge = edge * (KEEP * DT)
    turned = pltpu.roll(edge, TILES, 0)

    def pair(a, b, k):
        return jnp.where(inner, a[k], b[k]), jnp.where(inner, b[k], a[k])

    start, end, halo = [], [], []
    for k in range(13):
        one, two = pair(mine, other, k)
        one_flux, two_flux = pair(mine, other, 13 + k // 2)
        left, right = pair(got, swapped, k)
        left_flux, right_flux = pair(got, swapped, 13 + k // 2)
        start.append(one + jnp.where(low, edge * doubled(left_flux, k), 0.0))
        end.append(two + jnp.where(low, 0.0, edge * doubled(right_flux, k)))
        halo.append(
            jnp.where(low, right, left)
            + turned * jnp.where(low, doubled(two_flux, k), doubled(one_flux, k))
        )
    return start, end, halo


def bring_rims(pairs, ghosts, sems):
    odd = lax.rem(lax.axis_index("gx"), 2)
    copies = []
    for n in range(len(pairs) // 2):
        for m in range(2):
            at = 2 * n + (odd if m == 0 else 1 - odd)
            copies.append(
                pltpu.make_async_copy(pairs[2 * n + m], ghosts.at[at], sems.at[2 * n + m])
            )
    for copy in copies:
        copy.start()
    return copies


def second_kernel(count, source, mine_in, other_in, got, swapped, faces, kind, inflow, *refs):
    pairs = refs[:4]
    moved, mine, other, *out_rims = refs[4:9]
    state, ghosts, coefs, edges, lines, sums, sems = refs[9:]
    copies = bring_rims(pairs, ghosts, sems)
    vy = vy_of(lax.axis_index("vel"))
    start, end, halo = first_moments(mine_in, other_in, got, swapped, faces)
    spread(coefs, coefficients(start, vy), 0)
    spread(coefs, coefficients(end, vy), 8)
    spread(edges, coefficients(halo, vy), 0)
    relax(source, coefs, lines, state, SEC)
    for copy in copies:
        copy.wait()
    relax_ghosts(ghosts, edges, lines, state)
    add_rims(ghosts.at[pl.ds(2, 2)], faces, state)
    finish(state, faces, sums, kind, inflow, moved, mine, other, out_rims, count)


def third_kernel(count, old, pair_a, pair_b, got, swapped, faces, kind, inflow, *refs):
    state, moved, mine, other, ghosts, edges, lines, sums, sems = refs
    copies = bring_rims((pair_a, pair_b), ghosts, sems)
    iy = lax.axis_index("vel")
    pick = low_rows() != (lax.rem(iy, 2) == 0)
    values = [jnp.where(pick, got[k], swapped[k]) for k in range(13)]
    spread(edges, coefficients(values, vy_of(iy)), 0)
    for copy in copies:
        copy.wait()
    relax_ghosts(ghosts, edges, lines, state)
    finish(state, faces, sums, kind, inflow, moved, mine, other, (), count)


VM = pl.BlockSpec(memory_space=pltpu.VMEM)
ANY = pl.BlockSpec(memory_space=pl.ANY)
HBM = pl.BlockSpec(memory_space=pltpu.HBM)
PARAMS = pltpu.CompilerParams(vmem_limit_bytes=12 << 20)
F32 = jnp.float32
WHOLE = jax.ShapeDtypeStruct((ROWS, DEPTH * SEC), F32)
WIDE = jax.ShapeDtypeStruct((ROWS, (DEPTH + 2) * SEC), F32)
RIM = jax.ShapeDtypeStruct((HALF, SEC), F32)
PART = jax.ShapeDtypeStruct((13, 8, 128), F32)
FULL = jax.ShapeDtypeStruct((20, 8, 128), F32)
FACES = jax.ShapeDtypeStruct((5, DEPTH + 1, TILES, 8, 128), F32)
SUMS = pltpu.VMEM((8, OWN, 8, 128), F32)
LINES = pltpu.VMEM((2, 3, 8, 128), F32)


def move_first(dist, wall, kind, inflow, count):
    outs = (FACES, WHOLE, FULL, FULL, RIM, RIM)
    return pl.pallas_call(
        functools.partial(first_kernel, count),
        out_shape=outs,
        in_specs=[HBM, VM, VM, VM],
        out_specs=(VM,) * len(outs),
        scratch_shapes=[
            pltpu.VMEM(WIDE.shape, F32),
            SUMS,
            pltpu.VMEM((8, 8, 8, 128), F32),
            pltpu.SemaphoreType.DMA((DEPTH,)),
        ],
        compiler_params=PARAMS,
        name="move_first",
    )(dist, wall, kind, inflow)


def move_second(source, halves, faces, kind, inflow, pairs, count):
    outs = (WHOLE, PART, PART, RIM, RIM)
    return pl.pallas_call(
        functools.partial(second_kernel, count),
        out_shape=outs,
        in_specs=[VM] * 8 + [ANY] * 4,
        out_specs=(VM,) * len(outs),
        scratch_shapes=[
            pltpu.VMEM(WIDE.shape, F32),
            pltpu.VMEM((4, HALF, SEC), F32),
            pltpu.VMEM((9, OWN, 8, 128), F32),
            pltpu.VMEM((9, 8, 8, 128), F32),
            LINES,
            SUMS,
            pltpu.SemaphoreType.DMA((4,)),
        ],
        compiler_params=PARAMS,
        name="move_second",
    )(source, *halves, faces, kind, inflow, *pairs)


def move_third(state, pairs, got, swapped, faces, kind, inflow, count):
    outs = (WIDE, WHOLE, PART, PART)
    return pl.pallas_call(
        functools.partial(third_kernel, count),
        out_shape=outs,
        in_specs=[VM, ANY, ANY] + [VM] * 5,
        out_specs=(VM,) * len(outs),
        input_output_aliases={0: 0},
        scratch_shapes=[
            pltpu.VMEM((2, HALF, SEC), F32),
            pltpu.VMEM((9, 8, 8, 128), F32),
            LINES,
            SUMS,
            pltpu.SemaphoreType.DMA((2,)),
        ],
        compiler_params=PARAMS,
        name="move_third",
    )(state, *pairs, got, swapped, faces, kind, inflow)[1:]


def relax_kernel(shift, moved, mine, other, state, coefs, lines):
    own_coefficients(mine, other, coefs)
    relax(moved, coefs, lines, state, shift)


def relaxed(moved, mine, other, last):
    return pl.pallas_call(
        functools.partial(relax_kernel, 0 if last else SEC),
        out_shape=WHOLE if last else WIDE,
        in_specs=[VM, VM, VM],
        out_specs=VM,
        scratch_shapes=[pltpu.VMEM((9, OWN, 8, 128), F32), LINES],
        compiler_params=PARAMS,
        name="relax_last" if last else "relax",
    )(moved, mine, other)


def swap_cores(array):
    return lax.ppermute(array, "vel", [(i, i ^ 1) for i in range(VS)])


def shift_x(array, by):
    def mate(i):
        return i ^ (2 * by)

    return lax.ppermute(array, "vel", [(i, mate(i)) for i in range(VS)])


def flip_y(array):
    return lax.ppermute(array, "vel", [(i, i ^ 8) for i in range(VS)])


def sum_x(value):
    parts = []
    for by in (1, 3, 2):
        parts.append(shift_x(value, by))
    return (value + parts[2]) + (parts[0] + parts[1])


def sum_chips(value):
    value = sum_x(value)
    return value + flip_y(value)


def swap_rims(pair_a, pair_b, count):
    near = [(i, i ^ 1) for i in range(count)]
    far = []
    for i in range(1, count - 1, 2):
        far += [(i, i + 1), (i + 1, i)]
    pair_a = lax.ppermute(pair_a, "gx", near)
    pair_b = lax.ppermute(pair_b, "gx", far)
    return pair_a, pair_b


def swap_moments(half, count):
    pairs = []
    for v in range(0, VS, 2):
        for g in range(count - 1):
            one, two = (v + 1) * count + g, v * count + g + 1
            pairs += [(one, two), (two, one)]
    return lax.ppermute(half, ("vel", "gx"), pairs)


def per_device(distribution, wall_mask, boundary_kind, inflow):
    count = lax.axis_size("gx")
    inflow = inflow.reshape(2, 128)
    even = lax.rem(lax.axis_index("gx"), 2) == 0
    up = distribution[HALF:, (DEPTH - 1) * SEC :]
    down = distribution[:HALF, :SEC]
    start = swap_rims(jnp.where(even, up, down), jnp.where(even, down, up), count)
    outs = move_first(distribution, wall_mask, boundary_kind, inflow, count)
    faces, moved, mine, other, *rims = outs
    pairs = swap_rims(*rims, count)
    half = sum_chips(mine + swap_cores(other))
    halo = swap_moments(half, count)
    swapped = swap_cores(half)
    halves = (half, swapped, halo, swap_cores(halo))
    moved, mine, other, *rims = move_second(
        moved, halves, faces, boundary_kind, inflow, (*pairs, *start), count
    )
    pairs = swap_rims(*rims, count)
    half = sum_chips(mine + swap_cores(other))
    halo = swap_moments(half, count)
    state = relaxed(moved, half, swap_cores(half), False)
    halo, state = lax.optimization_barrier((halo, state))
    moved, mine, other = move_third(
        state, pairs, halo, swap_cores(halo), faces, boundary_kind, inflow, count
    )
    half = sum_chips(mine + swap_cores(other))
    return relaxed(moved, half, swap_cores(half), True)


def solution(mesh):
    placed = (P("vel", "gx"), P(), P(), P("vel"))
    return jax.shard_map(
        per_device, mesh=mesh, in_specs=placed, out_specs=P("vel", "gx"), check_vma=False
    )
```

```python
import functools
import math

import jax
import jax.numpy as jnp
from jax import lax
from jax.experimental import pallas as pl
from jax.experimental.pallas import tpu as pltpu
from jax.sharding import PartitionSpec as P


VS = 16
NY = 16
NZ = 32
SEC = NY * NZ
DEPTH = 4
TILES = SEC // 128

LIMIT = 4.5
DT = 0.075
RATE = 0.6
KEEP = 1.0 - RATE
RATIO = 0.6666667
H = 2.0 * LIMIT / VS
WEIGHT = H**3
HALF = VS * VS // 2
ROWS = VS * VS
OWN = DEPTH * TILES


def vy_of(index):
    return -LIMIT + (index.astype(jnp.float32) + 0.5) * H


def sub_iota():
    return lax.broadcasted_iota(jnp.int32, (8, 128), 0).astype(jnp.float32)


def vz_tile(b):
    q = sub_iota()
    return (q + 0.5) * H if b else (q - 7.5) * H


def row(ref, *index):
    return jnp.broadcast_to(ref[index], (8, 128))


def prepare_masks(wall_ref, faces, position, count, forward):
    opened = []
    for slot in range(DEPTH + 2):
        at = position * DEPTH + slot - 1
        inside = jnp.logical_and(at >= 0, at < count * DEPTH)
        line = wall_ref[pl.ds(jnp.clip(at, 0, count * DEPTH - 1), 1), :]
        opened.append(jnp.where(inside, (1 - line).astype(jnp.float32), 1.0))
    zero = jnp.zeros_like(opened[0])
    o = jnp.concatenate(opened + [zero, zero], axis=0)
    cell = lax.broadcasted_iota(jnp.int32, (8, SEC), 1)
    up_x = o * pltpu.roll(o, 7, 0)
    up_y = o * pltpu.roll(o, SEC - NZ, 1) * (cell < SEC - NZ).astype(jnp.float32)
    up_z = o * pltpu.roll(o, SEC - 1, 1) * ((cell & (NZ - 1)) < NZ - 1).astype(jnp.float32)
    down_y = pltpu.roll(up_y, NZ, 1)
    down_z = pltpu.roll(up_z, 1, 1)
    planes = [
        up_x, jnp.where(forward, up_y, down_y), jnp.where(forward, down_y, up_y), down_z, up_z
    ]
    for k, plane in enumerate(planes):
        for slot in range(DEPTH + 1):
            for t in range(TILES):
                line = plane[slot : slot + 1, t * 128 : (t + 1) * 128]
                faces[k, slot, t] = jnp.broadcast_to(line, (8, 128))


def fill_ends(state, inflow_ref, kind_ref, position, count):
    lane = lax.broadcasted_iota(jnp.int32, (8, 128), 1)
    sub = lax.broadcasted_iota(jnp.int32, (8, 128), 0)

    def one(side, base, inner, outer):
        @pl.when(position == (0 if side == 0 else count - 1))
        def _():
            for tile in range(HALF // 8):
                start = base + tile * 8
                line = row(inflow_ref, pl.ds(start // 128, 1), slice(None))
                picked = jnp.where(lane == sub + start % 128, line, 0.0)
                column = jnp.sum(picked, axis=1, keepdims=True)
                for t in range(TILES):
                    kind = row(kind_ref, pl.ds(side, 1), pl.ds(t * 128, 128))
                    inside = state[pl.ds(start, 8), pl.ds(inner * SEC + t * 128, 128)]
                    state[pl.ds(start, 8), pl.ds(outer * SEC + t * 128, 128)] = jnp.where(
                        kind == 1, jnp.broadcast_to(column, (8, 128)), inside
                    )

    one(0, HALF, 1, 0)
    one(1, 0, DEPTH, DEPTH + 1)


def transport(state, faces, moved, sums, iy):
    forward = iy >= VS // 2
    speed_y = jnp.abs(vy_of(iy)) * (KEEP * DT)
    lane = lax.broadcasted_iota(jnp.int32, (8, 128), 1)
    take = jnp.logical_or(
        jnp.logical_and(forward, lane < NZ), jnp.logical_and(~forward, lane >= 128 - NZ)
    )
    shift_y = jnp.where(forward, NZ, 128 - NZ)

    def section(i, carry):
        total = [[None] * 8 for _ in range(TILES)]
        tiles = [jnp.where(forward, k, TILES - 1 - k) for k in range(TILES)]
        lanes = [pl.multiple_of(t * 128, 128) for t in tiles]
        for b in range(2):
            vz = vz_tile(b)
            az = jnp.abs(vz) * (KEEP * DT)
            below = [faces[0, i, t] for t in tiles]
            above = [faces[0, i + 1, t] for t in tiles]
            keep, in_y, in_z = [], [], []
            for t in tiles:
                out_y = faces[1, i + 1, t]
                out_z = faces[4 if b else 3, i + 1, t]
                keep.append(KEEP - speed_y * out_y - az * out_z)
                in_y.append(speed_y * faces[2, i + 1, t])
                in_z.append(az * faces[3 if b else 4, i + 1, t])
            acc = [[None] * 4 for _ in range(TILES)]
            for a in range(VS // 2):
                speed = (a + 0.5) * H
                cx = KEEP * DT * speed
                lo = [cx * x for x in below]
                hi = [cx * x for x in above]
                both = []
                for sign in range(2):
                    start = sign * HALF + a * VS + 8 * b
                    here, shifted = [], []
                    for l in lanes:
                        at = pl.multiple_of((i + 1) * SEC + l, 128)
                        value = state[start : start + 8, pl.ds(at, 128)]
                        here.append(value)
                        shifted.append(pltpu.roll(value, shift_y, 1))
                    result = []
                    for k, l in enumerate(lanes):
                        at = pl.multiple_of((i + (0 if sign else 2)) * SEC + l, 128)
                        before = state[start : start + 8, pl.ds(at, 128)]
                        out_x, in_x = (hi[k], lo[k]) if sign else (lo[k], hi[k])
                        along_y = jnp.where(take, shifted[k - 1], shifted[k]) if k else shifted[k]
                        along_z = pltpu.roll(here[k], 1 if b else 127, 1)
                        value = (
                            here[k] * (keep[k] - out_x)
                            + before * in_x
                            + along_y * in_y[k]
                            + along_z * in_z[k]
                        )
                        at = pl.multiple_of(i * SEC + l, 128)
                        moved[start : start + 8, pl.ds(at, 128)] = value
                        result.append(value)
                    both.append(result)
                for k in range(TILES):
                    even = both[1][k] + both[0][k]
                    odd = both[1][k] - both[0][k]
                    terms = [even, speed * odd, (speed * speed) * even, (speed**3) * odd]
                    for p in range(4):
                        acc[k][p] = terms[p] if acc[k][p] is None else acc[k][p] + terms[p]
            vz2 = vz * vz
            for k in range(TILES):
                a0, a1, a2, a3 = acc[k]
                terms = [
                    a0, a1, vz * a0, a2, vz2 * a0, vz * a1,
                    a3 + vz2 * a1, vz * (a2 + vz2 * a0),
                ]
                for p in range(8):
                    total[k][p] = terms[p] if b == 0 else total[k][p] + terms[p]
        for k, t in enumerate(tiles):
            for p in range(8):
                sums[p, i * TILES + t] = total[k][p]
        return carry

    lax.fori_loop(0, DEPTH, section, 0)


def fold(sums, p, first):
    sub = lax.broadcasted_iota(jnp.int32, (8, 128), 0)
    values = [sums[p, first + t] for t in range(8)]
    for step in (4, 2, 1):
        low = (sub & step) == 0
        merged = []
        for t in range(step):
            a, b = values[t], values[t + step]
            a = a + pltpu.roll(a, 8 - step, 0)
            b = b + pltpu.roll(b, step, 0)
            merged.append(jnp.where(low, a, b))
        values = merged
    return values[0]


def expand(sums, vy):
    s0, sx, sz, sxx, szz, sxz, ex, ez = sums
    y2 = vy * vy
    return [
        s0, sx, vy * s0, sz, sxx, y2 * s0, szz, vy * sx, sxz, vy * sz,
        ex + y2 * sx, vy * (sxx + szz + y2 * s0), ez + y2 * sz,
    ]


def coefficients(m, vy):
    n = m[0]
    inverse = 1.0 / n
    ux, uy, uz = m[1] * inverse, m[2] * inverse, m[3] * inverse
    xx, yy, zz, xy, xz, yz = m[4:10]
    u2 = ux * ux + uy * uy + uz * uz
    trace = xx + yy + zz
    temp = (trace * inverse - u2) / 3.0
    px = xx * ux + xy * uy + xz * uz
    py = xy * ux + yy * uy + yz * uz
    pz = xz * ux + yz * uy + zz * uz
    common = 2.0 * n * u2 - trace
    qx = 0.5 * (m[10] - 2.0 * px + common * ux)
    qy = 0.5 * (m[11] - 2.0 * py + common * uy)
    qz = 0.5 * (m[12] - 2.0 * pz + common * uz)
    inv_t = 1.0 / temp
    kappa = (1.0 - RATIO) / 5.0 * inverse * inv_t * inv_t
    s = kappa * inv_t
    i2t = 0.5 * inv_t
    cy = vy - uy
    level = 0.5 * (
        jnp.log(n) - 1.5 * jnp.log((2.0 * math.pi) * temp) - cy * cy * i2t
    )
    return [ux, uz, i2t, level, qx, qz, s, qy * cy, s * cy * cy - 5.0 * kappa]


def point(coefs, j):
    return [coefs[k, j] for k in range(9)]


def across(values, sign):
    ux, _, i2t, level, qx, _, s, qyc, rest = values
    cx = (sub_iota() + 0.5) * (H if sign else -H) - ux
    c2 = cx * cx
    return jnp.exp(level - c2 * i2t) * RATE, qx * cx + qyc, s * c2 + rest


def along(values, b):
    _, uz, i2t, level, _, qz, s, _, _ = values
    cz = vz_tile(b) - uz
    c2 = cz * cz
    return jnp.exp(level - c2 * i2t), qz * cz, s * c2


def store_lines(lines, values, sign):
    for k, value in enumerate(across(values, sign)):
        lines[sign, k] = value


def relax_rows(read, write, lines, fixed, sign):
    for a in range(VS // 2):
        ex, qa, sa = [row(lines, sign, k, pl.ds(a, 1), slice(None)) for k in range(3)]
        for b in range(2):
            ez, qb, sb = fixed[b]
            start = a * VS + 8 * b
            write(start, read(start) + (ex * ez) * (1.0 + (qa + qb) * (sa + sb)))


def relax(moved, coefs, lines, state, shift, first=0, size=OWN):
    def tile(j, carry):
        values = point(coefs, j)
        for sign in range(2):
            store_lines(lines, values, sign)
        fixed = [along(values, b) for b in range(2)]
        at = pl.multiple_of(j * 128, 128)
        to = pl.multiple_of(j * 128 + shift, 128)
        for sign in range(2):
            base = sign * HALF

            def read(start):
                return moved[base + start : base + start + 8, pl.ds(at, 128)]

            def write(start, value):
                state[base + start : base + start + 8, pl.ds(to, 128)] = value

            relax_rows(read, write, lines, fixed, sign)
        return carry

    lax.fori_loop(first, first + size, tile, 0)


def relax_ghosts(ghosts, coefs, lines, state):
    def tile(t, carry):
        at = pl.multiple_of(t * 128, 128)
        for sign in range(2):
            values = point(coefs, t + TILES * sign)
            store_lines(lines, values, sign)
            fixed = [along(values, b) for b in range(2)]
            base = sign * HALF
            to = pl.multiple_of(t * 128 + (0 if sign else (DEPTH + 1) * SEC), 128)

            def read(start):
                return ghosts[sign, start : start + 8, pl.ds(at, 128)]

            def write(start, value):
                state[base + start : base + start + 8, pl.ds(to, 128)] = value

            relax_rows(read, write, lines, fixed, sign)
        return carry

    lax.fori_loop(0, TILES, tile, 0)


def spread(coefs, values, first):
    for k, value in enumerate(values):
        for t in range(8):
            coefs[k, first + t] = jnp.broadcast_to(value[t : t + 1], (8, 128))


def finish(state, faces, sums, kind, inflow, moved, mine, other, rims, count):
    iy = lax.axis_index("vel")
    position = lax.axis_index("gx")
    fill_ends(state, inflow, kind, position, count)
    transport(state, faces, moved, sums, iy)
    core = lax.rem(iy, 2)
    vy = vy_of(iy)
    for ref, first in ((mine, core * 8), (other, 8 - core * 8)):
        values = expand([fold(sums, p, first) * (WEIGHT / KEEP) for p in range(8)], vy)
        for k, value in enumerate(values):
            ref[k] = value
    if rims:
        even = lax.rem(position, 2) == 0
        up = (slice(HALF, ROWS), slice((DEPTH - 1) * SEC, DEPTH * SEC))
        down = (slice(0, HALF), slice(0, SEC))

        @pl.when(even)
        def _():
            rims[0][...] = moved[up]
            rims[1][...] = moved[down]

        @pl.when(~even)
        def _():
            rims[0][...] = moved[down]
            rims[1][...] = moved[up]


def low_rows():
    return lax.broadcasted_iota(jnp.int32, (8, 128), 0) < TILES


def pack(values):
    low = low_rows()
    values = values + [jnp.zeros_like(values[0])]
    return [jnp.where(low, values[k], values[k + 1]) for k in range(0, 14, 2)]


def doubled(packed, k):
    turned = pltpu.roll(packed, TILES, 0)
    if k % 2:
        return jnp.where(low_rows(), turned, packed)
    return jnp.where(low_rows(), packed, turned)


def rim_flux(state, sums):
    def tile(t, carry):
        for sign in range(2):
            at = pl.multiple_of((DEPTH if sign else 1) * SEC + t * 128, 128)
            total = [None] * 8
            for b in range(2):
                vz = vz_tile(b)
                vz2 = vz * vz
                acc = [None] * 4
                for a in range(VS // 2):
                    speed = (a + 0.5) * H
                    start = sign * HALF + a * VS + 8 * b
                    value = state[start : start + 8, pl.ds(at, 128)] * speed
                    for p in range(4):
                        acc[p] = value if acc[p] is None else acc[p] + value
                        value = value * (speed if sign else -speed)
                a0, a1, a2, a3 = acc
                terms = [
                    a0, a1, vz * a0, a2, vz2 * a0, vz * a1,
                    a3 + vz2 * a1, vz * (a2 + vz2 * a0),
                ]
                total = terms if b == 0 else [x + y for x, y in zip(total, terms)]
            for p in range(8):
                sums[p, TILES * sign + t] = total[p]
        return carry

    lax.fori_loop(0, TILES, tile, 0)


def first_kernel(count, dist, wall, kind, inflow, *refs):
    faces, moved, mine, other, rim_a, rim_b, state, sums, flux, wall_v, kind_v, inflow_v, sems = (
        refs
    )
    small = [
        pltpu.make_async_copy(wall, wall_v, sems.at[DEPTH]),
        pltpu.make_async_copy(kind, kind_v, sems.at[DEPTH + 1]),
        pltpu.make_async_copy(inflow, inflow_v, sems.at[DEPTH + 2]),
    ]
    for load in small:
        load.start()
    iy = lax.axis_index("vel")
    position = lax.axis_index("gx")
    loads = [
        pltpu.make_async_copy(
            dist.at[:, pl.ds(i * SEC, SEC)], state.at[:, pl.ds((i + 1) * SEC, SEC)], sems.at[i]
        )
        for i in range(DEPTH)
    ]
    for load in loads:
        load.start()
    state[HALF:, :SEC] = jnp.zeros((HALF, SEC), F32)
    state[:HALF, (DEPTH + 1) * SEC :] = jnp.zeros((HALF, SEC), F32)
    for load in small:
        load.wait()
    prepare_masks(wall_v, faces, position, count, iy >= VS // 2)
    for load in loads:
        load.wait()
    finish(state, faces, sums, kind_v, inflow_v, moved, mine, other, (rim_a, rim_b), count)
    rim_flux(state, flux)
    values = expand([fold(flux, p, 0) * (WEIGHT / KEEP) for p in range(8)], vy_of(iy))
    turned = [pltpu.roll(value, TILES, 0) for value in values]
    low = low_rows()
    halves = [
        pack([value if k % 2 == 0 else turned[k] for k, value in enumerate(values)]),
        pack([turned[k] if k % 2 == 0 else value for k, value in enumerate(values)]),
    ]
    inner = lax.rem(iy, 2) == 0
    for k in range(7):
        mine[13 + k] = jnp.where(inner, halves[0][k], halves[1][k])
        other[13 + k] = jnp.where(inner, halves[1][k], halves[0][k])


def add_rims(ghosts, faces, state):
    def tile(t, carry):
        at = pl.multiple_of(t * 128, 128)
        for sign in range(2):
            to = pl.multiple_of((1 if sign else DEPTH) * SEC + t * 128, 128)
            open_x = faces[0, 0 if sign else DEPTH, t]
            for a in range(VS // 2):
                scale = open_x * (KEEP * DT * (a + 0.5) * H)
                for b in range(2):
                    start = a * VS + 8 * b
                    rows = slice(sign * HALF + start, sign * HALF + start + 8)
                    state[rows, pl.ds(to, 128)] = state[rows, pl.ds(to, 128)] + scale * (
                        ghosts[sign, start : start + 8, pl.ds(at, 128)]
                    )
        return carry

    lax.fori_loop(0, TILES, tile, 0)


def own_coefficients(mine, other, coefs):
    iy = lax.axis_index("vel")
    core = lax.rem(iy, 2)
    for ref, half in ((mine, core), (other, 1 - core)):
        spread(coefs, coefficients([ref[k] for k in range(13)], vy_of(iy)), half * 8)


def first_moments(mine, other, got, swapped, faces):
    inner = lax.rem(lax.axis_index("vel"), 2) == 0
    low = low_rows()
    sub = lax.broadcasted_iota(jnp.int32, (8, 128), 0)
    edge = jnp.zeros((8, 128), F32)
    for t in range(TILES):
        edge = jnp.where(sub == t, faces[0, 0, t], edge)
        edge = jnp.where(sub == t + TILES, faces[0, DEPTH, t], edge)
    edge = edge * (KEEP * DT)
    turned = pltpu.roll(edge, TILES, 0)

    def pair(a, b, k):
        return jnp.where(inner, a[k], b[k]), jnp.where(inner, b[k], a[k])

    start, end, halo = [], [], []
    for k in range(13):
        one, two = pair(mine, other, k)
        one_flux, two_flux = pair(mine, other, 13 + k // 2)
        left, right = pair(got, swapped, k)
        left_flux, right_flux = pair(got, swapped, 13 + k // 2)
        start.append(one + jnp.where(low, edge * doubled(left_flux, k), 0.0))
        end.append(two + jnp.where(low, 0.0, edge * doubled(right_flux, k)))
        halo.append(
            jnp.where(low, right, left)
            + turned * jnp.where(low, doubled(two_flux, k), doubled(one_flux, k))
        )
    return start, end, halo


def bring_rims(pairs, ghosts, sems):
    odd = lax.rem(lax.axis_index("gx"), 2)
    copies = []
    for n in range(len(pairs) // 2):
        for m in range(2):
            at = 2 * n + (odd if m == 0 else 1 - odd)
            copies.append(
                pltpu.make_async_copy(pairs[2 * n + m], ghosts.at[at], sems.at[2 * n + m])
            )
    for copy in copies:
        copy.start()
    return copies


def second_kernel(count, source, mine_in, other_in, got, swapped, faces, kind, inflow, *refs):
    pairs = refs[:4]
    moved, mine, other, *out_rims = refs[4:9]
    state, ghosts, coefs, edges, lines, sums, sems = refs[9:]
    copies = bring_rims(pairs, ghosts, sems)
    vy = vy_of(lax.axis_index("vel"))
    start, end, halo = first_moments(mine_in, other_in, got, swapped, faces)
    spread(coefs, coefficients(start, vy), 0)
    spread(coefs, coefficients(end, vy), 8)
    spread(edges, coefficients(halo, vy), 0)
    relax(source, coefs, lines, state, SEC)
    for copy in copies:
        copy.wait()
    relax_ghosts(ghosts, edges, lines, state)
    add_rims(ghosts.at[pl.ds(2, 2)], faces, state)
    finish(state, faces, sums, kind, inflow, moved, mine, other, out_rims, count)


def third_kernel(count, old, pair_a, pair_b, got, swapped, faces, kind, inflow, *refs):
    state, moved, mine, other, ghosts, edges, lines, sums, sems = refs
    copies = bring_rims((pair_a, pair_b), ghosts, sems)
    iy = lax.axis_index("vel")
    pick = low_rows() != (lax.rem(iy, 2) == 0)
    values = [jnp.where(pick, got[k], swapped[k]) for k in range(13)]
    spread(edges, coefficients(values, vy_of(iy)), 0)
    for copy in copies:
        copy.wait()
    relax_ghosts(ghosts, edges, lines, state)
    finish(state, faces, sums, kind, inflow, moved, mine, other, (), count)


VM = pl.BlockSpec(memory_space=pltpu.VMEM)
ANY = pl.BlockSpec(memory_space=pl.ANY)
HBM = pl.BlockSpec(memory_space=pltpu.HBM)
PARAMS = pltpu.CompilerParams(vmem_limit_bytes=12 << 20)
F32 = jnp.float32
FIRST_LIMIT = 60_000_000
WHOLE = jax.ShapeDtypeStruct((ROWS, DEPTH * SEC), F32)
WIDE = jax.ShapeDtypeStruct((ROWS, (DEPTH + 2) * SEC), F32)
RIM = jax.ShapeDtypeStruct((HALF, SEC), F32)
PART = jax.ShapeDtypeStruct((13, 8, 128), F32)
FULL = jax.ShapeDtypeStruct((20, 8, 128), F32)
FACES = jax.ShapeDtypeStruct((5, DEPTH + 1, TILES, 8, 128), F32)
SUMS = pltpu.VMEM((8, OWN, 8, 128), F32)
LINES = pltpu.VMEM((2, 3, 8, 128), F32)


def move_first(dist, wall, kind, inflow, count):
    outs = (FACES, WHOLE, FULL, FULL, RIM, RIM)
    return pl.pallas_call(
        functools.partial(first_kernel, count),
        out_shape=outs,
        in_specs=[HBM] * 4,
        out_specs=(VM,) * len(outs),
        scratch_shapes=[
            pltpu.VMEM(WIDE.shape, F32),
            SUMS,
            pltpu.VMEM((8, 8, 8, 128), F32),
            pltpu.VMEM(wall.shape, jnp.int32),
            pltpu.VMEM(kind.shape, jnp.int32),
            pltpu.VMEM(inflow.shape, F32),
            pltpu.SemaphoreType.DMA((DEPTH + 3,)),
        ],
        compiler_params=pltpu.CompilerParams(vmem_limit_bytes=FIRST_LIMIT),
        name="move_first",
    )(dist, wall, kind, inflow)


def move_second(source, halves, faces, kind, inflow, pairs, count):
    outs = (WHOLE, PART, PART, RIM, RIM)
    return pl.pallas_call(
        functools.partial(second_kernel, count),
        out_shape=outs,
        in_specs=[VM] * 8 + [ANY] * 4,
        out_specs=(VM,) * len(outs),
        scratch_shapes=[
            pltpu.VMEM(WIDE.shape, F32),
            pltpu.VMEM((4, HALF, SEC), F32),
            pltpu.VMEM((9, OWN, 8, 128), F32),
            pltpu.VMEM((9, 8, 8, 128), F32),
            LINES,
            SUMS,
            pltpu.SemaphoreType.DMA((4,)),
        ],
        compiler_params=PARAMS,
        name="move_second",
    )(source, *halves, faces, kind, inflow, *pairs)


def move_third(state, pairs, got, swapped, faces, kind, inflow, count):
    outs = (WIDE, WHOLE, PART, PART)
    return pl.pallas_call(
        functools.partial(third_kernel, count),
        out_shape=outs,
        in_specs=[VM, ANY, ANY] + [VM] * 5,
        out_specs=(VM,) * len(outs),
        input_output_aliases={0: 0},
        scratch_shapes=[
            pltpu.VMEM((2, HALF, SEC), F32),
            pltpu.VMEM((9, 8, 8, 128), F32),
            LINES,
            SUMS,
            pltpu.SemaphoreType.DMA((2,)),
        ],
        compiler_params=PARAMS,
        name="move_third",
    )(state, *pairs, got, swapped, faces, kind, inflow)[1:]


def relax_kernel(moved, mine, other, state, coefs, lines):
    own_coefficients(mine, other, coefs)
    relax(moved, coefs, lines, state, SEC)


def last_kernel(moved, mine, other, out, state, coefs, lines, sems):
    own_coefficients(mine, other, coefs)

    def store(i):
        part = pl.ds(pl.multiple_of(i * SEC, SEC), SEC)
        return pltpu.make_async_copy(state.at[:, part], out.at[:, part], sems.at[i])

    def section(i, carry):
        relax(moved, coefs, lines, state, 0, i * TILES, TILES)
        store(i).start()
        return carry

    lax.fori_loop(0, DEPTH, section, 0)
    for i in range(DEPTH):
        store(i).wait()


def relaxed(moved, mine, other):
    return pl.pallas_call(
        relax_kernel,
        out_shape=WIDE,
        in_specs=[VM, VM, VM],
        out_specs=VM,
        scratch_shapes=[pltpu.VMEM((9, OWN, 8, 128), F32), LINES],
        compiler_params=PARAMS,
        name="relax",
    )(moved, mine, other)


def relax_last(moved, mine, other):
    return pl.pallas_call(
        last_kernel,
        out_shape=WHOLE,
        in_specs=[VM, VM, VM],
        out_specs=HBM,
        scratch_shapes=[
            pltpu.VMEM(WHOLE.shape, F32),
            pltpu.VMEM((9, OWN, 8, 128), F32),
            LINES,
            pltpu.SemaphoreType.DMA((DEPTH,)),
        ],
        compiler_params=PARAMS,
        name="relax_last",
    )(moved, mine, other)


def swap_cores(array):
    return lax.ppermute(array, "vel", [(i, i ^ 1) for i in range(VS)])


def shift_x(array, by):
    def mate(i):
        return i ^ (2 * by)

    return lax.ppermute(array, "vel", [(i, mate(i)) for i in range(VS)])


def flip_y(array):
    return lax.ppermute(array, "vel", [(i, i ^ 8) for i in range(VS)])


def sum_x(value):
    parts = []
    for by in (1, 3, 2):
        parts.append(shift_x(value, by))
    return (value + parts[2]) + (parts[0] + parts[1])


def sum_chips(value):
    value = sum_x(value)
    return value + flip_y(value)


def swap_rims(pair_a, pair_b, count):
    near = [(i, i ^ 1) for i in range(count)]
    far = []
    for i in range(1, count - 1, 2):
        far += [(i, i + 1), (i + 1, i)]
    pair_a = lax.ppermute(pair_a, "gx", near)
    pair_b = lax.ppermute(pair_b, "gx", far)
    return pair_a, pair_b


def swap_moments(half, count):
    pairs = []
    for v in range(0, VS, 2):
        for g in range(count - 1):
            one, two = (v + 1) * count + g, v * count + g + 1
            pairs += [(one, two), (two, one)]
    return lax.ppermute(half, ("vel", "gx"), pairs)


def per_device(distribution, wall_mask, boundary_kind, inflow):
    count = lax.axis_size("gx")
    inflow = inflow.reshape(2, 128)
    even = lax.rem(lax.axis_index("gx"), 2) == 0
    up = distribution[HALF:, (DEPTH - 1) * SEC :]
    down = distribution[:HALF, :SEC]
    start = swap_rims(jnp.where(even, up, down), jnp.where(even, down, up), count)
    outs = move_first(distribution, wall_mask, boundary_kind, inflow, count)
    faces, moved, mine, other, *rims = outs
    pairs = swap_rims(*rims, count)
    half = sum_chips(mine + swap_cores(other))
    halo = swap_moments(half, count)
    swapped = swap_cores(half)
    halves = (half, swapped, halo, swap_cores(halo))
    moved, mine, other, *rims = move_second(
        moved, halves, faces, boundary_kind, inflow, (*pairs, *start), count
    )
    pairs = swap_rims(*rims, count)
    half = sum_chips(mine + swap_cores(other))
    halo = swap_moments(half, count)
    state = relaxed(moved, half, swap_cores(half))
    halo, state = lax.optimization_barrier((halo, state))
    moved, mine, other = move_third(
        state, pairs, halo, swap_cores(halo), faces, boundary_kind, inflow, count
    )
    half = sum_chips(mine + swap_cores(other))
    return relax_last(moved, half, swap_cores(half))


def solution(mesh):
    placed = (P("vel", "gx"), P(), P(), P("vel"))
    return jax.shard_map(
        per_device, mesh=mesh, in_specs=placed, out_specs=P("vel", "gx"), check_vma=False
    )
```

```python
import functools
import math

import jax
import jax.numpy as jnp
from jax import lax
from jax.experimental import pallas as pl
from jax.experimental.pallas import tpu as pltpu
from jax.sharding import PartitionSpec as P


VS = 16
NY = 16
NZ = 32
SEC = NY * NZ
DEPTH = 4
TILES = SEC // 128

LIMIT = 4.5
DT = 0.075
RATE = 0.6
KEEP = 1.0 - RATE
RATIO = 0.6666667
H = 2.0 * LIMIT / VS
WEIGHT = H**3
HALF = VS * VS // 2
ROWS = VS * VS
OWN = DEPTH * TILES


def vy_of(index):
    return -LIMIT + (index.astype(jnp.float32) + 0.5) * H


def sub_iota():
    return lax.broadcasted_iota(jnp.int32, (8, 128), 0).astype(jnp.float32)


def vz_tile(b):
    q = sub_iota()
    return (q + 0.5) * H if b else (q - 7.5) * H


def row(ref, *index):
    return jnp.broadcast_to(ref[index], (8, 128))


def prepare_masks(wall_ref, faces, position, count, forward):
    opened = []
    for slot in range(DEPTH + 4):
        at = position * DEPTH + slot - 2
        inside = jnp.logical_and(at >= 0, at < count * DEPTH)
        line = wall_ref[pl.ds(jnp.clip(at, 0, count * DEPTH - 1), 1), :]
        opened.append(jnp.where(inside, (1 - line).astype(jnp.float32), 1.0))
    o = jnp.concatenate(opened, axis=0)
    cell = lax.broadcasted_iota(jnp.int32, (8, SEC), 1)
    up_x = o * pltpu.roll(o, 7, 0)
    up_y = o * pltpu.roll(o, SEC - NZ, 1) * (cell < SEC - NZ).astype(jnp.float32)
    up_z = o * pltpu.roll(o, SEC - 1, 1) * ((cell & (NZ - 1)) < NZ - 1).astype(jnp.float32)
    down_y = pltpu.roll(up_y, NZ, 1)
    down_z = pltpu.roll(up_z, 1, 1)
    planes = [
        up_x, jnp.where(forward, up_y, down_y), jnp.where(forward, down_y, up_y), down_z, up_z
    ]
    for k, plane in enumerate(planes):
        for slot in range(DEPTH + 3):
            for t in range(TILES):
                line = plane[slot : slot + 1, t * 128 : (t + 1) * 128]
                faces[k, slot, t] = jnp.broadcast_to(line, (8, 128))


def fill_ends(state, inflow_ref, kind_ref, position, count):
    lane = lax.broadcasted_iota(jnp.int32, (8, 128), 1)
    sub = lax.broadcasted_iota(jnp.int32, (8, 128), 0)

    def one(side, base, inner, outer):
        @pl.when(position == (0 if side == 0 else count - 1))
        def _():
            for tile in range(HALF // 8):
                start = base + tile * 8
                line = row(inflow_ref, pl.ds(start // 128, 1), slice(None))
                picked = jnp.where(lane == sub + start % 128, line, 0.0)
                column = jnp.sum(picked, axis=1, keepdims=True)
                for t in range(TILES):
                    kind = row(kind_ref, pl.ds(side, 1), pl.ds(t * 128, 128))
                    inside = state[pl.ds(start, 8), pl.ds(inner * SEC + t * 128, 128)]
                    state[pl.ds(start, 8), pl.ds(outer * SEC + t * 128, 128)] = jnp.where(
                        kind == 1, jnp.broadcast_to(column, (8, 128)), inside
                    )

    one(0, HALF, 1, 0)
    one(1, 0, DEPTH, DEPTH + 1)


def transport(state, faces, moved, sums, iy):
    forward = iy >= VS // 2
    speed_y = jnp.abs(vy_of(iy)) * (KEEP * DT)
    lane = lax.broadcasted_iota(jnp.int32, (8, 128), 1)
    take = jnp.logical_or(
        jnp.logical_and(forward, lane < NZ), jnp.logical_and(~forward, lane >= 128 - NZ)
    )
    shift_y = jnp.where(forward, NZ, 128 - NZ)

    def section(i, carry):
        total = [[None] * 8 for _ in range(TILES)]
        tiles = [jnp.where(forward, k, TILES - 1 - k) for k in range(TILES)]
        lanes = [pl.multiple_of(t * 128, 128) for t in tiles]
        for b in range(2):
            vz = vz_tile(b)
            az = jnp.abs(vz) * (KEEP * DT)
            below = [faces[0, i + 1, t] for t in tiles]
            above = [faces[0, i + 2, t] for t in tiles]
            keep, in_y, in_z = [], [], []
            for t in tiles:
                out_y = faces[1, i + 2, t]
                out_z = faces[4 if b else 3, i + 2, t]
                keep.append(KEEP - speed_y * out_y - az * out_z)
                in_y.append(speed_y * faces[2, i + 2, t])
                in_z.append(az * faces[3 if b else 4, i + 2, t])
            acc = [[None] * 4 for _ in range(TILES)]
            for a in range(VS // 2):
                speed = (a + 0.5) * H
                cx = KEEP * DT * speed
                lo = [cx * x for x in below]
                hi = [cx * x for x in above]
                both = []
                for sign in range(2):
                    start = sign * HALF + a * VS + 8 * b
                    here, shifted = [], []
                    for l in lanes:
                        at = pl.multiple_of((i + 1) * SEC + l, 128)
                        value = state[start : start + 8, pl.ds(at, 128)]
                        here.append(value)
                        shifted.append(pltpu.roll(value, shift_y, 1))
                    result = []
                    for k, l in enumerate(lanes):
                        at = pl.multiple_of((i + (0 if sign else 2)) * SEC + l, 128)
                        before = state[start : start + 8, pl.ds(at, 128)]
                        out_x, in_x = (hi[k], lo[k]) if sign else (lo[k], hi[k])
                        along_y = jnp.where(take, shifted[k - 1], shifted[k]) if k else shifted[k]
                        along_z = pltpu.roll(here[k], 1 if b else 127, 1)
                        value = (
                            here[k] * (keep[k] - out_x)
                            + before * in_x
                            + along_y * in_y[k]
                            + along_z * in_z[k]
                        )
                        at = pl.multiple_of(i * SEC + l, 128)
                        moved[start : start + 8, pl.ds(at, 128)] = value
                        result.append(value)
                    both.append(result)
                for k in range(TILES):
                    even = both[1][k] + both[0][k]
                    odd = both[1][k] - both[0][k]
                    terms = [even, speed * odd, (speed * speed) * even, (speed**3) * odd]
                    for p in range(4):
                        acc[k][p] = terms[p] if acc[k][p] is None else acc[k][p] + terms[p]
            vz2 = vz * vz
            for k in range(TILES):
                a0, a1, a2, a3 = acc[k]
                terms = [
                    a0, a1, vz * a0, a2, vz2 * a0, vz * a1,
                    a3 + vz2 * a1, vz * (a2 + vz2 * a0),
                ]
                for p in range(8):
                    total[k][p] = terms[p] if b == 0 else total[k][p] + terms[p]
        for k, t in enumerate(tiles):
            for p in range(8):
                sums[p, i * TILES + t] = total[k][p]
        return carry

    lax.fori_loop(0, DEPTH, section, 0)


def move_ghosts(raw, faces, ghosts, iy):
    forward = iy >= VS // 2
    speed_y = jnp.abs(vy_of(iy)) * (KEEP * DT)
    lane = lax.broadcasted_iota(jnp.int32, (8, 128), 1)
    take = jnp.logical_or(
        jnp.logical_and(forward, lane < NZ), jnp.logical_and(~forward, lane >= 128 - NZ)
    )
    shift_y = jnp.where(forward, NZ, 128 - NZ)
    tiles = [jnp.where(forward, k, TILES - 1 - k) for k in range(TILES)]
    lanes = [pl.multiple_of(t * 128, 128) for t in tiles]
    for sign in range(2):
        at = 1 if sign else DEPTH + 2
        out_at, in_at = (1, 0) if sign else (DEPTH + 1, DEPTH + 2)
        here_at, before_at = (SEC, 0) if sign else (0, SEC)
        for b in range(2):
            az = jnp.abs(vz_tile(b)) * (KEEP * DT)
            keep, in_y, in_z = [], [], []
            for t in tiles:
                keep.append(KEEP - speed_y * faces[1, at, t] - az * faces[4 if b else 3, at, t])
                in_y.append(speed_y * faces[2, at, t])
                in_z.append(az * faces[3 if b else 4, at, t])

            def rows(a, carry):
                cx = (KEEP * DT * H) * (a.astype(F32) + 0.5)
                start = pl.multiple_of(a * VS + 8 * b, 8)
                here, shifted = [], []
                for l in lanes:
                    value = raw[sign, pl.ds(start, 8), pl.ds(pl.multiple_of(here_at + l, 128), 128)]
                    here.append(value)
                    shifted.append(pltpu.roll(value, shift_y, 1))
                for k, (t, l) in enumerate(zip(tiles, lanes)):
                    before = raw[
                        sign, pl.ds(start, 8), pl.ds(pl.multiple_of(before_at + l, 128), 128)
                    ]
                    along_y = jnp.where(take, shifted[k - 1], shifted[k]) if k else shifted[k]
                    along_z = pltpu.roll(here[k], 1 if b else 127, 1)
                    ghosts[sign, pl.ds(start, 8), pl.ds(l, 128)] = (
                        here[k] * (keep[k] - cx * faces[0, out_at, t])
                        + before * (cx * faces[0, in_at, t])
                        + along_y * in_y[k]
                        + along_z * in_z[k]
                    )
                return carry

            lax.fori_loop(0, VS // 2, rows, 0)


def fold(sums, p, first):
    sub = lax.broadcasted_iota(jnp.int32, (8, 128), 0)
    values = [sums[p, first + t] for t in range(8)]
    for step in (4, 2, 1):
        low = (sub & step) == 0
        merged = []
        for t in range(step):
            a, b = values[t], values[t + step]
            a = a + pltpu.roll(a, 8 - step, 0)
            b = b + pltpu.roll(b, step, 0)
            merged.append(jnp.where(low, a, b))
        values = merged
    return values[0]


def expand(sums, vy):
    s0, sx, sz, sxx, szz, sxz, ex, ez = sums
    y2 = vy * vy
    return [
        s0, sx, vy * s0, sz, sxx, y2 * s0, szz, vy * sx, sxz, vy * sz,
        ex + y2 * sx, vy * (sxx + szz + y2 * s0), ez + y2 * sz,
    ]


def coefficients(m, vy):
    n = m[0]
    inverse = 1.0 / n
    ux, uy, uz = m[1] * inverse, m[2] * inverse, m[3] * inverse
    xx, yy, zz, xy, xz, yz = m[4:10]
    u2 = ux * ux + uy * uy + uz * uz
    trace = xx + yy + zz
    temp = (trace * inverse - u2) / 3.0
    px = xx * ux + xy * uy + xz * uz
    py = xy * ux + yy * uy + yz * uz
    pz = xz * ux + yz * uy + zz * uz
    common = 2.0 * n * u2 - trace
    qx = 0.5 * (m[10] - 2.0 * px + common * ux)
    qy = 0.5 * (m[11] - 2.0 * py + common * uy)
    qz = 0.5 * (m[12] - 2.0 * pz + common * uz)
    inv_t = 1.0 / temp
    kappa = (1.0 - RATIO) / 5.0 * inverse * inv_t * inv_t
    s = kappa * inv_t
    i2t = 0.5 * inv_t
    cy = vy - uy
    level = 0.5 * (
        jnp.log(n) - 1.5 * jnp.log((2.0 * math.pi) * temp) - cy * cy * i2t
    )
    return [ux, uz, i2t, level, qx, qz, s, qy * cy, s * cy * cy - 5.0 * kappa]


def point(coefs, j):
    return [coefs[k, j] for k in range(9)]


def across(values, sign):
    ux, _, i2t, level, qx, _, s, qyc, rest = values
    cx = (sub_iota() + 0.5) * (H if sign else -H) - ux
    c2 = cx * cx
    return jnp.exp(level - c2 * i2t) * RATE, qx * cx + qyc, s * c2 + rest


def along(values, b):
    _, uz, i2t, level, _, qz, s, _, _ = values
    cz = vz_tile(b) - uz
    c2 = cz * cz
    return jnp.exp(level - c2 * i2t), qz * cz, s * c2


def store_lines(lines, values, sign):
    for k, value in enumerate(across(values, sign)):
        lines[sign, k] = value


def relax_rows(read, write, lines, fixed, sign):
    for a in range(VS // 2):
        ex, qa, sa = [row(lines, sign, k, pl.ds(a, 1), slice(None)) for k in range(3)]
        for b in range(2):
            ez, qb, sb = fixed[b]
            start = a * VS + 8 * b
            write(start, read(start) + (ex * ez) * (1.0 + (qa + qb) * (sa + sb)))


def relax(moved, coefs, lines, state, shift, first=0, size=OWN):
    def tile(j, carry):
        values = point(coefs, j)
        for sign in range(2):
            store_lines(lines, values, sign)
        fixed = [along(values, b) for b in range(2)]
        at = pl.multiple_of(j * 128, 128)
        to = pl.multiple_of(j * 128 + shift, 128)
        for sign in range(2):
            base = sign * HALF

            def read(start):
                return moved[base + start : base + start + 8, pl.ds(at, 128)]

            def write(start, value):
                state[base + start : base + start + 8, pl.ds(to, 128)] = value

            relax_rows(read, write, lines, fixed, sign)
        return carry

    lax.fori_loop(first, first + size, tile, 0)


def relax_ghosts(ghosts, coefs, lines, state):
    def tile(t, carry):
        at = pl.multiple_of(t * 128, 128)
        for sign in range(2):
            values = point(coefs, t + TILES * sign)
            store_lines(lines, values, sign)
            fixed = [along(values, b) for b in range(2)]
            base = sign * HALF
            to = pl.multiple_of(t * 128 + (0 if sign else (DEPTH + 1) * SEC), 128)

            def read(start):
                return ghosts[sign, start : start + 8, pl.ds(at, 128)]

            def write(start, value):
                state[base + start : base + start + 8, pl.ds(to, 128)] = value

            relax_rows(read, write, lines, fixed, sign)
        return carry

    lax.fori_loop(0, TILES, tile, 0)


def spread(coefs, values, first):
    for k, value in enumerate(values):
        for t in range(8):
            coefs[k, first + t] = jnp.broadcast_to(value[t : t + 1], (8, 128))


def finish(state, faces, sums, kind, inflow, moved, mine, other, rims, count):
    iy = lax.axis_index("vel")
    position = lax.axis_index("gx")
    fill_ends(state, inflow, kind, position, count)
    transport(state, faces, moved, sums, iy)
    core = lax.rem(iy, 2)
    vy = vy_of(iy)
    for ref, first in ((mine, core * 8), (other, 8 - core * 8)):
        values = expand([fold(sums, p, first) * (WEIGHT / KEEP) for p in range(8)], vy)
        for k, value in enumerate(values):
            ref[k] = value
    if rims:
        even = lax.rem(position, 2) == 0
        up = (slice(HALF, ROWS), slice((DEPTH - 1) * SEC, DEPTH * SEC))
        down = (slice(0, HALF), slice(0, SEC))

        @pl.when(even)
        def _():
            rims[0][...] = moved[up]
            rims[1][...] = moved[down]

        @pl.when(~even)
        def _():
            rims[0][...] = moved[down]
            rims[1][...] = moved[up]


def low_rows():
    return lax.broadcasted_iota(jnp.int32, (8, 128), 0) < TILES


def pack(values):
    low = low_rows()
    values = values + [jnp.zeros_like(values[0])]
    return [jnp.where(low, values[k], values[k + 1]) for k in range(0, 14, 2)]


def doubled(packed, k):
    turned = pltpu.roll(packed, TILES, 0)
    if k % 2:
        return jnp.where(low_rows(), turned, packed)
    return jnp.where(low_rows(), packed, turned)


def rim_flux(state, sums):
    def tile(t, carry):
        for sign in range(2):
            at = pl.multiple_of((DEPTH if sign else 1) * SEC + t * 128, 128)
            total = [None] * 8
            for b in range(2):
                vz = vz_tile(b)
                vz2 = vz * vz
                acc = [None] * 4
                for a in range(VS // 2):
                    speed = (a + 0.5) * H
                    start = sign * HALF + a * VS + 8 * b
                    value = state[start : start + 8, pl.ds(at, 128)] * speed
                    for p in range(4):
                        acc[p] = value if acc[p] is None else acc[p] + value
                        value = value * (speed if sign else -speed)
                a0, a1, a2, a3 = acc
                terms = [
                    a0, a1, vz * a0, a2, vz2 * a0, vz * a1,
                    a3 + vz2 * a1, vz * (a2 + vz2 * a0),
                ]
                total = terms if b == 0 else [x + y for x, y in zip(total, terms)]
            for p in range(8):
                sums[p, TILES * sign + t] = total[p]
        return carry

    lax.fori_loop(0, TILES, tile, 0)


def first_kernel(count, dist, wall, kind, inflow, *refs):
    faces, moved, mine, other, state, sums, flux, wall_v, kind_v, inflow_v, sems = refs
    small = [
        pltpu.make_async_copy(wall, wall_v, sems.at[DEPTH]),
        pltpu.make_async_copy(kind, kind_v, sems.at[DEPTH + 1]),
        pltpu.make_async_copy(inflow, inflow_v, sems.at[DEPTH + 2]),
    ]
    for load in small:
        load.start()
    iy = lax.axis_index("vel")
    position = lax.axis_index("gx")
    loads = [
        pltpu.make_async_copy(
            dist.at[:, pl.ds(i * SEC, SEC)], state.at[:, pl.ds((i + 1) * SEC, SEC)], sems.at[i]
        )
        for i in range(DEPTH)
    ]
    for load in loads:
        load.start()
    state[HALF:, :SEC] = jnp.zeros((HALF, SEC), F32)
    state[:HALF, (DEPTH + 1) * SEC :] = jnp.zeros((HALF, SEC), F32)
    for load in small:
        load.wait()
    prepare_masks(wall_v, faces, position, count, iy >= VS // 2)
    for load in loads:
        load.wait()
    finish(state, faces, sums, kind_v, inflow_v, moved, mine, other, (), count)
    rim_flux(state, flux)
    values = expand([fold(flux, p, 0) * (WEIGHT / KEEP) for p in range(8)], vy_of(iy))
    turned = [pltpu.roll(value, TILES, 0) for value in values]
    low = low_rows()
    halves = [
        pack([value if k % 2 == 0 else turned[k] for k, value in enumerate(values)]),
        pack([turned[k] if k % 2 == 0 else value for k, value in enumerate(values)]),
    ]
    inner = lax.rem(iy, 2) == 0
    for k in range(7):
        mine[13 + k] = jnp.where(inner, halves[0][k], halves[1][k])
        other[13 + k] = jnp.where(inner, halves[1][k], halves[0][k])


def add_rims(ghosts, faces, state):
    def tile(t, carry):
        for sign in range(2):
            at = pl.multiple_of(t * 128 + (SEC if sign else 0), 128)
            to = pl.multiple_of((1 if sign else DEPTH) * SEC + t * 128, 128)
            open_x = faces[0, 1 if sign else DEPTH + 1, t]
            for a in range(VS // 2):
                scale = open_x * (KEEP * DT * (a + 0.5) * H)
                for b in range(2):
                    start = a * VS + 8 * b
                    rows = slice(sign * HALF + start, sign * HALF + start + 8)
                    state[rows, pl.ds(to, 128)] = state[rows, pl.ds(to, 128)] + scale * (
                        ghosts[sign, start : start + 8, pl.ds(at, 128)]
                    )
        return carry

    lax.fori_loop(0, TILES, tile, 0)


def own_coefficients(mine, other, coefs):
    iy = lax.axis_index("vel")
    core = lax.rem(iy, 2)
    for ref, half in ((mine, core), (other, 1 - core)):
        spread(coefs, coefficients([ref[k] for k in range(13)], vy_of(iy)), half * 8)


def first_moments(mine, other, got, swapped, faces):
    inner = lax.rem(lax.axis_index("vel"), 2) == 0
    low = low_rows()
    sub = lax.broadcasted_iota(jnp.int32, (8, 128), 0)
    edge = jnp.zeros((8, 128), F32)
    for t in range(TILES):
        edge = jnp.where(sub == t, faces[0, 1, t], edge)
        edge = jnp.where(sub == t + TILES, faces[0, DEPTH + 1, t], edge)
    edge = edge * (KEEP * DT)
    turned = pltpu.roll(edge, TILES, 0)

    def pair(a, b, k):
        return jnp.where(inner, a[k], b[k]), jnp.where(inner, b[k], a[k])

    start, end, halo = [], [], []
    for k in range(13):
        one, two = pair(mine, other, k)
        one_flux, two_flux = pair(mine, other, 13 + k // 2)
        left, right = pair(got, swapped, k)
        left_flux, right_flux = pair(got, swapped, 13 + k // 2)
        start.append(one + jnp.where(low, edge * doubled(left_flux, k), 0.0))
        end.append(two + jnp.where(low, 0.0, edge * doubled(right_flux, k)))
        halo.append(
            jnp.where(low, right, left)
            + turned * jnp.where(low, doubled(two_flux, k), doubled(one_flux, k))
        )
    return start, end, halo


def bring_rims(pairs, ghosts, sems):
    odd = lax.rem(lax.axis_index("gx"), 2)
    copies = []
    for n in range(len(pairs) // 2):
        for m in range(2):
            at = 2 * n + (odd if m == 0 else 1 - odd)
            copies.append(
                pltpu.make_async_copy(pairs[2 * n + m], ghosts.at[at], sems.at[2 * n + m])
            )
    for copy in copies:
        copy.start()
    return copies


def second_kernel(count, source, mine_in, other_in, got, swapped, faces, kind, inflow, *refs):
    pairs = refs[:2]
    moved, mine, other, *out_rims = refs[2:7]
    state, raw, ghosts, coefs, edges, lines, sums, sems = refs[7:]
    copies = bring_rims(pairs, raw, sems)
    vy = vy_of(lax.axis_index("vel"))
    start, end, halo = first_moments(mine_in, other_in, got, swapped, faces)
    spread(coefs, coefficients(start, vy), 0)
    spread(coefs, coefficients(end, vy), 8)
    spread(edges, coefficients(halo, vy), 0)
    relax(source, coefs, lines, state, SEC)
    for copy in copies:
        copy.wait()
    move_ghosts(raw, faces, ghosts, lax.axis_index("vel"))
    relax_ghosts(ghosts, edges, lines, state)
    add_rims(raw, faces, state)
    finish(state, faces, sums, kind, inflow, moved, mine, other, out_rims, count)


def third_kernel(count, old, pair_a, pair_b, got, swapped, faces, kind, inflow, *refs):
    state, moved, mine, other, ghosts, edges, lines, sums, sems = refs
    copies = bring_rims((pair_a, pair_b), ghosts, sems)
    iy = lax.axis_index("vel")
    pick = low_rows() != (lax.rem(iy, 2) == 0)
    values = [jnp.where(pick, got[k], swapped[k]) for k in range(13)]
    spread(edges, coefficients(values, vy_of(iy)), 0)
    for copy in copies:
        copy.wait()
    relax_ghosts(ghosts, edges, lines, state)
    finish(state, faces, sums, kind, inflow, moved, mine, other, (), count)


VM = pl.BlockSpec(memory_space=pltpu.VMEM)
ANY = pl.BlockSpec(memory_space=pl.ANY)
HBM = pl.BlockSpec(memory_space=pltpu.HBM)
PARAMS = pltpu.CompilerParams(vmem_limit_bytes=12 << 20)
F32 = jnp.float32
FIRST_LIMIT = 12 << 20
WHOLE = jax.ShapeDtypeStruct((ROWS, DEPTH * SEC), F32)
WIDE = jax.ShapeDtypeStruct((ROWS, (DEPTH + 2) * SEC), F32)
RIM = jax.ShapeDtypeStruct((HALF, SEC), F32)
PART = jax.ShapeDtypeStruct((13, 8, 128), F32)
FULL = jax.ShapeDtypeStruct((20, 8, 128), F32)
FACES = jax.ShapeDtypeStruct((5, DEPTH + 3, TILES, 8, 128), F32)
SUMS = pltpu.VMEM((8, OWN, 8, 128), F32)
LINES = pltpu.VMEM((2, 3, 8, 128), F32)


def move_first(dist, wall, kind, inflow, count):
    outs = (FACES, WHOLE, FULL, FULL)
    return pl.pallas_call(
        functools.partial(first_kernel, count),
        out_shape=outs,
        in_specs=[HBM] * 4,
        out_specs=(VM,) * len(outs),
        scratch_shapes=[
            pltpu.VMEM(WIDE.shape, F32),
            SUMS,
            pltpu.VMEM((8, 8, 8, 128), F32),
            pltpu.VMEM(wall.shape, jnp.int32),
            pltpu.VMEM(kind.shape, jnp.int32),
            pltpu.VMEM(inflow.shape, F32),
            pltpu.SemaphoreType.DMA((DEPTH + 3,)),
        ],
        compiler_params=pltpu.CompilerParams(vmem_limit_bytes=FIRST_LIMIT),
        name="move_first",
    )(dist, wall, kind, inflow)


def move_second(source, halves, faces, kind, inflow, pairs, count):
    outs = (WHOLE, PART, PART, RIM, RIM)
    return pl.pallas_call(
        functools.partial(second_kernel, count),
        out_shape=outs,
        in_specs=[VM] * 8 + [ANY] * 2,
        out_specs=(VM,) * len(outs),
        scratch_shapes=[
            pltpu.VMEM(WIDE.shape, F32),
            pltpu.VMEM((2, HALF, 2 * SEC), F32),
            pltpu.VMEM((2, HALF, SEC), F32),
            pltpu.VMEM((9, OWN, 8, 128), F32),
            pltpu.VMEM((9, 8, 8, 128), F32),
            LINES,
            SUMS,
            pltpu.SemaphoreType.DMA((2,)),
        ],
        compiler_params=PARAMS,
        name="move_second",
    )(source, *halves, faces, kind, inflow, *pairs)


def move_third(state, pairs, got, swapped, faces, kind, inflow, count):
    outs = (WIDE, WHOLE, PART, PART)
    return pl.pallas_call(
        functools.partial(third_kernel, count),
        out_shape=outs,
        in_specs=[VM, ANY, ANY] + [VM] * 5,
        out_specs=(VM,) * len(outs),
        input_output_aliases={0: 0},
        scratch_shapes=[
            pltpu.VMEM((2, HALF, SEC), F32),
            pltpu.VMEM((9, 8, 8, 128), F32),
            LINES,
            SUMS,
            pltpu.SemaphoreType.DMA((2,)),
        ],
        compiler_params=PARAMS,
        name="move_third",
    )(state, *pairs, got, swapped, faces, kind, inflow)[1:]


def relax_kernel(moved, mine, other, state, coefs, lines):
    own_coefficients(mine, other, coefs)
    relax(moved, coefs, lines, state, SEC)


def last_kernel(moved, mine, other, out, state, coefs, lines, sems):
    own_coefficients(mine, other, coefs)

    def store(i):
        part = pl.ds(pl.multiple_of(i * SEC, SEC), SEC)
        return pltpu.make_async_copy(state.at[:, part], out.at[:, part], sems.at[i])

    def section(i, carry):
        relax(moved, coefs, lines, state, 0, i * TILES, TILES)
        store(i).start()
        return carry

    lax.fori_loop(0, DEPTH, section, 0)
    for i in range(DEPTH):
        store(i).wait()


def relaxed(moved, mine, other):
    return pl.pallas_call(
        relax_kernel,
        out_shape=WIDE,
        in_specs=[VM, VM, VM],
        out_specs=VM,
        scratch_shapes=[pltpu.VMEM((9, OWN, 8, 128), F32), LINES],
        compiler_params=PARAMS,
        name="relax",
    )(moved, mine, other)


def relax_last(moved, mine, other):
    return pl.pallas_call(
        last_kernel,
        out_shape=WHOLE,
        in_specs=[VM, VM, VM],
        out_specs=HBM,
        scratch_shapes=[
            pltpu.VMEM(WHOLE.shape, F32),
            pltpu.VMEM((9, OWN, 8, 128), F32),
            LINES,
            pltpu.SemaphoreType.DMA((DEPTH,)),
        ],
        compiler_params=PARAMS,
        name="relax_last",
    )(moved, mine, other)


def swap_cores(array):
    return lax.ppermute(array, "vel", [(i, i ^ 1) for i in range(VS)])


def shift_x(array, by):
    def mate(i):
        return i ^ (2 * by)

    return lax.ppermute(array, "vel", [(i, mate(i)) for i in range(VS)])


def flip_y(array):
    return lax.ppermute(array, "vel", [(i, i ^ 8) for i in range(VS)])


def sum_x(value):
    parts = []
    for by in (1, 3, 2):
        parts.append(shift_x(value, by))
    return (value + parts[2]) + (parts[0] + parts[1])


def sum_chips(value):
    value = sum_x(value)
    return value + flip_y(value)


def swap_rims(pair_a, pair_b, count):
    near = [(i, i ^ 1) for i in range(count)]
    far = []
    for i in range(1, count - 1, 2):
        far += [(i, i + 1), (i + 1, i)]
    pair_a = lax.ppermute(pair_a, "gx", near)
    pair_b = lax.ppermute(pair_b, "gx", far)
    return pair_a, pair_b


def swap_moments(half, count):
    pairs = []
    for v in range(0, VS, 2):
        for g in range(count - 1):
            one, two = (v + 1) * count + g, v * count + g + 1
            pairs += [(one, two), (two, one)]
    return lax.ppermute(half, ("vel", "gx"), pairs)


def per_device(distribution, wall_mask, boundary_kind, inflow):
    count = lax.axis_size("gx")
    inflow = inflow.reshape(2, 128)
    even = lax.rem(lax.axis_index("gx"), 2) == 0
    up = distribution[HALF:, (DEPTH - 2) * SEC :]
    down = distribution[:HALF, : 2 * SEC]
    start = swap_rims(jnp.where(even, up, down), jnp.where(even, down, up), count)
    outs = move_first(distribution, wall_mask, boundary_kind, inflow, count)
    faces, moved, mine, other = outs
    half = sum_chips(mine + swap_cores(other))
    halo = swap_moments(half, count)
    swapped = swap_cores(half)
    halves = (half, swapped, halo, swap_cores(halo))
    moved, mine, other, *rims = move_second(
        moved, halves, faces, boundary_kind, inflow, start, count
    )
    pairs = swap_rims(*rims, count)
    half = sum_chips(mine + swap_cores(other))
    halo = swap_moments(half, count)
    state = relaxed(moved, half, swap_cores(half))
    halo, state = lax.optimization_barrier((halo, state))
    moved, mine, other = move_third(
        state, pairs, halo, swap_cores(halo), faces, boundary_kind, inflow, count
    )
    half = sum_chips(mine + swap_cores(other))
    return relax_last(moved, half, swap_cores(half))


def solution(mesh):
    placed = (P("vel", "gx"), P(), P(), P("vel"))
    return jax.shard_map(
        per_device, mesh=mesh, in_specs=placed, out_specs=P("vel", "gx"), check_vma=False
    )
```

```python
import functools
import math

import jax
import jax.numpy as jnp
from jax import lax
from jax.experimental import pallas as pl
from jax.experimental.pallas import tpu as pltpu
from jax.sharding import PartitionSpec as P


VS = 16
NY = 16
NZ = 32
SEC = NY * NZ
DEPTH = 4
TILES = SEC // 128

LIMIT = 4.5
DT = 0.075
RATE = 0.6
KEEP = 1.0 - RATE
RATIO = 0.6666667
H = 2.0 * LIMIT / VS
WEIGHT = H**3
HALF = VS * VS // 2
ROWS = VS * VS
OWN = DEPTH * TILES


def vy_of(index):
    return -LIMIT + (index.astype(jnp.float32) + 0.5) * H


def sub_iota():
    return lax.broadcasted_iota(jnp.int32, (8, 128), 0).astype(jnp.float32)


def vz_tile(b):
    q = sub_iota()
    return (q + 0.5) * H if b else (q - 7.5) * H


def row(ref, *index):
    return jnp.broadcast_to(ref[index], (8, 128))


def prepare_masks(wall_ref, faces, position, count, forward):
    opened = []
    for slot in range(DEPTH + 2):
        at = position * DEPTH + slot - 1
        inside = jnp.logical_and(at >= 0, at < count * DEPTH)
        line = wall_ref[pl.ds(jnp.clip(at, 0, count * DEPTH - 1), 1), :]
        opened.append(jnp.where(inside, (1 - line).astype(jnp.float32), 1.0))
    zero = jnp.zeros_like(opened[0])
    o = jnp.concatenate(opened + [zero, zero], axis=0)
    cell = lax.broadcasted_iota(jnp.int32, (8, SEC), 1)
    up_x = o * pltpu.roll(o, 7, 0)
    up_y = o * pltpu.roll(o, SEC - NZ, 1) * (cell < SEC - NZ).astype(jnp.float32)
    up_z = o * pltpu.roll(o, SEC - 1, 1) * ((cell & (NZ - 1)) < NZ - 1).astype(jnp.float32)
    down_y = pltpu.roll(up_y, NZ, 1)
    down_z = pltpu.roll(up_z, 1, 1)
    planes = [
        up_x, jnp.where(forward, up_y, down_y), jnp.where(forward, down_y, up_y), down_z, up_z
    ]
    for k, plane in enumerate(planes):
        for slot in range(DEPTH + 1):
            for t in range(TILES):
                line = plane[slot : slot + 1, t * 128 : (t + 1) * 128]
                faces[k, slot, t] = jnp.broadcast_to(line, (8, 128))


def fill_ends(state, inflow_ref, kind_ref, position, count):
    lane = lax.broadcasted_iota(jnp.int32, (8, 128), 1)
    sub = lax.broadcasted_iota(jnp.int32, (8, 128), 0)

    def one(side, base, inner, outer):
        @pl.when(position == (0 if side == 0 else count - 1))
        def _():
            for tile in range(HALF // 8):
                start = base + tile * 8
                line = row(inflow_ref, pl.ds(start // 128, 1), slice(None))
                picked = jnp.where(lane == sub + start % 128, line, 0.0)
                column = jnp.sum(picked, axis=1, keepdims=True)
                for t in range(TILES):
                    kind = row(kind_ref, pl.ds(side, 1), pl.ds(t * 128, 128))
                    inside = state[pl.ds(start, 8), pl.ds(inner * SEC + t * 128, 128)]
                    state[pl.ds(start, 8), pl.ds(outer * SEC + t * 128, 128)] = jnp.where(
                        kind == 1, jnp.broadcast_to(column, (8, 128)), inside
                    )

    one(0, HALF, 1, 0)
    one(1, 0, DEPTH, DEPTH + 1)


def transport(state, faces, moved, sums, iy):
    forward = iy >= VS // 2
    speed_y = jnp.abs(vy_of(iy)) * (KEEP * DT)
    lane = lax.broadcasted_iota(jnp.int32, (8, 128), 1)
    take = jnp.logical_or(
        jnp.logical_and(forward, lane < NZ), jnp.logical_and(~forward, lane >= 128 - NZ)
    )
    shift_y = jnp.where(forward, NZ, 128 - NZ)

    def section(i, carry):
        total = [[None] * 8 for _ in range(TILES)]
        tiles = [jnp.where(forward, k, TILES - 1 - k) for k in range(TILES)]
        lanes = [pl.multiple_of(t * 128, 128) for t in tiles]
        for b in range(2):
            vz = vz_tile(b)
            az = jnp.abs(vz) * (KEEP * DT)
            below = [faces[0, i, t] for t in tiles]
            above = [faces[0, i + 1, t] for t in tiles]
            keep, in_y, in_z = [], [], []
            for t in tiles:
                out_y = faces[1, i + 1, t]
                out_z = faces[4 if b else 3, i + 1, t]
                keep.append(KEEP - speed_y * out_y - az * out_z)
                in_y.append(speed_y * faces[2, i + 1, t])
                in_z.append(az * faces[3 if b else 4, i + 1, t])
            acc = [[None] * 4 for _ in range(TILES)]
            for a in range(VS // 2):
                speed = (a + 0.5) * H
                cx = KEEP * DT * speed
                lo = [cx * x for x in below]
                hi = [cx * x for x in above]
                both = []
                for sign in range(2):
                    start = sign * HALF + a * VS + 8 * b
                    here, shifted = [], []
                    for l in lanes:
                        at = pl.multiple_of((i + 1) * SEC + l, 128)
                        value = state[start : start + 8, pl.ds(at, 128)]
                        here.append(value)
                        shifted.append(pltpu.roll(value, shift_y, 1))
                    result = []
                    for k, l in enumerate(lanes):
                        at = pl.multiple_of((i + (0 if sign else 2)) * SEC + l, 128)
                        before = state[start : start + 8, pl.ds(at, 128)]
                        out_x, in_x = (hi[k], lo[k]) if sign else (lo[k], hi[k])
                        along_y = jnp.where(take, shifted[k - 1], shifted[k]) if k else shifted[k]
                        along_z = pltpu.roll(here[k], 1 if b else 127, 1)
                        value = (
                            here[k] * (keep[k] - out_x)
                            + before * in_x
                            + along_y * in_y[k]
                            + along_z * in_z[k]
                        )
                        at = pl.multiple_of(i * SEC + l, 128)
                        moved[start : start + 8, pl.ds(at, 128)] = value
                        result.append(value)
                    both.append(result)
                for k in range(TILES):
                    even = both[1][k] + both[0][k]
                    odd = both[1][k] - both[0][k]
                    terms = [even, speed * odd, (speed * speed) * even, (speed**3) * odd]
                    for p in range(4):
                        acc[k][p] = terms[p] if acc[k][p] is None else acc[k][p] + terms[p]
            vz2 = vz * vz
            for k in range(TILES):
                a0, a1, a2, a3 = acc[k]
                terms = [
                    a0, a1, vz * a0, a2, vz2 * a0, vz * a1,
                    a3 + vz2 * a1, vz * (a2 + vz2 * a0),
                ]
                for p in range(8):
                    total[k][p] = terms[p] if b == 0 else total[k][p] + terms[p]
        for k, t in enumerate(tiles):
            for p in range(8):
                sums[p, i * TILES + t] = total[k][p]
        return carry

    lax.fori_loop(0, DEPTH, section, 0)


def fold(sums, p, first):
    sub = lax.broadcasted_iota(jnp.int32, (8, 128), 0)
    values = [sums[p, first + t] for t in range(8)]
    for step in (4, 2, 1):
        low = (sub & step) == 0
        merged = []
        for t in range(step):
            a, b = values[t], values[t + step]
            a = a + pltpu.roll(a, 8 - step, 0)
            b = b + pltpu.roll(b, step, 0)
            merged.append(jnp.where(low, a, b))
        values = merged
    return values[0]


def expand(sums, vy):
    s0, sx, sz, sxx, szz, sxz, ex, ez = sums
    y2 = vy * vy
    return [
        s0, sx, vy * s0, sz, sxx, y2 * s0, szz, vy * sx, sxz, vy * sz,
        ex + y2 * sx, vy * (sxx + szz + y2 * s0), ez + y2 * sz,
    ]


def coefficients(m, vy):
    n = m[0]
    inverse = 1.0 / n
    ux, uy, uz = m[1] * inverse, m[2] * inverse, m[3] * inverse
    xx, yy, zz, xy, xz, yz = m[4:10]
    u2 = ux * ux + uy * uy + uz * uz
    trace = xx + yy + zz
    temp = (trace * inverse - u2) / 3.0
    px = xx * ux + xy * uy + xz * uz
    py = xy * ux + yy * uy + yz * uz
    pz = xz * ux + yz * uy + zz * uz
    common = 2.0 * n * u2 - trace
    qx = 0.5 * (m[10] - 2.0 * px + common * ux)
    qy = 0.5 * (m[11] - 2.0 * py + common * uy)
    qz = 0.5 * (m[12] - 2.0 * pz + common * uz)
    inv_t = 1.0 / temp
    kappa = (1.0 - RATIO) / 5.0 * inverse * inv_t * inv_t
    s = kappa * inv_t
    i2t = 0.5 * inv_t
    cy = vy - uy
    level = 0.5 * (
        jnp.log(n) - 1.5 * jnp.log((2.0 * math.pi) * temp) - cy * cy * i2t
    )
    return [ux, uz, i2t, level, qx, qz, s, qy * cy, s * cy * cy - 5.0 * kappa]


def point(coefs, j):
    return [coefs[k, j] for k in range(9)]


def across(values, sign):
    ux, _, i2t, level, qx, _, s, qyc, rest = values
    cx = (sub_iota() + 0.5) * (H if sign else -H) - ux
    c2 = cx * cx
    return jnp.exp(level - c2 * i2t) * RATE, qx * cx + qyc, s * c2 + rest


def along(values, b):
    _, uz, i2t, level, _, qz, s, _, _ = values
    cz = vz_tile(b) - uz
    c2 = cz * cz
    return jnp.exp(level - c2 * i2t), qz * cz, s * c2


def store_lines(lines, values, sign):
    for k, value in enumerate(across(values, sign)):
        lines[sign, k] = value


def relax_rows(read, write, lines, fixed, sign):
    for a in range(VS // 2):
        ex, qa, sa = [row(lines, sign, k, pl.ds(a, 1), slice(None)) for k in range(3)]
        for b in range(2):
            ez, qb, sb = fixed[b]
            start = a * VS + 8 * b
            write(start, read(start) + (ex * ez) * (1.0 + (qa + qb) * (sa + sb)))


def relax(moved, coefs, lines, state, shift, first=0, size=OWN):
    def tile(j, carry):
        values = point(coefs, j)
        for sign in range(2):
            store_lines(lines, values, sign)
        fixed = [along(values, b) for b in range(2)]
        at = pl.multiple_of(j * 128, 128)
        to = pl.multiple_of(j * 128 + shift, 128)
        for sign in range(2):
            base = sign * HALF

            def read(start):
                return moved[base + start : base + start + 8, pl.ds(at, 128)]

            def write(start, value):
                state[base + start : base + start + 8, pl.ds(to, 128)] = value

            relax_rows(read, write, lines, fixed, sign)
        return carry

    lax.fori_loop(first, first + size, tile, 0)


def relax_ghosts(ghosts, coefs, lines, state):
    def tile(t, carry):
        at = pl.multiple_of(t * 128, 128)
        for sign in range(2):
            values = point(coefs, t + TILES * sign)
            store_lines(lines, values, sign)
            fixed = [along(values, b) for b in range(2)]
            base = sign * HALF
            to = pl.multiple_of(t * 128 + (0 if sign else (DEPTH + 1) * SEC), 128)

            def read(start):
                return ghosts[sign, start : start + 8, pl.ds(at, 128)]

            def write(start, value):
                state[base + start : base + start + 8, pl.ds(to, 128)] = value

            relax_rows(read, write, lines, fixed, sign)
        return carry

    lax.fori_loop(0, TILES, tile, 0)


def spread(coefs, values, first):
    for k, value in enumerate(values):
        for t in range(8):
            coefs[k, first + t] = jnp.broadcast_to(value[t : t + 1], (8, 128))


def finish(state, faces, sums, kind, inflow, moved, mine, other, rims, count):
    iy = lax.axis_index("vel")
    position = lax.axis_index("gx")
    fill_ends(state, inflow, kind, position, count)
    transport(state, faces, moved, sums, iy)
    core = lax.rem(iy, 2)
    vy = vy_of(iy)
    for ref, first in ((mine, core * 8), (other, 8 - core * 8)):
        values = expand([fold(sums, p, first) * (WEIGHT / KEEP) for p in range(8)], vy)
        for k, value in enumerate(values):
            ref[k] = value
    if rims:
        even = lax.rem(position, 2) == 0
        up = (slice(HALF, ROWS), slice((DEPTH - 1) * SEC, DEPTH * SEC))
        down = (slice(0, HALF), slice(0, SEC))

        @pl.when(even)
        def _():
            rims[0][...] = moved[up]
            rims[1][...] = moved[down]

        @pl.when(~even)
        def _():
            rims[0][...] = moved[down]
            rims[1][...] = moved[up]


def low_rows():
    return lax.broadcasted_iota(jnp.int32, (8, 128), 0) < TILES


def pack(values):
    low = low_rows()
    values = values + [jnp.zeros_like(values[0])]
    return [jnp.where(low, values[k], values[k + 1]) for k in range(0, 14, 2)]


def doubled(packed, k):
    turned = pltpu.roll(packed, TILES, 0)
    if k % 2:
        return jnp.where(low_rows(), turned, packed)
    return jnp.where(low_rows(), packed, turned)


def rim_flux(state, sums):
    def tile(t, carry):
        for sign in range(2):
            at = pl.multiple_of((DEPTH if sign else 1) * SEC + t * 128, 128)
            total = [None] * 8
            for b in range(2):
                vz = vz_tile(b)
                vz2 = vz * vz
                acc = [None] * 4
                for a in range(VS // 2):
                    speed = (a + 0.5) * H
                    start = sign * HALF + a * VS + 8 * b
                    value = state[start : start + 8, pl.ds(at, 128)] * speed
                    for p in range(4):
                        acc[p] = value if acc[p] is None else acc[p] + value
                        value = value * (speed if sign else -speed)
                a0, a1, a2, a3 = acc
                terms = [
                    a0, a1, vz * a0, a2, vz2 * a0, vz * a1,
                    a3 + vz2 * a1, vz * (a2 + vz2 * a0),
                ]
                total = terms if b == 0 else [x + y for x, y in zip(total, terms)]
            for p in range(8):
                sums[p, TILES * sign + t] = total[p]
        return carry

    lax.fori_loop(0, TILES, tile, 0)


def first_kernel(count, dist, wall, kind, inflow, *refs):
    faces, moved, mine, other, rim_a, rim_b, state, sums, flux, wall_v, kind_v, inflow_v, sems = (
        refs
    )
    small = [
        pltpu.make_async_copy(wall, wall_v, sems.at[DEPTH]),
        pltpu.make_async_copy(kind, kind_v, sems.at[DEPTH + 1]),
        pltpu.make_async_copy(inflow, inflow_v, sems.at[DEPTH + 2]),
    ]
    for load in small:
        load.start()
    iy = lax.axis_index("vel")
    position = lax.axis_index("gx")
    loads = [
        pltpu.make_async_copy(
            dist.at[:, pl.ds(i * SEC, SEC)], state.at[:, pl.ds((i + 1) * SEC, SEC)], sems.at[i]
        )
        for i in range(DEPTH)
    ]
    for load in loads:
        load.start()
    state[HALF:, :SEC] = jnp.zeros((HALF, SEC), F32)
    state[:HALF, (DEPTH + 1) * SEC :] = jnp.zeros((HALF, SEC), F32)
    for load in small:
        load.wait()
    prepare_masks(wall_v, faces, position, count, iy >= VS // 2)
    for load in loads:
        load.wait()
    finish(state, faces, sums, kind_v, inflow_v, moved, mine, other, (rim_a, rim_b), count)
    rim_flux(state, flux)
    values = expand([fold(flux, p, 0) * (WEIGHT / KEEP) for p in range(8)], vy_of(iy))
    turned = [pltpu.roll(value, TILES, 0) for value in values]
    low = low_rows()
    halves = [
        pack([value if k % 2 == 0 else turned[k] for k, value in enumerate(values)]),
        pack([turned[k] if k % 2 == 0 else value for k, value in enumerate(values)]),
    ]
    inner = lax.rem(iy, 2) == 0
    for k in range(7):
        mine[13 + k] = jnp.where(inner, halves[0][k], halves[1][k])
        other[13 + k] = jnp.where(inner, halves[1][k], halves[0][k])


def add_rims(ghosts, faces, state):
    def tile(t, carry):
        at = pl.multiple_of(t * 128, 128)
        for sign in range(2):
            to = pl.multiple_of((1 if sign else DEPTH) * SEC + t * 128, 128)
            open_x = faces[0, 0 if sign else DEPTH, t]
            for a in range(VS // 2):
                scale = open_x * (KEEP * DT * (a + 0.5) * H)
                for b in range(2):
                    start = a * VS + 8 * b
                    rows = slice(sign * HALF + start, sign * HALF + start + 8)
                    state[rows, pl.ds(to, 128)] = state[rows, pl.ds(to, 128)] + scale * (
                        ghosts[sign, start : start + 8, pl.ds(at, 128)]
                    )
        return carry

    lax.fori_loop(0, TILES, tile, 0)


def own_coefficients(mine, other, coefs):
    iy = lax.axis_index("vel")
    core = lax.rem(iy, 2)
    for ref, half in ((mine, core), (other, 1 - core)):
        spread(coefs, coefficients([ref[k] for k in range(13)], vy_of(iy)), half * 8)


def first_moments(mine, other, got, swapped, faces):
    inner = lax.rem(lax.axis_index("vel"), 2) == 0
    low = low_rows()
    sub = lax.broadcasted_iota(jnp.int32, (8, 128), 0)
    edge = jnp.zeros((8, 128), F32)
    for t in range(TILES):
        edge = jnp.where(sub == t, faces[0, 0, t], edge)
        edge = jnp.where(sub == t + TILES, faces[0, DEPTH, t], edge)
    edge = edge * (KEEP * DT)
    turned = pltpu.roll(edge, TILES, 0)

    def pair(a, b, k):
        return jnp.where(inner, a[k], b[k]), jnp.where(inner, b[k], a[k])

    start, end, halo = [], [], []
    for k in range(13):
        one, two = pair(mine, other, k)
        one_flux, two_flux = pair(mine, other, 13 + k // 2)
        left, right = pair(got, swapped, k)
        left_flux, right_flux = pair(got, swapped, 13 + k // 2)
        start.append(one + jnp.where(low, edge * doubled(left_flux, k), 0.0))
        end.append(two + jnp.where(low, 0.0, edge * doubled(right_flux, k)))
        halo.append(
            jnp.where(low, right, left)
            + turned * jnp.where(low, doubled(two_flux, k), doubled(one_flux, k))
        )
    return start, end, halo


def bring_rims(pairs, ghosts, sems):
    odd = lax.rem(lax.axis_index("gx"), 2)
    copies = []
    for n in range(len(pairs) // 2):
        for m in range(2):
            at = 2 * n + (odd if m == 0 else 1 - odd)
            copies.append(
                pltpu.make_async_copy(pairs[2 * n + m], ghosts.at[at], sems.at[2 * n + m])
            )
    for copy in copies:
        copy.start()
    return copies


def second_kernel(count, source, mine_in, other_in, got, swapped, faces, kind, inflow, *refs):
    pairs = refs[:4]
    moved, mine, other, *out_rims = refs[4:9]
    state, ghosts, coefs, edges, lines, sums, sems = refs[9:]
    copies = bring_rims(pairs, ghosts, sems)
    vy = vy_of(lax.axis_index("vel"))
    start, end, halo = first_moments(mine_in, other_in, got, swapped, faces)
    spread(coefs, coefficients(start, vy), 0)
    spread(coefs, coefficients(end, vy), 8)
    spread(edges, coefficients(halo, vy), 0)
    relax(source, coefs, lines, state, SEC)
    for copy in copies:
        copy.wait()
    relax_ghosts(ghosts, edges, lines, state)
    add_rims(ghosts.at[pl.ds(2, 2)], faces, state)
    finish(state, faces, sums, kind, inflow, moved, mine, other, out_rims, count)


def third_kernel(count, old, pair_a, pair_b, got, swapped, faces, kind, inflow, *refs):
    state, moved, mine, other, ghosts, edges, lines, sums, sems = refs
    copies = bring_rims((pair_a, pair_b), ghosts, sems)
    iy = lax.axis_index("vel")
    pick = low_rows() != (lax.rem(iy, 2) == 0)
    values = [jnp.where(pick, got[k], swapped[k]) for k in range(13)]
    spread(edges, coefficients(values, vy_of(iy)), 0)
    for copy in copies:
        copy.wait()
    relax_ghosts(ghosts, edges, lines, state)
    finish(state, faces, sums, kind, inflow, moved, mine, other, (), count)


VM = pl.BlockSpec(memory_space=pltpu.VMEM)
ANY = pl.BlockSpec(memory_space=pl.ANY)
HBM = pl.BlockSpec(memory_space=pltpu.HBM)
PARAMS = pltpu.CompilerParams(vmem_limit_bytes=12 << 20)
F32 = jnp.float32
FIRST_LIMIT = 12 << 20
WHOLE = jax.ShapeDtypeStruct((ROWS, DEPTH * SEC), F32)
WIDE = jax.ShapeDtypeStruct((ROWS, (DEPTH + 2) * SEC), F32)
RIM = jax.ShapeDtypeStruct((HALF, SEC), F32)
PART = jax.ShapeDtypeStruct((13, 8, 128), F32)
FULL = jax.ShapeDtypeStruct((20, 8, 128), F32)
FACES = jax.ShapeDtypeStruct((5, DEPTH + 1, TILES, 8, 128), F32)
SUMS = pltpu.VMEM((8, OWN, 8, 128), F32)
LINES = pltpu.VMEM((2, 3, 8, 128), F32)


def move_first(dist, wall, kind, inflow, count):
    outs = (FACES, WHOLE, FULL, FULL, RIM, RIM)
    return pl.pallas_call(
        functools.partial(first_kernel, count),
        out_shape=outs,
        in_specs=[HBM] * 4,
        out_specs=(VM,) * len(outs),
        scratch_shapes=[
            pltpu.VMEM(WIDE.shape, F32),
            SUMS,
            pltpu.VMEM((8, 8, 8, 128), F32),
            pltpu.VMEM(wall.shape, jnp.int32),
            pltpu.VMEM(kind.shape, jnp.int32),
            pltpu.VMEM(inflow.shape, F32),
            pltpu.SemaphoreType.DMA((DEPTH + 3,)),
        ],
        compiler_params=pltpu.CompilerParams(vmem_limit_bytes=FIRST_LIMIT),
        name="move_first",
    )(dist, wall, kind, inflow)


def cut_kernel(dist, near, far, sems):
    even = lax.rem(lax.axis_index("gx"), 2) == 0

    def cut(up, down):
        copies = [
            pltpu.make_async_copy(
                dist.at[pl.ds(HALF, HALF), pl.ds((DEPTH - 1) * SEC, SEC)], up, sems.at[0]
            ),
            pltpu.make_async_copy(dist.at[pl.ds(0, HALF), pl.ds(0, SEC)], down, sems.at[1]),
        ]
        for copy in copies:
            copy.start()
        for copy in copies:
            copy.wait()

    pl.when(even)(lambda: cut(near, far))
    pl.when(~even)(lambda: cut(far, near))


def cut_rims(dist):
    return pl.pallas_call(
        cut_kernel,
        out_shape=(RIM, RIM),
        in_specs=[HBM],
        out_specs=(VM, VM),
        scratch_shapes=[pltpu.SemaphoreType.DMA((2,))],
        compiler_params=pltpu.CompilerParams(vmem_limit_bytes=54_000_000),
        name="cut_rims",
    )(dist)


def move_second(source, halves, faces, kind, inflow, pairs, count):
    outs = (WHOLE, PART, PART, RIM, RIM)
    return pl.pallas_call(
        functools.partial(second_kernel, count),
        out_shape=outs,
        in_specs=[VM] * 8 + [ANY] * 4,
        out_specs=(VM,) * len(outs),
        scratch_shapes=[
            pltpu.VMEM(WIDE.shape, F32),
            pltpu.VMEM((4, HALF, SEC), F32),
            pltpu.VMEM((9, OWN, 8, 128), F32),
            pltpu.VMEM((9, 8, 8, 128), F32),
            LINES,
            SUMS,
            pltpu.SemaphoreType.DMA((4,)),
        ],
        compiler_params=PARAMS,
        name="move_second",
    )(source, *halves, faces, kind, inflow, *pairs)


def move_third(state, pairs, got, swapped, faces, kind, inflow, count):
    outs = (WIDE, WHOLE, PART, PART)
    return pl.pallas_call(
        functools.partial(third_kernel, count),
        out_shape=outs,
        in_specs=[VM, ANY, ANY] + [VM] * 5,
        out_specs=(VM,) * len(outs),
        input_output_aliases={0: 0},
        scratch_shapes=[
            pltpu.VMEM((2, HALF, SEC), F32),
            pltpu.VMEM((9, 8, 8, 128), F32),
            LINES,
            SUMS,
            pltpu.SemaphoreType.DMA((2,)),
        ],
        compiler_params=PARAMS,
        name="move_third",
    )(state, *pairs, got, swapped, faces, kind, inflow)[1:]


def relax_kernel(moved, mine, other, state, coefs, lines):
    own_coefficients(mine, other, coefs)
    relax(moved, coefs, lines, state, SEC)


def last_kernel(moved, mine, other, out, state, coefs, lines, sems):
    own_coefficients(mine, other, coefs)

    def store(i):
        part = pl.ds(pl.multiple_of(i * SEC, SEC), SEC)
        return pltpu.make_async_copy(state.at[:, part], out.at[:, part], sems.at[i])

    def section(i, carry):
        relax(moved, coefs, lines, state, 0, i * TILES, TILES)
        store(i).start()
        return carry

    lax.fori_loop(0, DEPTH, section, 0)
    for i in range(DEPTH):
        store(i).wait()


def relaxed(moved, mine, other):
    return pl.pallas_call(
        relax_kernel,
        out_shape=WIDE,
        in_specs=[VM, VM, VM],
        out_specs=VM,
        scratch_shapes=[pltpu.VMEM((9, OWN, 8, 128), F32), LINES],
        compiler_params=PARAMS,
        name="relax",
    )(moved, mine, other)


def relax_last(moved, mine, other):
    return pl.pallas_call(
        last_kernel,
        out_shape=WHOLE,
        in_specs=[VM, VM, VM],
        out_specs=HBM,
        scratch_shapes=[
            pltpu.VMEM(WHOLE.shape, F32),
            pltpu.VMEM((9, OWN, 8, 128), F32),
            LINES,
            pltpu.SemaphoreType.DMA((DEPTH,)),
        ],
        compiler_params=PARAMS,
        name="relax_last",
    )(moved, mine, other)


def swap_cores(array):
    return lax.ppermute(array, "vel", [(i, i ^ 1) for i in range(VS)])


def shift_x(array, by):
    def mate(i):
        return i ^ (2 * by)

    return lax.ppermute(array, "vel", [(i, mate(i)) for i in range(VS)])


def flip_y(array):
    return lax.ppermute(array, "vel", [(i, i ^ 8) for i in range(VS)])


def sum_x(value):
    parts = []
    for by in (1, 3, 2):
        parts.append(shift_x(value, by))
    return (value + parts[2]) + (parts[0] + parts[1])


def sum_chips(value):
    value = sum_x(value)
    return value + flip_y(value)


def swap_rims(pair_a, pair_b, count):
    near = [(i, i ^ 1) for i in range(count)]
    far = []
    for i in range(1, count - 1, 2):
        far += [(i, i + 1), (i + 1, i)]
    pair_a = lax.ppermute(pair_a, "gx", near)
    pair_b = lax.ppermute(pair_b, "gx", far)
    return pair_a, pair_b


def swap_moments(half, count):
    pairs = []
    for v in range(0, VS, 2):
        for g in range(count - 1):
            one, two = (v + 1) * count + g, v * count + g + 1
            pairs += [(one, two), (two, one)]
    return lax.ppermute(half, ("vel", "gx"), pairs)


def per_device(distribution, wall_mask, boundary_kind, inflow):
    count = lax.axis_size("gx")
    inflow = inflow.reshape(2, 128)
    even = lax.rem(lax.axis_index("gx"), 2) == 0
    near, far = cut_rims(distribution)
    start = swap_rims(near, far, count)
    outs = move_first(distribution, wall_mask, boundary_kind, inflow, count)
    faces, moved, mine, other, *rims = outs
    pairs = swap_rims(*rims, count)
    half = sum_chips(mine + swap_cores(other))
    halo = swap_moments(half, count)
    swapped = swap_cores(half)
    halves = (half, swapped, halo, swap_cores(halo))
    moved, mine, other, *rims = move_second(
        moved, halves, faces, boundary_kind, inflow, (*pairs, *start), count
    )
    pairs = swap_rims(*rims, count)
    half = sum_chips(mine + swap_cores(other))
    halo = swap_moments(half, count)
    state = relaxed(moved, half, swap_cores(half))
    halo, state = lax.optimization_barrier((halo, state))
    moved, mine, other = move_third(
        state, pairs, halo, swap_cores(halo), faces, boundary_kind, inflow, count
    )
    half = sum_chips(mine + swap_cores(other))
    return relax_last(moved, half, swap_cores(half))


def solution(mesh):
    placed = (P("vel", "gx"), P(), P(), P("vel"))
    return jax.shard_map(
        per_device, mesh=mesh, in_specs=placed, out_specs=P("vel", "gx"), check_vma=False
    )
```
